32 devices in a mesh: dp: 8 (over z, x), ctx: 2 (over y), tp: 2 (over core).
Axes of the slice: x: 2, y: 2, z: 4, core: 2. Of those that a mesh axis runs over, the one named last changes fastest.
Arguments:
- tokens: bfloat16 [16, 1024, 768], P('dp', 'ctx'), may hold values from -6 to 6
- lengths: int32 [16], P('dp'), may hold values from 256 to 1024, as said below
- ln1_gain: float32 [768], P('dp'), may hold values from 0.5 to 1.5
- ln1_bias: float32 [768], P('dp'), may hold values from -1.75 to 1.75
- w_qkv: bfloat16 [768, 3, 768], P('dp', None, 'tp'), may hold values from -0.21875 to 0.21875
- qv_bias: float32 [384, 2, 2], P('dp', None, 'tp'), may hold values from -1.25 to 1.25
- w_out: bfloat16 [768, 768], P('dp', 'tp'), may hold values from -1.75 to 1.75
- out_bias: float32 [768], P('dp'), may hold values from -1.75 to 1.75
- ln2_gain: float32 [768], P('dp'), may hold values from 0.5 to 1.5
- ln2_bias: float32 [768], P('dp'), may hold values from -1.75 to 1.75
- w_fc: bfloat16 [768, 3072], P('dp', 'tp'), may hold values from -0.21875 to 0.21875
- fc_bias: float32 [1536, 2], P('dp', 'tp'), may hold values from -1.75 to 1.75
- w_proj: bfloat16 [768, 3072], P('dp', 'tp'), may hold values from -0.21875 to 0.21875
- proj_bias: float32 [768], P('dp'), may hold values from -1.75 to 1.75
- cotangent: bfloat16 [16, 1024, 768], P('dp', 'ctx'), may hold values from -6 to 6
Outputs:
- output: bfloat16 [16, 1024, 768], P('dp', 'ctx')
- grad_tokens: bfloat16 [16, 1024, 768], P('dp', 'ctx')
- grad_ln1_gain: float32 [768], P('dp')
- grad_ln1_bias: float32 [768], P('dp')
- grad_w_qkv: float32 [768, 3, 768], P('dp', None, 'tp')
- grad_qv_bias: float32 [384, 2, 2], P('dp', None, 'tp')
- grad_w_out: float32 [768, 768], P('dp', 'tp')
- grad_out_bias: float32 [768], P('dp')
- grad_ln2_gain: float32 [768], P('dp')
- grad_ln2_bias: float32 [768], P('dp')
- grad_w_fc: float32 [768, 3072], P('dp', 'tp')
- grad_fc_bias: float32 [1536, 2], P('dp', 'tp')
- grad_w_proj: float32 [768, 3072], P('dp', 'tp')
- grad_proj_bias: float32 [768], P('dp')
The draws below stay inside these ranges and needn't reach their ends.
Inputs may be any that keep to these rules, and one draw needn't show every extreme that they name: lengths[s] is the number of valid slots of sequence s; slots from lengths[s] on are padding.
All inputs are finite; a program needn't handle non-finite values.
Results may differ from the reference program's by a relative error of at most 0.03.
Values may be sent and summed in bfloat16 or wider, within the bound.
A program may use at most 192 MiB of HBM per device.

```python
import jax
import jax.numpy as jnp
from jax import lax

D = 768
H = 12
HD = 64
FF = 3072
SLOTS = 1024
MIN_LEN = 256
SEQS = 16
N_TP = 2


def draw_lengths(key, part):
    first_key, second_key = jax.random.split(key)
    drawn = jax.random.randint(first_key, (SEQS,), MIN_LEN, SLOTS + 1)
    order = jax.random.permutation(second_key, SEQS)
    places = jnp.arange(SEQS)
    drawn = jnp.where(places == order[0], SLOTS, drawn)
    drawn = jnp.where(places == order[1], MIN_LEN, drawn)
    return drawn.astype(jnp.int32)


def block_scale(own_key, extent, cuts, low, high):
    factor_of = 1.0
    for position, parts in cuts:
        steps = jax.random.uniform(jax.random.fold_in(jax.random.fold_in(own_key, 6), position), (parts,), jnp.float32, low / len(cuts), high / len(cuts))
        factor_of = factor_of * jnp.repeat(jnp.exp(steps), extent[position] // parts).reshape((-1,) + (1,) * (len(extent) - 1 - position))
    return factor_of


def noise(rng, shape, scale, limit, cuts=(), held_as=jnp.bfloat16):
    entries = scale * jax.random.normal(rng, shape, jnp.float32)
    if cuts:
        entries = entries * block_scale(rng, shape, cuts, -0.22, 0.18)
    return jnp.clip(entries, -limit, limit).astype(held_as)


def setup_inputs(seed: int = 0) -> dict:
    key_of = jax.random.split(jax.random.key(seed), 16)
    tokens = noise(key_of[0], (SEQS, SLOTS, D), 1.0, 6.0, ((0, 8), (1, 2)))
    lengths = draw_lengths(jax.random.fold_in(key_of[15], 71), 0)
    ln1_gain = jnp.clip(1.0 + 0.1 * jax.random.normal(key_of[2], (D,), jnp.float32), 0.5, 1.5)
    ln1_bias = noise(key_of[3], (D,), 0.3, 1.75, ((0, 8),), jnp.float32)
    w_qkv = noise(key_of[4], (D, 3, D), D ** -0.5, 0.21875, ((0, 8), (2, 2)))
    qv_bias = noise(key_of[5], (D // N_TP, 2, N_TP), 0.2, 1.25, ((0, 8), (2, 2)), jnp.float32)
    w_out = noise(key_of[6], (D, D), (D // 64) ** -0.5, 1.75, ((0, 8), (1, 2)))
    out_bias = noise(key_of[7], (D,), 0.3, 1.75, ((0, 8),), jnp.float32)
    ln2_gain = jnp.clip(1.0 + 0.1 * jax.random.normal(key_of[8], (D,), jnp.float32), 0.5, 1.5)
    ln2_bias = noise(key_of[9], (D,), 0.3, 1.75, ((0, 8),), jnp.float32)
    w_fc = noise(key_of[10], (D, FF), D ** -0.5, 0.21875, ((0, 8), (1, 2)))
    fc_bias = noise(key_of[11], (FF // N_TP, N_TP), 0.3, 1.75, ((0, 8), (1, 2)), jnp.float32)
    w_proj = noise(key_of[12], (D, FF), (FF // 4) ** -0.5, 0.21875, ((0, 8), (1, 2)))
    proj_bias = noise(key_of[13], (D,), 0.3, 1.75, ((0, 8),), jnp.float32)
    cotangent = noise(key_of[14], (SEQS, SLOTS, D), 1.0, 6.0, ((0, 8), (1, 2)))
    return dict(tokens=tokens, lengths=lengths, ln1_gain=ln1_gain, ln1_bias=ln1_bias, w_qkv=w_qkv, qv_bias=qv_bias, w_out=w_out, out_bias=out_bias, ln2_gain=ln2_gain, ln2_bias=ln2_bias, w_fc=w_fc, fc_bias=fc_bias, w_proj=w_proj, proj_bias=proj_bias, cotangent=cotangent)


@jax.custom_vjp
def low(v):
    return lax.optimization_barrier(v.astype(jnp.bfloat16)).astype(jnp.float32)

@jax.custom_vjp
def low_back(v):
    return v

def low_keep(v):
    return (low(v), None)

def low_pass(kept, grad):
    return (grad,)

def back_keep(v):
    return (v, None)

def back_low(kept, grad):
    return (low(grad),)
low.defvjp(low_keep, low_pass)
low_back.defvjp(back_keep, back_low)
epsilon = 1e-05

def product_high(left_side, right_side):
    return jnp.matmul(left_side, right_side, precision=lax.Precision.HIGHEST)

def apply_layer_norm(row_values, gain_vec, shift_vec):
    centred = row_values - lax.optimization_barrier(jnp.mean(row_values, axis=-1, keepdims=True))
    variance = lax.optimization_barrier(jnp.mean(centred * centred, axis=-1, keepdims=True))
    return centred * lax.rsqrt(variance + epsilon) * gain_vec + shift_vec

def block_forward(row_values, group_lengths, param_list):
    first_norm_gain, first_norm_shift, proj_qkv, qv_table, proj_out, bias_out, second_norm_gain, second_norm_shift, proj_fc, fc_table, proj_back, bias_back = param_list
    seq_count = row_values.shape[0]
    query_bias = qv_table[:, 0, :].T.reshape(D)
    value_bias = qv_table[:, 1, :].T.reshape(D)
    fc_shift = fc_table.T.reshape(FF)
    first_hidden_rows = low(apply_layer_norm(row_values, first_norm_gain, first_norm_shift))
    query_rows = low_back(low(product_high(first_hidden_rows, proj_qkv[:, 0]) + query_bias))
    key_rows = low_back(low(product_high(first_hidden_rows, proj_qkv[:, 1])))
    value_rows = low_back(low(product_high(first_hidden_rows, proj_qkv[:, 2]) + value_bias))

    def split_heads(table):
        return table.reshape(seq_count, SLOTS, H, HD)
    scores = low_back(jnp.einsum('sqhe,skhe->shqk', split_heads(query_rows), split_heads(key_rows), precision=lax.Precision.HIGHEST) * HD ** (-0.5))
    valid_keys = jnp.arange(SLOTS)[None, :] < group_lengths[:, None]
    scores = jnp.where(valid_keys[:, None, None, :], scores, -1e+30)
    prob_rows = low(jax.nn.softmax(scores, axis=-1))
    mixed_rows = jnp.einsum('shqk,skhe->sqhe', prob_rows, split_heads(value_rows), precision=lax.Precision.HIGHEST)
    mixed_rows = low_back(low(mixed_rows.reshape(seq_count, SLOTS, D)))
    residual_middle = row_values + low_back(product_high(mixed_rows, proj_out.T)) + bias_out
    second_hidden_rows = low(apply_layer_norm(residual_middle, second_norm_gain, second_norm_shift))
    pre_act = low_back(product_high(second_hidden_rows, proj_fc) + fc_shift)
    act_rows = low(pre_act * jax.nn.sigmoid(1.702 * pre_act))
    return residual_middle + low_back(product_high(act_rows, proj_back.T)) + bias_back

def reference(tokens, lengths, ln1_gain, ln1_bias, w_qkv, qv_bias, w_out, out_bias, ln2_gain, ln2_bias, w_fc, fc_bias, w_proj, proj_bias, cotangent):
    param_list = tuple((entry.astype(jnp.float32) for entry in (ln1_gain, ln1_bias, w_qkv, qv_bias, w_out, out_bias, ln2_gain, ln2_bias, w_fc, fc_bias, w_proj, proj_bias)))
    group_size = 4
    group_count = SEQS // group_size

    def group_step(totals, packed):
        group_rows, group_lengths, group_grads = packed

        def forward_of(row_values, params_in):
            return block_forward(row_values, group_lengths, params_in)
        result, pullback = jax.vjp(forward_of, group_rows.astype(jnp.float32), param_list)
        live_rows = (jnp.arange(SLOTS)[None, :] < group_lengths[:, None])[..., None]
        seed_grad = jnp.where(live_rows, group_grads.astype(jnp.float32), jnp.zeros_like(result))
        grad_rows, grad_params = pullback(seed_grad)
        totals = jax.tree.map(jnp.add, totals, grad_params)
        return (totals, (result.astype(jnp.bfloat16), grad_rows.astype(jnp.bfloat16)))
    zero_totals = jax.tree.map(jnp.zeros_like, param_list)
    stacked = (tokens.reshape(group_count, group_size, SLOTS, D), lengths.reshape(group_count, group_size), cotangent.reshape(group_count, group_size, SLOTS, D))
    totals, (outputs, grad_rows) = lax.scan(group_step, zero_totals, stacked)
    return (outputs.reshape(SEQS, SLOTS, D), grad_rows.reshape(SEQS, SLOTS, D), totals[0], totals[1], totals[2], totals[3], totals[4], totals[5], totals[6], totals[7], totals[8], totals[9], totals[10], totals[11])
```

```python
import functools

import jax
import jax.numpy as jnp
from jax import lax
from jax.experimental import pallas as pl
from jax.experimental.pallas import tpu as pltpu
from jax.sharding import PartitionSpec as P

HD = 64
EPS = 1e-05
NEG = -1e30
GELU = 1.702
SCALE = HD ** (-0.5)
F32 = jnp.float32
BF16 = jnp.bfloat16
MESH = pl.DeviceIdType.MESH
LIMIT = 60 * 2**20
NN = (((1,), (0,)), ((), ()))
NT = (((1,), (1,)), ((), ()))


def dot(a, b, dims=NN):
    return lax.dot_general(a, b, dims, preferred_element_type=F32)


class Net:
    def __init__(self, send, recv):
        self.send, self.recv, self.used, self.all = send, recv, 0, []

    def put(self, src, dst, dev):
        k = self.used
        self.used += 1
        copy = pltpu.make_async_remote_copy(
            src_ref=src, dst_ref=dst, send_sem=self.send.at[k], recv_sem=self.recv.at[k],
            device_id=dev, device_id_type=MESH,
        )
        copy.start()
        self.all.append(copy)
        return copy

    def finish(self):
        for copy in self.all:
            copy.wait_send()


class Place:
    def __init__(self, n_dp):
        self.d = lax.axis_index("dp")
        self.c = lax.axis_index("ctx")
        self.t = lax.axis_index("tp")
        self.n_o = n_dp // 2
        self.o, self.i = self.d // 2, self.d % 2

    def outer(self, s):
        return (lax.rem(self.o + s, self.n_o) * 2 + self.i, self.c, self.t)

    def from_outer(self, s):
        return lax.rem(self.o + self.n_o - s, self.n_o) * 2 + self.i

    @property
    def inner(self):
        return (self.o * 2 + 1 - self.i, self.c, self.t)

    @property
    def ctx(self):
        return (self.d, 1 - self.c, self.t)

    @property
    def tp(self):
        return (self.d, self.c, 1 - self.t)

    def barrier(self):
        sem = pltpu.get_barrier_semaphore()
        peers = [self.outer(s) for s in range(1, self.n_o)] + [self.inner, self.ctx, self.tp]
        for peer in peers:
            pl.semaphore_signal(sem, 1, device_id=peer, device_id_type=MESH)
        pl.semaphore_wait(sem, len(peers))


def gather_kernel(
    n_dp, tok, cot, small, wq, wo, wf, wp,
    xs, gs, small_all, wq_all, wo_all, wf_all, wp_all, send, recv, local,
):
    me = Place(n_dp)
    net = Net(send, recv)
    d, c, t = me.d, me.c, me.t
    shifts = list(range(1, me.n_o))
    half = tok.shape[1]
    quarter = half // 2
    rows = wf.shape[0]
    hrow = rows // 2
    me.barrier()

    def own(src, dst, k):
        copy = pltpu.make_async_copy(src, dst, local.at[k])
        copy.start()
        return copy

    def whole(src, dst):
        return [net.put(src, dst.at[d], me.outer(s)) for s in shifts] + [
            net.put(src, dst.at[d], me.inner)
        ]

    def cut(ref, dev):
        return ref.at[dev, pl.ds(c * hrow, hrow)]

    def spread(src, dst):
        return [
            net.put(src.at[pl.ds(c * hrow, hrow)], cut(dst, d), me.outer(s)) for s in shifts
        ]

    mine = pl.ds(c * half + t * quarter, quarter)
    theirs = pl.ds((1 - c) * half + t * quarter, quarter)
    tok_y = net.put(tok.at[1 - c, pl.ds(t * quarter, quarter)], xs.at[mine], me.ctx)
    small_o = whole(small, small_all)
    q_o = whole(wq, wq_all)
    o_o = whole(wo, wo_all)
    cot_y = net.put(cot.at[1 - c, pl.ds(t * quarter, quarter)], gs.at[mine], me.ctx)
    f_o = spread(wf, wf_all)
    p_o = spread(wp, wp_all)
    locals_ = [
        own(tok.at[c], xs.at[pl.ds(c * half, half)], 0),
        own(cot.at[c], gs.at[pl.ds(c * half, half)], 1),
        own(small, small_all.at[d], 2),
        own(wq, wq_all.at[d], 3),
        own(wo, wo_all.at[d], 4),
        own(wf, wf_all.at[d], 5),
        own(wp, wp_all.at[d], 6),
    ]

    def relay(copies, dst):
        out = []
        for s, copy in zip(shifts, copies):
            copy.wait_recv()
            src = dst.at[me.from_outer(s)]
            out.append(net.put(src, src, me.inner))
        return out

    rest = relay(small_o, small_all)
    tok_y.wait_recv()
    rest.append(net.put(xs.at[theirs], xs.at[theirs], me.tp))
    rest += relay(q_o, wq_all)
    rest += relay(o_o, wo_all)
    cot_y.wait_recv()
    rest.append(net.put(gs.at[theirs], gs.at[theirs], me.tp))
    rest += [small_o[-1], q_o[-1], o_o[-1]]

    def wide(copies, src, dst):
        out, over = [], [net.put(src.at[pl.ds(c * hrow, hrow)], cut(dst, d), me.inner)]
        for s, copy in zip(shifts, copies):
            copy.wait_recv()
            piece = cut(dst, me.from_outer(s))
            over.append(net.put(piece, piece, me.inner))
            out.append(net.put(piece, piece, me.ctx))
        for s, copy in zip([0] + shifts, over):
            copy.wait_recv()
            piece = cut(dst, lax.rem(me.o + me.n_o - s, me.n_o) * 2 + 1 - me.i)
            out.append(net.put(piece, piece, me.ctx))
        return out

    rest += wide(f_o, wf, wf_all)
    rest += wide(p_o, wp, wp_all)
    for copy in rest:
        copy.wait_recv()
    net.finish()
    for copy in locals_:
        copy.wait()


def add_rows(dst, parts, rows, step):
    @pl.loop(0, rows // step)
    def _(j):
        at = pl.ds(pl.multiple_of(j * step, step), step)
        total = parts[0][at, :].astype(F32)
        for part in parts[1:]:
            total = total + part[at, :].astype(F32)
        dst[at, :] = total.astype(dst.dtype)


def reduce_kernel(
    n_dp, gq, go, gf, gp, small, out_seq, tok_seq,
    rq, ro, rf, rp, rsmall, out, gtok,
    xq, zq, sq, yq, xo, zo, so, yo, xf, zf, sf, yf, xp, zp, sp, yp, xm, zm, sm, ym,
    send, recv, local,
):
    me = Place(n_dp)
    net = Net(send, recv)
    d, c, t = me.d, me.c, me.t
    shifts = list(range(1, me.n_o))
    half = out.shape[1]
    quarter = half // 2
    me.barrier()

    mine = pl.ds((1 - c) * half + t * quarter, quarter)
    final = []
    seq_y = []
    for src, dst in ((out_seq, out), (tok_seq, gtok)):
        seq_y.append(net.put(src.at[mine], dst.at[c, pl.ds(t * quarter, quarter)], me.ctx))
    locals_ = []
    for k, (src, dst) in enumerate(((out_seq, out), (tok_seq, gtok))):
        copy = pltpu.make_async_copy(src.at[pl.ds(c * half, half)], dst.at[c], local.at[k])
        copy.start()
        locals_.append(copy)

    def outer_of(s):
        return lax.rem(me.o + s, me.n_o)

    def first(g, x):
        return [
            net.put(g.at[outer_of(s) * 2 + 1 - me.i], x.at[s], me.inner)
            for s in shifts + [0]
        ]

    def second(g, x, z, sums, copies, rows, step):
        out = []
        for s, copy in zip(shifts + [0], copies):
            copy.wait_recv()
            add_rows(sums.at[s], [g.at[outer_of(s) * 2 + me.i], x.at[s]], rows, step)
            if s:
                out.append(net.put(sums.at[s], z.at[s - 1], me.outer(s)))
        return out

    def third(z, sums, y, copies, rows, step):
        for copy in copies:
            copy.wait_recv()
        add_rows(y.at[0], [sums.at[0]] + [z.at[s - 1] for s in shifts], rows, step)
        return net.put(y.at[0], y.at[1], me.ctx)

    def fourth(y, r, copy, rows, step):
        copy.wait_recv()
        add_rows(r, [y.at[0], y.at[1]], rows, step)

    groups = [
        (gp, xp, zp, sp, yp, rp, 16),
        (gf, xf, zf, sf, yf, rf, 16),
        (go, xo, zo, so, yo, ro, 16),
        (gq, xq, zq, sq, yq, rq, 16),
        (small, xm, zm, sm, ym, rsmall, 8),
    ]
    ones = [first(g, x) for g, x, _, _, _, _, _ in groups]
    twos = []
    for copy, (src, dst) in zip(seq_y, ((out_seq, out), (tok_seq, gtok))):
        copy.wait_recv()
        place = dst.at[1 - c, pl.ds(t * quarter, quarter)]
        final.append(net.put(place, place, me.tp))
    for (g, x, z, s, y, r, step), copies in zip(groups, ones):
        twos.append(second(g, x, z, s, copies, r.shape[0], step))
    threes = []
    for (g, x, z, s, y, r, step), copies in zip(groups, twos):
        threes.append(third(z, s, y, copies, r.shape[0], step))
    for (g, x, z, s, y, r, step), copy in zip(groups, threes):
        fourth(y, r, copy, r.shape[0], step)
    for copy in final:
        copy.wait_recv()
    net.finish()
    for copy in locals_:
        copy.wait()


def norm(x):
    centred = x - jnp.mean(x, axis=-1, keepdims=True)
    inv = lax.rsqrt(jnp.mean(centred * centred, axis=-1, keepdims=True) + EPS)
    return centred * inv, inv


def block(j, size):
    return pl.ds(pl.multiple_of(j * size, size), size)


def forward_kernel(
    length, xs, vec, bq, bv, wq, wo, q, k, v, kt, h1t, o, ot, pt, part, vt
):
    rows, width = xs.shape
    cols = q.shape[1]
    step = 256

    @pl.loop(0, rows // step)
    def _(j):
        at = block(j, step)
        n, _ = norm(xs[at, :].astype(F32))
        h1 = (n * vec[0:1, :] + vec[1:2, :]).astype(BF16)
        h1t[:, at] = h1.T
        proj = dot(h1, wq[...])
        q[at, :] = (proj[:, :cols] + bq[...]).astype(BF16) * SCALE
        kk = proj[:, cols : 2 * cols].astype(BF16)
        vv = (proj[:, 2 * cols :] + bv[...]).astype(BF16)
        k[at, :] = kk
        v[at, :] = vv
        kt[:, at] = kk.T
        vt[:, at] = vv.T

    live = lax.broadcasted_iota(jnp.int32, (rows, step), 0) < length[0]
    side = lax.broadcasted_iota(jnp.int32, (step, 128), 1) // HD

    @pl.loop(0, cols // 128)
    def _(p):
        pair = block(p, 128)

        @pl.loop(0, rows // step)
        def _(j):
            at = block(j, step)
            for hh in range(2):
                qm = jnp.where(side == hh, q[at, pair], jnp.zeros((), BF16))
                s = dot(k[:, pair], qm, NT)
                s = jnp.where(live, s, NEG)
                e = jnp.exp(s - jnp.max(s, axis=0, keepdims=True))
                pb = (e * (1.0 / jnp.sum(e, axis=0, keepdims=True))).astype(BF16)
                pt[p * 2 + hh, :, at] = pb
                head = block(p * 2 + hh, HD)
                ot[head, at] = dot(vt[head, :], pb).astype(BF16)

    @pl.loop(0, rows // step)
    def _(j):
        at = block(j, step)
        ob = ot[:, at].T
        o[at, :] = ob
        part[at, :] = dot(ob, wo[...], NT).astype(BF16)


def mlp_kernel(
    length, xs, gs, vec, bf, p0, p1, wf, wp, r1, a, du, h2t, gt, part2, part3
):
    rows, width = xs.shape
    step = 256

    @pl.loop(0, rows // step)
    def _(j):
        at = block(j, step)
        mid = xs[at, :].astype(F32) + (p0[at, :].astype(F32) + p1[at, :].astype(F32)) + vec[2:3, :]
        r1[at, :] = mid
        n, _ = norm(mid)
        h2 = (n * vec[3:4, :] + vec[4:5, :]).astype(BF16)
        h2t[:, at] = h2.T
        live = j * step + lax.broadcasted_iota(jnp.int32, (step, width), 0) < length[0]
        g = jnp.where(live, gs[at, :], jnp.zeros((), BF16))
        gt[:, at] = g.T
        u = dot(h2, wf[...]) + bf[...]
        s = jax.nn.sigmoid(GELU * u)
        act = (u * s).astype(BF16)
        a[at, :] = act
        part2[at, :] = dot(act, wp[...], NT).astype(BF16)
        slope = s * (1.0 + GELU * u * (1.0 - s))
        dub = (dot(g, wp[...]) * slope).astype(BF16)
        du[at, :] = dub
        part3[at, :] = dot(dub, wf[...], NT).astype(BF16)


def weights_kernel(gt, h2t, a, du, gp, gf, bp, bfg):
    width = gt.shape[0]
    step = 128

    @pl.loop(0, width // step)
    def _(j):
        at = block(j, step)
        gp[at, :] = dot(gt[at, :], a[...]).astype(BF16)
        gf[at, :] = dot(h2t[at, :], du[...]).astype(BF16)

    bp[...] = jnp.zeros_like(bp)
    bfg[...] = jnp.zeros_like(bfg)

    @pl.loop(0, du.shape[0] // 128)
    def _(j):
        at = block(j, 128)
        bfg[...] += jnp.sum(du[at, :].astype(F32), axis=0, keepdims=True)
        bp[...] += jnp.sum(gt[:, at].astype(F32).T, axis=0, keepdims=True)


def middle_kernel(
    length, gs, vec, r1, p2a, p2b, p3a, p3b, o, wo, out, dr1, do, go, sums, dt
):
    rows, width = gs.shape
    step = 256
    sums[...] = jnp.zeros_like(sums)

    @pl.loop(0, rows // step)
    def _(j):
        at = block(j, step)
        mid = r1[at, :]
        out[at, :] = (
            mid + (p2a[at, :].astype(F32) + p2b[at, :].astype(F32)) + vec[5:6, :]
        ).astype(BF16)
        n, inv = norm(mid)
        dh = p3a[at, :].astype(F32) + p3b[at, :].astype(F32)
        e = dh * vec[3:4, :]
        live = j * step + lax.broadcasted_iota(jnp.int32, (step, width), 0) < length[0]
        g = jnp.where(live, gs[at, :].astype(F32), 0.0)
        grad = g + inv * (
            e - jnp.mean(e, axis=-1, keepdims=True) - n * jnp.mean(e * n, axis=-1, keepdims=True)
        )
        dr1[at, :] = grad
        sums[0:1, :] += jnp.sum(grad, axis=0, keepdims=True)
        sums[1:2, :] += jnp.sum(dh * n, axis=0, keepdims=True)
        sums[2:3, :] += jnp.sum(dh, axis=0, keepdims=True)
        gb = grad.astype(BF16)
        dt[:, at] = gb.T
        do[at, :] = dot(gb, wo[...]).astype(BF16)

    @pl.loop(0, width // step)
    def _(j):
        at = block(j, step)
        go[at, :] = dot(dt[at, :], o[...]).astype(BF16)


def backward_kernel(
    q, k, v, kt, h1t, ot, pt, do, wq, gq, part, sums, dot_t, dst, dqt, dqkv
):
    rows, cols = q.shape
    step = 256
    side = lax.broadcasted_iota(jnp.int32, (step, 128), 1) // HD
    side_all = lax.broadcasted_iota(jnp.int32, (rows, 128), 1) // HD
    zero = jnp.zeros((), BF16)

    @pl.loop(0, rows // step)
    def _(j):
        at = block(j, step)
        dot_t[:, at] = do[at, :].T

    @pl.loop(0, cols // 128)
    def _(p):
        pair = block(p, 128)
        for hh in range(2):
            head = block(p * 2 + hh, HD)

            @pl.loop(0, rows // step)
            def _(j):
                at = block(j, step)
                inner = jnp.sum(
                    dot_t[head, at].astype(F32) * ot[head, at].astype(F32), axis=0, keepdims=True
                )
                dp = dot(v[:, pair], jnp.where(side == hh, do[at, pair], zero), NT)
                ds = (pt[p * 2 + hh, :, at].astype(F32) * (dp - inner)).astype(BF16)
                dst[hh, :, at] = ds
                dqt[head, at] = dot(kt[head, :], ds)

        qp = q[:, pair]
        dp_ = do[:, pair]
        dk = dot(dst[0], jnp.where(side_all == 0, qp, zero)) + dot(
            dst[1], jnp.where(side_all == 1, qp, zero)
        )
        dv = dot(pt[p * 2], jnp.where(side_all == 0, dp_, zero)) + dot(
            pt[p * 2 + 1], jnp.where(side_all == 1, dp_, zero)
        )
        dqkv[:, pl.ds(pl.multiple_of(cols + p * 128, 128), 128)] = dk.astype(BF16)
        dqkv[:, pl.ds(pl.multiple_of(2 * cols + p * 128, 128), 128)] = dv.astype(BF16)

    sums[...] = jnp.zeros_like(sums)

    @pl.loop(0, rows // step)
    def _(j):
        at = block(j, step)
        dqkv[at, 0:cols] = (dqt[:, at].T * SCALE).astype(BF16)
        low = dqkv[at, :]
        sums[0:1, :] += jnp.sum(low.astype(F32), axis=0, keepdims=True)
        part[at, :] = dot(low, wq[...], NT).astype(BF16)

    @pl.loop(0, h1t.shape[0] // step)
    def _(j):
        at = block(j, step)
        gq[at, :] = dot(h1t[at, :], dqkv[...]).astype(BF16)


def last_kernel(xs, vec, dr1, pa, pb, gtok, sums):
    rows, width = xs.shape
    step = 256
    sums[...] = jnp.zeros_like(sums)

    @pl.loop(0, rows // step)
    def _(j):
        at = block(j, step)
        n, inv = norm(xs[at, :].astype(F32))
        dh = pa[at, :].astype(F32) + pb[at, :].astype(F32)
        e = dh * vec[0:1, :]
        gtok[at, :] = (
            dr1[at, :]
            + inv
            * (e - jnp.mean(e, axis=-1, keepdims=True) - n * jnp.mean(e * n, axis=-1, keepdims=True))
        ).astype(BF16)
        sums[0:1, :] += jnp.sum(dh * n, axis=0, keepdims=True)
        sums[1:2, :] += jnp.sum(dh, axis=0, keepdims=True)


VM = pl.BlockSpec(memory_space=pltpu.VMEM)
SM = pl.BlockSpec(memory_space=pltpu.SMEM)
ANY = pl.BlockSpec(memory_space=pl.ANY)


def call(body, ins, outs, scratch=(), specs=None, out_specs=None, name=None, cid=None):
    params = dict(vmem_limit_bytes=LIMIT)
    if cid is not None:
        params.update(collective_id=cid, has_side_effects=True)
    return pl.pallas_call(
        body,
        out_shape=[jax.ShapeDtypeStruct(s, t) for s, t in outs],
        in_specs=specs or [VM] * len(ins),
        out_specs=out_specs or [VM] * len(outs),
        scratch_shapes=list(scratch),
        name=name,
        compiler_params=pltpu.CompilerParams(**params),
    )(*ins)


def on_device(n_dp, tokens, lengths, ln1_gain, ln1_bias, w_qkv, qv_bias, w_out, out_bias,
              ln2_gain, ln2_bias, w_fc, fc_bias, w_proj, proj_bias, cotangent):
    _, half, width = tokens.shape
    rows = 2 * half
    shard = w_fc.shape[0]
    cols = w_out.shape[1]
    ff = w_fc.shape[1]
    dma = pltpu.SemaphoreType.DMA
    ctx = lax.axis_index("ctx")
    length = lax.dynamic_slice(lengths, (ctx,), (1,))
    lines = [ln1_gain, ln1_bias, out_bias, ln2_gain, ln2_bias, proj_bias,
             qv_bias[:, :, 0].T.reshape(shard)] + list(fc_bias[:, 0].reshape(2, shard))
    small = jnp.pad(jnp.stack(lines), ((0, 16 - len(lines)), (0, 128 - shard)))
    wq_own = w_qkv.reshape(shard, 3 * cols)
    if n_dp == 8:
        outs = [((rows, width), BF16), ((rows, width), BF16), ((n_dp, 16, 128), F32),
                ((n_dp, shard, 3 * cols), BF16), ((n_dp, shard, cols), BF16),
                ((n_dp, shard, ff), BF16), ((n_dp, shard, ff), BF16)]
        xs, gs, small_all, wq, wo, wf, wp = call(
            functools.partial(gather_kernel, n_dp),
            (tokens, cotangent, small, wq_own, w_out, w_fc, w_proj), outs,
            [dma((64,)), dma((64,)), dma((7,))], [ANY] * 7, [ANY] * 7, "gather", 1)
    else:
        def whole(a):
            return lax.all_gather(a, "ctx", axis=1, tiled=True)

        xs = lax.dynamic_index_in_dim(whole(tokens), ctx, 0, False)
        gs = lax.dynamic_index_in_dim(whole(cotangent), ctx, 0, False)
        small_all, wq, wo, wf, wp = [
            lax.all_gather(a, "dp") for a in (small, wq_own, w_out, w_fc, w_proj)]
    wq, wo, wf, wp = [a.reshape(n_dp * shard, -1) for a in (wq, wo, wf, wp)]
    vec = small_all[:, :6, :shard].transpose(1, 0, 2).reshape(6, width)
    vec = jnp.pad(vec, ((0, 2), (0, 0)))
    qv = small_all[:, 6, :shard].reshape(n_dp, 2, shard // 2).transpose(1, 0, 2).reshape(2, cols)
    bf = small_all[:, 7:9, :shard].reshape(1, ff)

    act = ((rows, width), BF16)
    head = ((rows, cols), BF16)
    head_t = ((cols, rows), BF16)
    q, k, v, kt, h1t, o, ot, pt, part1 = call(
        forward_kernel, (length, xs, vec, qv[0:1], qv[1:2], wq, wo),
        [head, head, head, head_t, ((width, rows), BF16), head, head_t,
         ((cols // HD, rows, rows), BF16), act],
        [pltpu.VMEM((cols, rows), BF16)], [SM] + [VM] * 6, name="forward")

    def other(a):
        return lax.ppermute(a, "tp", [(0, 1), (1, 0)])

    r1, a, du, h2t, gt, part2, part3 = call(
        mlp_kernel, (length, xs, gs, vec, bf, part1, other(part1), wf, wp),
        [((rows, width), F32), ((rows, ff), BF16), ((rows, ff), BF16),
         ((width, rows), BF16), ((width, rows), BF16), act, act],
        specs=[SM] + [VM] * 8, name="mlp")
    gp, gf, bp, bfg = call(
        weights_kernel, (gt, h2t, a, du),
        [((width, ff), BF16), ((width, ff), BF16), ((1, width), F32), ((1, ff), F32)],
        name="weights")
    out_seq, dr1, do, go, sums2 = call(
        middle_kernel,
        (length, gs, vec, r1, part2, other(part2), part3, other(part3), o, wo),
        [act, ((rows, width), F32), head, ((width, cols), BF16), ((8, width), F32)],
        [pltpu.VMEM((width, rows), BF16)], [SM] + [VM] * 9, name="middle")
    gq, part4, sums3 = call(
        backward_kernel, (q, k, v, kt, h1t, ot, pt, do, wq),
        [((width, 3 * cols), BF16), act, ((8, 3 * cols), F32)],
        [pltpu.VMEM((cols, rows), BF16), pltpu.VMEM((2, rows, rows), BF16),
         pltpu.VMEM((cols, rows), F32), pltpu.VMEM((rows, 3 * cols), BF16)], name="backward")
    tok_seq, sums1 = call(
        last_kernel, (xs, vec, dr1, part4, other(part4)),
        [act, ((8, width), F32)], name="last")

    gvec = jnp.concatenate([sums1[0:2], sums2[0:3], bp])
    gvec = gvec.reshape(6, n_dp, shard).transpose(1, 0, 2)
    gqv = jnp.stack([sums3[0, :cols], sums3[0, 2 * cols :]]).reshape(2, n_dp, shard // 2)
    gqv = gqv.transpose(1, 0, 2).reshape(n_dp, 1, shard)
    gsmall = jnp.concatenate([gvec, gqv, bfg.reshape(n_dp, 2, shard)], axis=1)
    gsmall = jnp.pad(gsmall, ((0, 0), (0, 7), (0, 128 - shard)))
    gq, go, gf, gp = [a.reshape(n_dp, shard, -1) for a in (gq, go, gf, gp)]
    if n_dp == 8:
        n_o = n_dp // 2
        scratch = []
        for n, r, kind in ((3 * cols, shard, BF16), (cols, shard, BF16), (ff, shard, BF16),
                           (ff, shard, BF16), (128, 16, F32)):
            scratch += [pltpu.VMEM((n_o, r, n), kind), pltpu.VMEM((n_o - 1, r, n), kind),
                        pltpu.VMEM((n_o, r, n), kind), pltpu.VMEM((2, r, n), kind)]
        rq, ro, rf, rp, rs, out, gtok = call(
            functools.partial(reduce_kernel, n_dp),
            (gq, go, gf, gp, gsmall, out_seq, tok_seq),
            [((shard, 3 * cols), F32), ((shard, cols), F32), ((shard, ff), F32),
             ((shard, ff), F32), ((16, 128), F32), ((2, half, width), BF16),
             ((2, half, width), BF16)],
            scratch + [dma((64,)), dma((64,)), dma((2,))],
            [VM] * 5 + [ANY] * 2, [VM] * 5 + [ANY] * 2, "reduce", 2)
    else:
        def summed(a):
            return lax.psum(lax.psum_scatter(a, "dp", scatter_dimension=0), "ctx")

        rq, ro, rf, rp = [summed(a).astype(F32) for a in (gq, go, gf, gp)]
        rs = summed(gsmall)

        def back(a):
            pieces = lax.all_gather(a, "ctx", axis=0)
            return lax.dynamic_slice(pieces, (0, ctx * half, 0), (2, half, width))

        out, gtok = back(out_seq), back(tok_seq)
    line = [rs[j, :shard] for j in range(7)]
    return (out, gtok, line[0], line[1], rq.reshape(shard, 3, cols),
            line[6].reshape(2, shard // 2).T[:, :, None], ro, line[2], line[3], line[4],
            rf, rs[7:9, :shard].reshape(2 * shard, 1), rp, line[5])


def solution(mesh):
    dp, seq = P("dp"), P("dp", "ctx", None)
    wide, flat = P("dp", None, "tp"), P("dp", "tp")
    params = (dp, dp, wide, wide, flat, dp, dp, dp, flat, flat, flat, dp)
    return jax.shard_map(
        functools.partial(on_device, mesh.shape["dp"]),
        mesh=mesh,
        in_specs=(seq, dp) + params + (seq,),
        out_specs=(seq, seq) + params,
        check_vma=False,
    )
```

```python
import functools

import jax
import jax.numpy as jnp
from jax import lax
from jax.experimental import pallas as pl
from jax.experimental.pallas import tpu as pltpu
from jax.sharding import PartitionSpec as P

HD = 64
EPS = 1e-05
NEG = -1e30
GELU = 1.702
SCALE = HD ** (-0.5)
F32 = jnp.float32
BF16 = jnp.bfloat16
MESH = pl.DeviceIdType.MESH
LIMIT = 60 * 2**20
NN = (((1,), (0,)), ((), ()))
NT = (((1,), (1,)), ((), ()))


def dot(a, b, dims=NN):
    return lax.dot_general(a, b, dims, preferred_element_type=F32)


class Net:
    def __init__(self, send, recv):
        self.send, self.recv, self.used, self.all = send, recv, 0, []

    def build(self, k, src, dst, dev):
        return pltpu.make_async_remote_copy(
            src_ref=src, dst_ref=dst, send_sem=self.send.at[k], recv_sem=self.recv.at[k],
            device_id=dev, device_id_type=MESH,
        )

    def take(self, count):
        self.used += count
        return self.used - count

    def make(self, src, dst, dev):
        copy = self.build(self.take(1), src, dst, dev)
        self.all.append(copy)
        return copy

    def put(self, src, dst, dev):
        copy = self.make(src, dst, dev)
        copy.start()
        return copy

    def finish(self):
        for copy in self.all:
            copy.wait_send()


class Place:
    def __init__(self, n_dp, direct=True):
        self.d = lax.axis_index("dp")
        self.c = lax.axis_index("ctx")
        self.t = lax.axis_index("tp")
        self.direct = direct
        self.n_o = n_dp // 2
        self.o, self.i = self.d // 2, self.d % 2

    def outer(self, s):
        return (lax.rem(self.o + s, self.n_o) * 2 + self.i, self.c, self.t)

    def from_outer(self, s):
        return lax.rem(self.o + self.n_o - s, self.n_o) * 2 + self.i

    @property
    def inner(self):
        return (self.o * 2 + 1 - self.i, self.c, self.t)

    @property
    def ctx(self):
        return (self.d, 1 - self.c, self.t)

    @property
    def tp(self):
        return (self.d, self.c, 1 - self.t)

    def barrier(self):
        sem = pltpu.get_barrier_semaphore()
        peers = [self.tp]
        if self.direct:
            peers += [self.outer(s) for s in range(1, self.n_o)] + [self.inner, self.ctx]
        for peer in peers:
            pl.semaphore_signal(sem, 1, device_id=peer, device_id_type=MESH)
        pl.semaphore_wait(sem, len(peers))


def add_rows(dst, parts, rows, step):
    @pl.loop(0, rows // step)
    def _(j):
        at = pl.ds(pl.multiple_of(j * step, step), step)
        total = parts[0][at, :].astype(F32)
        for part in parts[1:]:
            total = total + part[at, :].astype(F32)
        dst[at, :] = total.astype(dst.dtype)


def reduce_kernel(
    n_dp, gq, go, gf, gp, small, out_seq, tok_seq,
    rq, ro, rf, rp, rsmall, out, gtok,
    xq, zq, sq, yq, xo, zo, so, yo, xf, zf, sf, yf, xp, zp, sp, yp, xm, zm, sm, ym,
    send, recv, local,
):
    me = Place(n_dp)
    net = Net(send, recv)
    d, c, t = me.d, me.c, me.t
    shifts = list(range(1, me.n_o))
    half = out.shape[1]
    quarter = half // 2
    me.barrier()

    mine = pl.ds((1 - c) * half + t * quarter, quarter)
    final = []
    seq_y = []
    for src, dst in ((out_seq, out), (tok_seq, gtok)):
        seq_y.append(net.put(src.at[mine], dst.at[c, pl.ds(t * quarter, quarter)], me.ctx))
    locals_ = []
    for k, (src, dst) in enumerate(((out_seq, out), (tok_seq, gtok))):
        copy = pltpu.make_async_copy(src.at[pl.ds(c * half, half)], dst.at[c], local.at[k])
        copy.start()
        locals_.append(copy)

    def outer_of(s):
        return lax.rem(me.o + s, me.n_o)

    def first(g, x):
        return [
            net.put(g.at[outer_of(s) * 2 + 1 - me.i], x.at[s], me.inner)
            for s in shifts + [0]
        ]

    def second(g, x, z, sums, copies, rows, step):
        out = []
        for s, copy in zip(shifts + [0], copies):
            copy.wait_recv()
            add_rows(sums.at[s], [g.at[outer_of(s) * 2 + me.i], x.at[s]], rows, step)
            if s:
                out.append(net.put(sums.at[s], z.at[s - 1], me.outer(s)))
        return out

    def third(z, sums, y, copies, rows, step):
        for copy in copies:
            copy.wait_recv()
        add_rows(y.at[0], [sums.at[0]] + [z.at[s - 1] for s in shifts], rows, step)
        return net.put(y.at[0], y.at[1], me.ctx)

    def fourth(y, r, copy, rows, step):
        copy.wait_recv()
        add_rows(r, [y.at[0], y.at[1]], rows, step)

    groups = [
        (gp, xp, zp, sp, yp, rp, 16),
        (gf, xf, zf, sf, yf, rf, 16),
        (go, xo, zo, so, yo, ro, 16),
        (gq, xq, zq, sq, yq, rq, 16),
        (small, xm, zm, sm, ym, rsmall, 8),
    ]
    ones = [first(g, x) for g, x, _, _, _, _, _ in groups]
    twos = []
    for copy, (src, dst) in zip(seq_y, ((out_seq, out), (tok_seq, gtok))):
        copy.wait_recv()
        place = dst.at[1 - c, pl.ds(t * quarter, quarter)]
        final.append(net.put(place, place, me.tp))
    for (g, x, z, s, y, r, step), copies in zip(groups, ones):
        twos.append(second(g, x, z, s, copies, r.shape[0], step))
    threes = []
    for (g, x, z, s, y, r, step), copies in zip(groups, twos):
        threes.append(third(z, s, y, copies, r.shape[0], step))
    for (g, x, z, s, y, r, step), copy in zip(groups, threes):
        fourth(y, r, copy, r.shape[0], step)
    for copy in final:
        copy.wait_recv()
    net.finish()
    for copy in locals_:
        copy.wait()


def norm(x):
    centred = x - jnp.mean(x, axis=-1, keepdims=True)
    inv = lax.rsqrt(jnp.mean(centred * centred, axis=-1, keepdims=True) + EPS)
    return centred * inv, inv


def block(j, size):
    return pl.ds(pl.multiple_of(j * size, size), size)


class Stage:
    def __init__(self, me, net, src, dst, halves):
        self.src, self.dst, self.halves, self.me = src, dst, halves, me
        rows = dst.shape[1]
        part = pl.ds(me.c * (rows // 2), rows // 2)

        def cut(dev):
            return dst.at[dev, part] if halves else dst.at[dev]

        own = src.at[part] if halves else src
        shifts = list(range(1, me.n_o))
        self.outer = [net.make(own, cut(me.d), me.outer(s)) for s in shifts]
        self.inner = [net.make(own, cut(me.d), me.inner)]
        self.ctx = []
        for s in shifts:
            piece = cut(me.from_outer(s))
            self.inner.append(net.make(piece, piece, me.inner))
            if halves:
                self.ctx.append(net.make(piece, piece, me.ctx))
        self.far = []
        if halves:
            for s in [0] + shifts:
                piece = cut(lax.rem(me.o + me.n_o - s, me.n_o) * 2 + 1 - me.i)
                self.far.append(net.make(piece, piece, me.ctx))

    def begin(self):
        for copy in self.outer:
            copy.start()

    def begin_inner(self):
        self.inner[0].start()

    def relay(self, s):
        self.outer[s].wait_recv()
        self.inner[s + 1].start()
        if self.halves:
            self.ctx[s].start()

    def cross(self, s):
        self.inner[s].wait_recv()
        self.far[s].start()

    def arrive(self):
        for copy in self.ctx + self.far if self.halves else self.inner:
            copy.wait_recv()


def placed(small_all, row, first, count, stride, offset, size):
    lane = lax.broadcasted_iota(jnp.int32, (128, size), 0)
    col = lax.broadcasted_iota(jnp.int32, (128, size), 1)
    inside = (lane >= first) & (lane < first + count)

    def add(d, total):
        spot = inside & (col == lane - first + (d * stride + offset))
        return total + lax.dot_general(
            small_all[d, row : row + 8, :], spot.astype(F32), NN,
            precision=lax.Precision.HIGHEST, preferred_element_type=F32,
        )

    return lax.fori_loop(0, small_all.shape[0], add, jnp.zeros((8, size), F32))


def forward_kernel(
    n_dp, direct, length, tok, cot, small, wq, wo, wf, wp,
    vec, g_o, gt_o, x_o, h1t_o, q_o, k_o, v_o, kt_o, o_o, ot_o, pt_o, r1_o, a_o, sl_o, h2t_o,
    wq_o, wo_o, wf_o, wp_o,
    small_v, wq_v, wo_v, wf_v, x, gv, gm, gt, h1, h1t, q, k, v, kt, vt, o, ot, pt, ps, pr, r1, a, sl, h2t,
    bias, fcb, send, recv, local, pts, rows_s,
):
    me = Place(n_dp, direct)
    net = Net(send, recv)
    d, c, t = me.d, me.c, me.t
    rows, width = x.shape
    cols = q.shape[1]
    half, step = rows // 2, 256
    quarter = half // 2
    shard = width // n_dp
    n_blocks = rows // step
    me.barrier()
    done = []

    def own(src, dst):
        copy = pltpu.make_async_copy(src, dst, local.at[len(done)])
        copy.start()
        done.append(copy)
        return copy

    mine = pl.ds(c * half + t * quarter, quarter)
    theirs = pl.ds((1 - c) * half + t * quarter, quarter)
    first = net.take(n_blocks)

    def exchange(j):
        at = block(j, step)
        return net.build(first + j, ps.at[at], pr.at[at], me.tp)

    if direct:
        tok_y = net.make(tok.at[1 - c, pl.ds(t * quarter, quarter)], x.at[mine], me.ctx)
        tok_t = net.make(x.at[theirs], x.at[theirs], me.tp)
        cot_y = net.make(cot.at[1 - c, pl.ds(t * quarter, quarter)], gv.at[mine], me.ctx)
        cot_t = net.make(gv.at[theirs], gv.at[theirs], me.tp)
        st_s = Stage(me, net, small, small_v, False)
        st_q = Stage(me, net, wq, wq_v, True)
        st_o = Stage(me, net, wo, wo_v, True)
        st_f = Stage(me, net, wf, wf_v, True)
        st_p = Stage(me, net, wp, wp_o, False)
        tok_y.start()
        st_s.begin()
        st_s.begin_inner()
        st_q.begin()
        st_q.begin_inner()
        st_o.begin()
        st_o.begin_inner()
        st_f.begin()
        st_p.begin()
        loads = [
            own(tok.at[c], x.at[pl.ds(c * half, half)]),
            own(cot.at[c], gv.at[pl.ds(c * half, half)]),
            own(small, small_v.at[d]),
            own(wq, wq_v.at[d]),
            own(wo, wo_v.at[d]),
            own(wf, wf_v.at[d]),
        ]
        own(wp, wp_o.at[d])
        n_s = me.n_o - 1
        for s in range(n_s):
            st_s.relay(s)
        tok_y.wait_recv()
        tok_t.start()
        for s in (0, 2, 1) if n_s == 3 else range(n_s):
            st_q.relay(s)
        cot_y.start()
        st_s.arrive()
        loads[2].wait()
    else:
        loads = [own(tok, x), own(cot, gv), own(small, small_v), own(wq, wq_v), own(wo, wo_v),
                 own(wf, wf_v)]
        own(wp, wp_o)
        loads[2].wait()

    vec[...] = placed(small_v, 0, 0, shard, shard, 0, width)
    for s in range(2):
        bias[8 * s : 8 * s + 8, :] = placed(
            small_v, 6, s * (shard // 2), shard // 2, shard // 2, 0, cols
        )
    fcb[...] = placed(small_v, 7, 0, shard, 2 * shard, 0, fcb.shape[1])
    fcb[0:1, :] = fcb[0:1, :] + placed(small_v, 8, 0, shard, 2 * shard, shard, fcb.shape[1])[0:1, :]
    if direct:
        for s in range(me.n_o):
            st_q.cross(s)
        for s in (0, 2, 1) if n_s == 3 else range(n_s):
            st_o.relay(s)
        tok_t.wait_recv()
    loads[0].wait()

    @pl.loop(0, n_blocks)
    def _(j):
        at = block(j, step)
        n, _ = norm(x[at, :].astype(F32))
        low = (n * vec[0:1, :] + vec[1:2, :]).astype(BF16)
        h1[at, :] = low
        h1t[:, at] = low.T

    own(x, x_o)
    own(h1t, h1t_o)
    if direct:
        for s in range(me.n_o):
            st_o.cross(s)
        st_f.begin_inner()
        for s in (0, 2, 1) if n_s == 3 else range(n_s):
            st_f.relay(s)
        st_p.begin_inner()
        st_q.arrive()
    loads[3].wait()

    @pl.loop(0, n_blocks)
    def _(j):
        at = block(j, step)
        proj = dot(h1[at, :], wq_v[...].reshape(width, 3 * cols))
        q[at, :] = (proj[:, :cols] + bias[0:1, :]).astype(BF16) * SCALE
        kk = proj[:, cols : 2 * cols].astype(BF16)
        vv = (proj[:, 2 * cols :] + bias[8:9, :]).astype(BF16)
        k[at, :] = kk
        v[at, :] = vv
        kt[:, at] = kk.T
        vt[:, at] = vv.T

    own(wq_v, wq_o)
    for src, dst in ((q, q_o), (k, k_o), (v, v_o), (kt, kt_o)):
        own(src, dst)
    if direct:
        for s in range(me.n_o):
            st_f.cross(s)
        cot_y.wait_recv()
        cot_t.start()

    live = lax.broadcasted_iota(jnp.int32, (rows, step), 0) < length[0]
    side = lax.broadcasted_iota(jnp.int32, (step, 128), 1) // HD

    def spill(slot, p, at):
        return [
            pltpu.make_async_copy(pt.at[slot, hh], pt_o.at[p * 2 + hh, :, at], pts.at[slot, hh])
            for hh in range(2)
        ]

    steps = (cols // 128) * n_blocks

    @pl.loop(0, steps)
    def _(it):
        p, j = it // n_blocks, it % n_blocks
        pair, at, slot = block(p, 128), block(j, step), it % 2
        if direct:
            for s in range(n_s):

                @pl.when(it == 2 + 3 * s if n_s == 3 else it == 2)
                def _():
                    st_p.relay(s)

        @pl.when(it >= 2)
        def _():
            for copy in spill(slot, p, at):
                copy.wait()

        for hh in range(2):
            qm = jnp.where(side == hh, q[at, pair], jnp.zeros((), BF16))
            s = dot(k[:, pair], qm, NT)
            s = jnp.where(live, s, NEG)
            e = jnp.exp(s - jnp.max(s, axis=0, keepdims=True))
            pb = (e * (1.0 / jnp.sum(e, axis=0, keepdims=True))).astype(BF16)
            pt[slot, hh] = pb
            head = block(p * 2 + hh, HD)
            ot[head, at] = dot(vt[head, :], pb).astype(BF16)
        for copy in spill(slot, p, at):
            copy.start()

    for slot in range(2):
        for copy in spill(slot, 0, pl.ds(0, step)):
            copy.wait()
    own(ot, ot_o)
    if direct:
        st_o.arrive()
    loads[4].wait()

    @pl.loop(0, n_blocks)
    def _(j):
        at = block(j, step)
        ob = ot[:, at].T
        o[at, :] = ob
        ps[at, :] = dot(ob, wo_v[...].reshape(width, cols), NT).astype(BF16)

        @pl.when(j > 0)
        def _():
            exchange(j - 1).start()

    own(wo_v, wo_o)
    own(o, o_o)
    exchange(n_blocks - 1).start()
    if direct:
        cot_t.wait_recv()
        st_f.arrive()
    loads[1].wait()
    loads[5].wait()
    own(wf_v, wf_o)

    @pl.loop(0, n_blocks)
    def _(j):
        at = block(j, step)
        on = j * step + lax.broadcasted_iota(jnp.int32, (step, width), 0) < length[0]
        g = jnp.where(on, gv[at, :], jnp.zeros((), BF16))
        gm[at, :] = g
        gt[:, at] = g.T

    own(gm, g_o)
    own(gt, gt_o)

    @pl.loop(0, n_blocks)
    def _(j):
        at = block(j, step)
        exchange(j).wait_recv()
        mid = x[at, :].astype(F32) + (ps[at, :].astype(F32) + pr[at, :].astype(F32)) + vec[2:3, :]
        r1[at, :] = mid
        n, _ = norm(mid)
        h2 = (n * vec[3:4, :] + vec[4:5, :]).astype(BF16)
        h2t[:, at] = h2.T
        u = dot(h2, wf_v[...].reshape(width, fcb.shape[1])) + fcb[0:1, :]
        s = jax.nn.sigmoid(GELU * u)
        a[at, :] = (u * s).astype(BF16)
        sl[at, :] = (s * (1.0 + GELU * u * (1.0 - s))).astype(BF16)
        for n, (src, dst) in enumerate(((r1, r1_o), (a, a_o), (sl, sl_o))):
            pltpu.make_async_copy(src.at[at], dst.at[at], rows_s.at[n, j]).start()

    own(h2t, h2t_o)
    if direct:
        st_p.arrive()
    net.finish()

    @pl.loop(0, n_blocks)
    def _(j):
        at = block(j, step)
        exchange(j).wait_send()
        for n, (src, dst) in enumerate(((r1, r1_o), (a, a_o), (sl, sl_o))):
            pltpu.make_async_copy(src.at[at], dst.at[at], rows_s.at[n, j]).wait()

    for copy in done[6:]:
        copy.wait()


def mlp_kernel(g, a, sl, wf, wp, du, part2, part3):
    step = 256

    @pl.loop(0, g.shape[0] // step)
    def _(j):
        at = block(j, step)
        part2[at, :] = dot(a[at, :], wp[...], NT).astype(BF16)
        dub = (dot(g[at, :], wp[...]) * sl[at, :].astype(F32)).astype(BF16)
        du[at, :] = dub
        part3[at, :] = dot(dub, wf[...], NT).astype(BF16)


def weights_kernel(gt, h2t, a, du, gp, gf, bp, bfg):
    width = gt.shape[0]
    step = 128

    @pl.loop(0, width // step)
    def _(j):
        at = block(j, step)
        gp[at, :] = dot(gt[at, :], a[...]).astype(BF16)
        gf[at, :] = dot(h2t[at, :], du[...]).astype(BF16)

    bp[...] = jnp.zeros_like(bp)
    bfg[...] = jnp.zeros_like(bfg)

    @pl.loop(0, du.shape[0] // 128)
    def _(j):
        at = block(j, 128)
        bfg[...] += jnp.sum(du[at, :].astype(F32), axis=0, keepdims=True)
        bp[...] += jnp.sum(gt[:, at].astype(F32).T, axis=0, keepdims=True)


def middle_kernel(
    gs, vec, r1, p2a, p2b, p3a, p3b, o, wo, out, dr1, do, go, sums, dt
):
    rows, width = gs.shape
    step = 256
    sums[...] = jnp.zeros_like(sums)

    @pl.loop(0, rows // step)
    def _(j):
        at = block(j, step)
        mid = r1[at, :]
        out[at, :] = (
            mid + (p2a[at, :].astype(F32) + p2b[at, :].astype(F32)) + vec[5:6, :]
        ).astype(BF16)
        n, inv = norm(mid)
        dh = p3a[at, :].astype(F32) + p3b[at, :].astype(F32)
        e = dh * vec[3:4, :]
        grad = gs[at, :].astype(F32) + inv * (
            e - jnp.mean(e, axis=-1, keepdims=True) - n * jnp.mean(e * n, axis=-1, keepdims=True)
        )
        dr1[at, :] = grad
        sums[0:1, :] += jnp.sum(grad, axis=0, keepdims=True)
        sums[1:2, :] += jnp.sum(dh * n, axis=0, keepdims=True)
        sums[2:3, :] += jnp.sum(dh, axis=0, keepdims=True)
        gb = grad.astype(BF16)
        dt[:, at] = gb.T
        do[at, :] = dot(gb, wo[...]).astype(BF16)

    @pl.loop(0, width // step)
    def _(j):
        at = block(j, step)
        go[at, :] = dot(dt[at, :], o[...]).astype(BF16)


def backward_kernel(
    q, k, v, kt, h1t, ot, pt, do, wq, gq, part, sums, dot_t, dst, dqt, dqkv
):
    rows, cols = q.shape
    step = 256
    side = lax.broadcasted_iota(jnp.int32, (step, 128), 1) // HD
    side_all = lax.broadcasted_iota(jnp.int32, (rows, 128), 1) // HD
    zero = jnp.zeros((), BF16)

    @pl.loop(0, rows // step)
    def _(j):
        at = block(j, step)
        dot_t[:, at] = do[at, :].T

    @pl.loop(0, cols // 128)
    def _(p):
        pair = block(p, 128)
        for hh in range(2):
            head = block(p * 2 + hh, HD)

            @pl.loop(0, rows // step)
            def _(j):
                at = block(j, step)
                inner = jnp.sum(
                    dot_t[head, at].astype(F32) * ot[head, at].astype(F32), axis=0, keepdims=True
                )
                dp = dot(v[:, pair], jnp.where(side == hh, do[at, pair], zero), NT)
                ds = (pt[p * 2 + hh, :, at].astype(F32) * (dp - inner)).astype(BF16)
                dst[hh, :, at] = ds
                dqt[head, at] = dot(kt[head, :], ds)

        qp = q[:, pair]
        dp_ = do[:, pair]
        dk = dot(dst[0], jnp.where(side_all == 0, qp, zero)) + dot(
            dst[1], jnp.where(side_all == 1, qp, zero)
        )
        dv = dot(pt[p * 2], jnp.where(side_all == 0, dp_, zero)) + dot(
            pt[p * 2 + 1], jnp.where(side_all == 1, dp_, zero)
        )
        dqkv[:, pl.ds(pl.multiple_of(cols + p * 128, 128), 128)] = dk.astype(BF16)
        dqkv[:, pl.ds(pl.multiple_of(2 * cols + p * 128, 128), 128)] = dv.astype(BF16)

    sums[...] = jnp.zeros_like(sums)

    @pl.loop(0, rows // step)
    def _(j):
        at = block(j, step)
        dqkv[at, 0:cols] = (dqt[:, at].T * SCALE).astype(BF16)
        low = dqkv[at, :]
        sums[0:1, :] += jnp.sum(low.astype(F32), axis=0, keepdims=True)
        part[at, :] = dot(low, wq[...], NT).astype(BF16)

    @pl.loop(0, h1t.shape[0] // step)
    def _(j):
        at = block(j, step)
        gq[at, :] = dot(h1t[at, :], dqkv[...]).astype(BF16)


def last_kernel(xs, vec, dr1, pa, pb, gtok, sums):
    rows, width = xs.shape
    step = 256
    sums[...] = jnp.zeros_like(sums)

    @pl.loop(0, rows // step)
    def _(j):
        at = block(j, step)
        n, inv = norm(xs[at, :].astype(F32))
        dh = pa[at, :].astype(F32) + pb[at, :].astype(F32)
        e = dh * vec[0:1, :]
        gtok[at, :] = (
            dr1[at, :]
            + inv
            * (e - jnp.mean(e, axis=-1, keepdims=True) - n * jnp.mean(e * n, axis=-1, keepdims=True))
        ).astype(BF16)
        sums[0:1, :] += jnp.sum(dh * n, axis=0, keepdims=True)
        sums[1:2, :] += jnp.sum(dh, axis=0, keepdims=True)


VM = pl.BlockSpec(memory_space=pltpu.VMEM)
SM = pl.BlockSpec(memory_space=pltpu.SMEM)
ANY = pl.BlockSpec(memory_space=pl.ANY)


def call(body, ins, outs, scratch=(), specs=None, out_specs=None, name=None, cid=None):
    params = dict(vmem_limit_bytes=LIMIT)
    if cid is not None:
        params.update(collective_id=cid, has_side_effects=True)
    return pl.pallas_call(
        body,
        out_shape=[jax.ShapeDtypeStruct(s, t) for s, t in outs],
        in_specs=specs or [VM] * len(ins),
        out_specs=out_specs or [VM] * len(outs),
        scratch_shapes=list(scratch),
        name=name,
        compiler_params=pltpu.CompilerParams(**params),
    )(*ins)


def on_device(n_dp, tokens, lengths, ln1_gain, ln1_bias, w_qkv, qv_bias, w_out, out_bias,
              ln2_gain, ln2_bias, w_fc, fc_bias, w_proj, proj_bias, cotangent):
    _, half, width = tokens.shape
    rows = 2 * half
    shard = w_fc.shape[0]
    cols = w_out.shape[1]
    ff = w_fc.shape[1]
    dma = pltpu.SemaphoreType.DMA
    ctx = lax.axis_index("ctx")
    length = lax.dynamic_slice(lengths, (ctx,), (1,))
    lines = [ln1_gain, ln1_bias, out_bias, ln2_gain, ln2_bias, proj_bias,
             qv_bias[:, :, 0].T.reshape(shard)] + list(fc_bias[:, 0].reshape(2, shard))
    small = jnp.pad(jnp.stack(lines), ((0, 16 - len(lines)), (0, 128 - shard)))
    wq_own = w_qkv.reshape(shard, 3 * cols)
    direct = n_dp == 8
    if direct:
        ins = (length, tokens, cotangent, small, wq_own, w_out, w_fc, w_proj)
    else:
        def whole(a):
            return lax.dynamic_index_in_dim(
                lax.all_gather(a, "ctx", axis=1, tiled=True), ctx, 0, False)

        ins = (length, whole(tokens), whole(cotangent)) + tuple(
            lax.all_gather(a, "dp") for a in (small, wq_own, w_out, w_fc, w_proj))
    act = ((rows, width), BF16)
    act_t = ((width, rows), BF16)
    head = ((rows, cols), BF16)
    head_t = ((cols, rows), BF16)
    wide = ((rows, ff), BF16)
    mats = [((n_dp, shard, n), BF16) for n in (3 * cols, cols, ff, ff)]
    outs = [((8, width), F32), act, act_t, act, act_t, head, head, head, head_t, head, head_t,
            ((cols // HD, rows, rows), BF16), ((rows, width), F32), wide, wide, act_t] + mats
    step = 256
    held = [((n_dp, 16, 128), F32)] + mats[:3] + [
        act, act, act, act_t, act, act_t, head, head, head, head_t, head_t, head, head_t,
        ((2, 2, rows, step), BF16), act, act, ((rows, width), F32), wide, wide, act_t,
        ((16, cols), F32), ((8, ff), F32)]
    (vec, g, gt, xs, h1t, q, k, v, kt, o, ot, pt, r1, a, sl, h2t, wq, wo, wf, wp) = call(
        functools.partial(forward_kernel, n_dp, direct), ins, outs,
        [pltpu.VMEM(*h) for h in held]
        + [dma((72,)), dma((72,)), dma((40,)), dma((2, 2)), dma((3, rows // step))],
        [SM] + [ANY] * 7, [VM] + [ANY] * 19, "forward", 1)
    wq, wo, wf, wp = [w.reshape(width, -1) for w in (wq, wo, wf, wp)]

    def other(a):
        return lax.ppermute(a, "tp", [(0, 1), (1, 0)])

    du, part2, part3 = call(mlp_kernel, (g, a, sl, wf, wp), [wide, act, act], name="mlp")
    gp, gf, bp, bfg = call(
        weights_kernel, (gt, h2t, a, du),
        [((width, ff), BF16), ((width, ff), BF16), ((1, width), F32), ((1, ff), F32)],
        name="weights")
    out_seq, dr1, do, go, sums2 = call(
        middle_kernel,
        (g, vec, r1, part2, other(part2), part3, other(part3), o, wo),
        [act, ((rows, width), F32), head, ((width, cols), BF16), ((8, width), F32)],
        [pltpu.VMEM((width, rows), BF16)], name="middle")
    gq, part4, sums3 = call(
        backward_kernel, (q, k, v, kt, h1t, ot, pt, do, wq),
        [((width, 3 * cols), BF16), act, ((8, 3 * cols), F32)],
        [pltpu.VMEM((cols, rows), BF16), pltpu.VMEM((2, rows, rows), BF16),
         pltpu.VMEM((cols, rows), F32), pltpu.VMEM((rows, 3 * cols), BF16)], name="backward")
    tok_seq, sums1 = call(
        last_kernel, (xs, vec, dr1, part4, other(part4)),
        [act, ((8, width), F32)], name="last")

    gvec = jnp.concatenate([sums1[0:2], sums2[0:3], bp])
    gvec = gvec.reshape(6, n_dp, shard).transpose(1, 0, 2)
    gqv = jnp.stack([sums3[0, :cols], sums3[0, 2 * cols :]]).reshape(2, n_dp, shard // 2)
    gqv = gqv.transpose(1, 0, 2).reshape(n_dp, 1, shard)
    gsmall = jnp.concatenate([gvec, gqv, bfg.reshape(n_dp, 2, shard)], axis=1)
    gsmall = jnp.pad(gsmall, ((0, 0), (0, 7), (0, 128 - shard)))
    gq, go, gf, gp = [a.reshape(n_dp, shard, -1) for a in (gq, go, gf, gp)]
    if n_dp == 8:
        n_o = n_dp // 2
        scratch = []
        for n, r, kind in ((3 * cols, shard, BF16), (cols, shard, BF16), (ff, shard, BF16),
                           (ff, shard, BF16), (128, 16, F32)):
            scratch += [pltpu.VMEM((n_o, r, n), kind), pltpu.VMEM((n_o - 1, r, n), kind),
                        pltpu.VMEM((n_o, r, n), kind), pltpu.VMEM((2, r, n), kind)]
        rq, ro, rf, rp, rs, out, gtok = call(
            functools.partial(reduce_kernel, n_dp),
            (gq, go, gf, gp, gsmall, out_seq, tok_seq),
            [((shard, 3 * cols), F32), ((shard, cols), F32), ((shard, ff), F32),
             ((shard, ff), F32), ((16, 128), F32), ((2, half, width), BF16),
             ((2, half, width), BF16)],
            scratch + [dma((64,)), dma((64,)), dma((2,))],
            [VM] * 5 + [ANY] * 2, [VM] * 5 + [ANY] * 2, "reduce", 2)
    else:
        def summed(a):
            return lax.psum(lax.psum_scatter(a, "dp", scatter_dimension=0), "ctx")

        rq, ro, rf, rp = [summed(a).astype(F32) for a in (gq, go, gf, gp)]
        rs = summed(gsmall)

        def back(a):
            pieces = lax.all_gather(a, "ctx", axis=0)
            return lax.dynamic_slice(pieces, (0, ctx * half, 0), (2, half, width))

        out, gtok = back(out_seq), back(tok_seq)
    line = [rs[j, :shard] for j in range(7)]
    return (out, gtok, line[0], line[1], rq.reshape(shard, 3, cols),
            line[6].reshape(2, shard // 2).T[:, :, None], ro, line[2], line[3], line[4],
            rf, rs[7:9, :shard].reshape(2 * shard, 1), rp, line[5])


def solution(mesh):
    dp, seq = P("dp"), P("dp", "ctx", None)
    wide, flat = P("dp", None, "tp"), P("dp", "tp")
    params = (dp, dp, wide, wide, flat, dp, dp, dp, flat, flat, flat, dp)
    return jax.shard_map(
        functools.partial(on_device, mesh.shape["dp"]),
        mesh=mesh,
        in_specs=(seq, dp) + params + (seq,),
        out_specs=(seq, seq) + params,
        check_vma=False,
    )
```

```python
import functools

import jax
import jax.numpy as jnp
from jax import lax
from jax.experimental import pallas as pl
from jax.experimental.pallas import tpu as pltpu
from jax.sharding import PartitionSpec as P

HD = 64
EPS = 1e-05
NEG = -1e30
GELU = 1.702
SCALE = HD ** (-0.5)
F32 = jnp.float32
BF16 = jnp.bfloat16
MESH = pl.DeviceIdType.MESH
LIMIT = 67_000_000
NN = (((1,), (0,)), ((), ()))
NT = (((1,), (1,)), ((), ()))


def dot(a, b, dims=NN):
    return lax.dot_general(a, b, dims, preferred_element_type=F32)


class Net:
    def __init__(self, send, recv):
        self.send, self.recv, self.used, self.all = send, recv, 0, []

    def build(self, k, src, dst, dev):
        return pltpu.make_async_remote_copy(
            src_ref=src, dst_ref=dst, send_sem=self.send.at[k], recv_sem=self.recv.at[k],
            device_id=dev, device_id_type=MESH,
        )

    def take(self, count):
        self.used += count
        return self.used - count

    def make(self, src, dst, dev):
        copy = self.build(self.take(1), src, dst, dev)
        self.all.append(copy)
        return copy

    def put(self, src, dst, dev):
        copy = self.make(src, dst, dev)
        copy.start()
        return copy

    def finish(self):
        for copy in self.all:
            copy.wait_send()


class Place:
    def __init__(self, n_dp, direct=True):
        self.d = lax.axis_index("dp")
        self.c = lax.axis_index("ctx")
        self.t = lax.axis_index("tp")
        self.direct = direct
        self.n_o = n_dp // 2
        self.o, self.i = self.d // 2, self.d % 2

    def outer(self, s):
        return (lax.rem(self.o + s, self.n_o) * 2 + self.i, self.c, self.t)

    def from_outer(self, s):
        return lax.rem(self.o + self.n_o - s, self.n_o) * 2 + self.i

    @property
    def inner(self):
        return (self.o * 2 + 1 - self.i, self.c, self.t)

    @property
    def ctx(self):
        return (self.d, 1 - self.c, self.t)

    @property
    def tp(self):
        return (self.d, self.c, 1 - self.t)

    def barrier(self, ctx=False):
        sem = pltpu.get_barrier_semaphore()
        peers = [self.tp]
        if self.direct or ctx:
            peers.append(self.ctx)
        if self.direct:
            peers += [self.outer(s) for s in range(1, self.n_o)] + [self.inner]
        for peer in peers:
            pl.semaphore_signal(sem, 1, device_id=peer, device_id_type=MESH)
        pl.semaphore_wait(sem, len(peers))


def add_rows(dst, parts, rows, step):
    @pl.loop(0, rows // step)
    def _(j):
        at = pl.ds(pl.multiple_of(j * step, step), step)
        total = parts[0][at, :].astype(F32)
        for part in parts[1:]:
            total = total + part[at, :].astype(F32)
        dst[at, :] = total.astype(dst.dtype)


def norm(x):
    centred = x - jnp.mean(x, axis=-1, keepdims=True)
    inv = lax.rsqrt(jnp.mean(centred * centred, axis=-1, keepdims=True) + EPS)
    return centred * inv, inv


def block(j, size):
    return pl.ds(pl.multiple_of(j * size, size), size)


class Stage:
    def __init__(self, me, net, src, dst, halves):
        self.src, self.dst, self.halves, self.me = src, dst, halves, me
        rows = dst.shape[1]
        part = pl.ds(me.c * (rows // 2), rows // 2)

        def cut(dev):
            return dst.at[dev, part] if halves else dst.at[dev]

        own = src.at[part] if halves else src
        shifts = list(range(1, me.n_o))
        self.outer = [net.make(own, cut(me.d), me.outer(s)) for s in shifts]
        self.inner = [net.make(own, cut(me.d), me.inner)]
        self.ctx = []
        for s in shifts:
            piece = cut(me.from_outer(s))
            self.inner.append(net.make(piece, piece, me.inner))
            if halves:
                self.ctx.append(net.make(piece, piece, me.ctx))
        self.far = []
        if halves:
            for s in [0] + shifts:
                piece = cut(lax.rem(me.o + me.n_o - s, me.n_o) * 2 + 1 - me.i)
                self.far.append(net.make(piece, piece, me.ctx))

    def begin(self):
        for copy in self.outer:
            copy.start()

    def begin_inner(self):
        self.inner[0].start()

    def relay(self, s):
        self.outer[s].wait_recv()
        self.inner[s + 1].start()
        if self.halves:
            self.ctx[s].start()

    def cross(self, s):
        self.inner[s].wait_recv()
        self.far[s].start()

    def arrive(self):
        for copy in self.ctx + self.far if self.halves else self.inner:
            copy.wait_recv()


def placed(small_all, row, first, count, stride, offset, size):
    lane = lax.broadcasted_iota(jnp.int32, (128, size), 0)
    col = lax.broadcasted_iota(jnp.int32, (128, size), 1)
    inside = (lane >= first) & (lane < first + count)

    def add(d, total):
        spot = inside & (col == lane - first + (d * stride + offset))
        return total + lax.dot_general(
            small_all[d, row : row + 8, :], spot.astype(F32), NN,
            precision=lax.Precision.HIGHEST, preferred_element_type=F32,
        )

    return lax.fori_loop(0, small_all.shape[0], add, jnp.zeros((8, size), F32))


def forward_kernel(
    n_dp, direct, length, tok, cot, small, wq, wo, wf, wp,
    vec, g_o, gt_o, x_o, h1t_o, q_o, k_o, v_o, kt_o, o_o, ot_o, pt_o, r1_o, a_o, sl_o, h2t_o,
    wq_o, wo_o, wf_o, wp_o,
    small_v, wq_v, wo_v, wf_v, x, gv, gm, gt, h1, h1t, q, k, v, kt, vt, o, ot, pt, ps, pr, r1, a, sl, h2t,
    bias, fcb, send, recv, local, pts, rows_s,
):
    me = Place(n_dp, direct)
    net = Net(send, recv)
    d, c, t = me.d, me.c, me.t
    rows, width = x.shape
    cols = q.shape[1]
    half, step = rows // 2, 256
    quarter = half // 2
    shard = width // n_dp
    n_blocks = rows // step
    me.barrier()
    done = []

    def own(src, dst):
        copy = pltpu.make_async_copy(src, dst, local.at[len(done)])
        copy.start()
        done.append(copy)
        return copy

    mine = pl.ds(c * half + t * quarter, quarter)
    theirs = pl.ds((1 - c) * half + t * quarter, quarter)
    first = net.take(n_blocks)

    def exchange(j):
        at = block(j, step)
        return net.build(first + j, ps.at[at], pr.at[at], me.tp)

    if direct:
        tok_y = net.make(tok.at[1 - c, pl.ds(t * quarter, quarter)], x.at[mine], me.ctx)
        tok_t = net.make(x.at[theirs], x.at[theirs], me.tp)
        cot_y = net.make(cot.at[1 - c, pl.ds(t * quarter, quarter)], gv.at[mine], me.ctx)
        cot_t = net.make(gv.at[theirs], gv.at[theirs], me.tp)
        st_s = Stage(me, net, small, small_v, False)
        st_q = Stage(me, net, wq, wq_v, True)
        st_o = Stage(me, net, wo, wo_v, True)
        st_f = Stage(me, net, wf, wf_v, True)
        st_p = Stage(me, net, wp, wp_o, False)
        tok_y.start()
        st_s.begin()
        st_s.begin_inner()
        st_q.begin()
        st_q.begin_inner()
        st_o.begin()
        st_o.begin_inner()
        st_f.begin()
        st_p.begin()
        loads = [
            own(tok.at[c], x.at[pl.ds(c * half, half)]),
            own(cot.at[c], gv.at[pl.ds(c * half, half)]),
            own(small, small_v.at[d]),
            own(wq, wq_v.at[d]),
            own(wo, wo_v.at[d]),
            own(wf, wf_v.at[d]),
        ]
        own(wp, wp_o.at[d])
        n_s = me.n_o - 1
        for s in range(n_s):
            st_s.relay(s)
        tok_y.wait_recv()
        tok_t.start()
        for s in (0, 2, 1) if n_s == 3 else range(n_s):
            st_q.relay(s)
        cot_y.start()
        st_s.arrive()
        loads[2].wait()
    else:
        loads = [own(tok, x), own(cot, gv), own(small, small_v), own(wq, wq_v), own(wo, wo_v),
                 own(wf, wf_v)]
        own(wp, wp_o)
        loads[2].wait()

    vec[...] = placed(small_v, 0, 0, shard, shard, 0, width)
    for s in range(2):
        bias[8 * s : 8 * s + 8, :] = placed(
            small_v, 6, s * (shard // 2), shard // 2, shard // 2, 0, cols
        )
    fcb[...] = placed(small_v, 7, 0, shard, 2 * shard, 0, fcb.shape[1])
    fcb[0:1, :] = fcb[0:1, :] + placed(small_v, 8, 0, shard, 2 * shard, shard, fcb.shape[1])[0:1, :]
    if direct:
        for s in range(me.n_o):
            st_q.cross(s)
        for s in (0, 2, 1) if n_s == 3 else range(n_s):
            st_o.relay(s)
        tok_t.wait_recv()
    loads[0].wait()

    @pl.loop(0, n_blocks)
    def _(j):
        at = block(j, step)
        n, _ = norm(x[at, :].astype(F32))
        low = (n * vec[0:1, :] + vec[1:2, :]).astype(BF16)
        h1[at, :] = low
        h1t[:, at] = low.T

    own(x, x_o)
    own(h1t, h1t_o)
    if direct:
        for s in range(me.n_o):
            st_o.cross(s)
        st_f.begin_inner()
        for s in (0, 2, 1) if n_s == 3 else range(n_s):
            st_f.relay(s)
        st_p.begin_inner()
        st_q.arrive()
    loads[3].wait()

    @pl.loop(0, n_blocks)
    def _(j):
        at = block(j, step)
        proj = dot(h1[at, :], wq_v[...].reshape(width, 3 * cols))
        q[at, :] = (proj[:, :cols] + bias[0:1, :]).astype(BF16) * SCALE
        kk = proj[:, cols : 2 * cols].astype(BF16)
        vv = (proj[:, 2 * cols :] + bias[8:9, :]).astype(BF16)
        k[at, :] = kk
        v[at, :] = vv
        kt[:, at] = kk.T
        vt[:, at] = vv.T

    own(wq_v, wq_o)
    for src, dst in ((q, q_o), (k, k_o), (v, v_o), (kt, kt_o)):
        own(src, dst)
    if direct:
        for s in range(me.n_o):
            st_f.cross(s)
        cot_y.wait_recv()
        cot_t.start()

    live = lax.broadcasted_iota(jnp.int32, (rows, step), 0) < length[0]
    side = lax.broadcasted_iota(jnp.int32, (step, 128), 1) // HD

    def spill(slot, p, at):
        return [
            pltpu.make_async_copy(pt.at[slot, hh], pt_o.at[p * 2 + hh, :, at], pts.at[slot, hh])
            for hh in range(2)
        ]

    steps = (cols // 128) * n_blocks

    @pl.loop(0, steps)
    def _(it):
        p, j = it // n_blocks, it % n_blocks
        pair, at, slot = block(p, 128), block(j, step), it % 2
        if direct:
            for s in range(n_s):

                @pl.when(it == 2 + 3 * s if n_s == 3 else it == 2)
                def _():
                    st_p.relay(s)

        @pl.when(it >= 2)
        def _():
            for copy in spill(slot, p, at):
                copy.wait()

        for hh in range(2):
            qm = jnp.where(side == hh, q[at, pair], jnp.zeros((), BF16))
            s = dot(k[:, pair], qm, NT)
            s = jnp.where(live, s, NEG)
            e = jnp.exp(s - jnp.max(s, axis=0, keepdims=True))
            pb = (e * (1.0 / jnp.sum(e, axis=0, keepdims=True))).astype(BF16)
            pt[slot, hh] = pb
            head = block(p * 2 + hh, HD)
            ot[head, at] = dot(vt[head, :], pb).astype(BF16)
        for copy in spill(slot, p, at):
            copy.start()

    for slot in range(2):
        for copy in spill(slot, 0, pl.ds(0, step)):
            copy.wait()
    own(ot, ot_o)
    if direct:
        st_o.arrive()
    loads[4].wait()

    @pl.loop(0, n_blocks)
    def _(j):
        at = block(j, step)
        ob = ot[:, at].T
        o[at, :] = ob
        ps[at, :] = dot(ob, wo_v[...].reshape(width, cols), NT).astype(BF16)

        @pl.when(j > 0)
        def _():
            exchange(j - 1).start()

    own(wo_v, wo_o)
    own(o, o_o)
    exchange(n_blocks - 1).start()
    if direct:
        cot_t.wait_recv()
        st_f.arrive()
    loads[1].wait()
    loads[5].wait()
    own(wf_v, wf_o)

    @pl.loop(0, n_blocks)
    def _(j):
        at = block(j, step)
        on = j * step + lax.broadcasted_iota(jnp.int32, (step, width), 0) < length[0]
        g = jnp.where(on, gv[at, :], jnp.zeros((), BF16))
        gm[at, :] = g
        gt[:, at] = g.T

    own(gm, g_o)
    own(gt, gt_o)

    @pl.loop(0, n_blocks)
    def _(j):
        at = block(j, step)
        exchange(j).wait_recv()
        mid = x[at, :].astype(F32) + (ps[at, :].astype(F32) + pr[at, :].astype(F32)) + vec[2:3, :]
        r1[at, :] = mid
        n, _ = norm(mid)
        h2 = (n * vec[3:4, :] + vec[4:5, :]).astype(BF16)
        h2t[:, at] = h2.T
        u = dot(h2, wf_v[...].reshape(width, fcb.shape[1])) + fcb[0:1, :]
        s = jax.nn.sigmoid(GELU * u)
        a[at, :] = (u * s).astype(BF16)
        sl[at, :] = (s * (1.0 + GELU * u * (1.0 - s))).astype(BF16)
        for n, (src, dst) in enumerate(((r1, r1_o), (a, a_o), (sl, sl_o))):
            pltpu.make_async_copy(src.at[at], dst.at[at], rows_s.at[n, j]).start()

    own(h2t, h2t_o)
    if direct:
        st_p.arrive()
    net.finish()

    @pl.loop(0, n_blocks)
    def _(j):
        at = block(j, step)
        exchange(j).wait_send()
        for n, (src, dst) in enumerate(((r1, r1_o), (a, a_o), (sl, sl_o))):
            pltpu.make_async_copy(src.at[at], dst.at[at], rows_s.at[n, j]).wait()

    for copy in done[6:]:
        copy.wait()


def gather_lanes(dst, values, first, count, stride, offset):
    size = values.shape[1]
    lane = lax.broadcasted_iota(jnp.int32, (128, size), 0)
    col = lax.broadcasted_iota(jnp.int32, (128, size), 1)
    inside = (lane >= first) & (lane < first + count)

    @pl.loop(0, dst.shape[0])
    def _(d):
        spot = inside & (col == lane - first + (d * stride + offset))
        dst[d] += lax.dot_general(
            values, spot.astype(F32), NT,
            precision=lax.Precision.HIGHEST, preferred_element_type=F32,
        )


class Sum:
    def __init__(self, me, net, g, x, z, y, step):
        self.me, self.g, self.x, self.z, self.y, self.step = me, g, x, z, y, step
        self.shifts = list(range(1, me.n_o))
        self.order = self.shifts + [0]
        self.one = {
            s: net.make(g.at[self.at(s) * 2 + 1 - me.i], x.at[s], me.inner) for s in self.order
        }
        self.two = {
            s: net.make(g.at[self.at(s) * 2 + me.i], z.at[s - 1], me.outer(s)) for s in self.shifts
        }
        self.three = net.make(g.at[me.d], y, me.ctx)

    def at(self, s):
        return lax.rem(self.me.o + s, self.me.n_o)

    def begin(self):
        for s in self.order:
            self.one[s].start()

    def add(self, s):
        self.one[s].wait_recv()
        part = self.g.at[self.at(s) * 2 + self.me.i]
        add_rows(part, [part, self.x.at[s]], part.shape[0], self.step)
        if s:
            self.two[s].start()

    def total(self):
        for s in self.shifts:
            self.two[s].wait_recv()
        part = self.g.at[self.me.d]
        add_rows(part, [part] + [self.z.at[s - 1] for s in self.shifts], part.shape[0], self.step)
        self.three.start()

    def final(self, write):
        self.three.wait_recv()
        part = self.g.at[self.me.d]

        @pl.loop(0, part.shape[0] // self.step)
        def _(j):
            at = block(j, self.step)
            write(at, part[at, :].astype(F32) + self.y[at, :].astype(F32))


class SumCtx:
    def __init__(self, me, net, g, y, x, z, w, step):
        self.me, self.g, self.y, self.x, self.z, self.w, self.step = me, g, y, x, z, w, step
        self.rows = g.shape[1] // 2
        self.shifts = list(range(1, me.n_o))
        self.order = self.shifts + [0]
        self.mine = pl.ds(me.c * self.rows, self.rows)
        other = pl.ds((1 - me.c) * self.rows, self.rows)
        self.zero, self.zero_own = {}, {}
        for s in self.order:
            dev = self.at(s) * 2 + 1 - me.i
            self.zero[s] = net.make(g.at[dev, other], y.at[dev], me.ctx)
        for s in self.order:
            dev = self.at(s) * 2 + me.i
            self.zero_own[s] = net.make(g.at[dev, other], y.at[dev], me.ctx)
        self.one = {
            s: net.make(g.at[self.at(s) * 2 + 1 - me.i, self.mine], x.at[s], me.inner)
            for s in self.order
        }
        self.two = {
            s: net.make(g.at[self.at(s) * 2 + me.i, self.mine], z.at[s - 1], me.outer(s))
            for s in self.shifts
        }
        self.three = net.make(g.at[me.d, self.mine], w, me.ctx)

    at = Sum.at

    def begin_row(self, s):
        self.zero[s].start()
        self.zero_own[s].start()

    def cross(self, s):
        self.zero[s].wait_recv()
        dev = self.at(s) * 2 + 1 - self.me.i
        part = self.g.at[dev, self.mine]
        add_rows(part, [part, self.y.at[dev]], self.rows, self.step)
        self.one[s].start()

    def add(self, s):
        self.zero_own[s].wait_recv()
        self.one[s].wait_recv()
        dev = self.at(s) * 2 + self.me.i
        part = self.g.at[dev, self.mine]
        add_rows(part, [part, self.y.at[dev], self.x.at[s]], self.rows, self.step)
        if s:
            self.two[s].start()

    def total(self):
        for s in self.shifts:
            self.two[s].wait_recv()
        part = self.g.at[self.me.d, self.mine]
        add_rows(part, [part] + [self.z.at[s - 1] for s in self.shifts], self.rows, self.step)
        self.three.start()

    def final(self, write):
        self.three.wait_recv()
        part = self.g.at[self.me.d, self.mine]

        @pl.loop(0, self.rows // self.step)
        def _(j):
            at = block(j, self.step)
            here = pl.ds(pl.multiple_of(self.me.c * self.rows + j * self.step, self.step), self.step)
            there = pl.ds(
                pl.multiple_of((1 - self.me.c) * self.rows + j * self.step, self.step), self.step
            )
            write(here, part[at, :].astype(F32))
            write(there, self.w[at, :].astype(F32))


def backward_kernel(
    n_dp, direct, vec, g_i, gt_i, x_i, h1t_i, q_i, k_i, v_i, kt_i, o_i, ot_i, pt_i, r1_i, a_i,
    sl_i, h2t_i, wq_i, wo_i, wf_i, wp_i, *refs
):
    n_out = 7
    out, gtok, rsmall, rq, ro, rf, rp = refs[:n_out]
    (wq, wo, wf, wp, a, du, g, gt, ht, p2s, p2r, p3s, p3r, p4r, gp, gf, go, gq, small,
     r1, o, do, dot_t, q, k, v, kt, ot, pt, dqt, dqkv, sums, low_sums, fcs, qvs) = refs[n_out : n_out + 35]
    refs = refs[n_out + 35 :]
    send, recv, local = refs[-3:]
    buffers = refs[:-3]
    me = Place(n_dp, direct)
    net = Net(send, recv)
    d, c, t = me.d, me.c, me.t
    rows, width = g.shape
    cols = q.shape[1]
    ff = a.shape[1]
    half, step = rows // 2, 256
    quarter = half // 2
    n_blocks = rows // step
    groups, shard = gp.shape[0], gp.shape[1]
    n_pairs = cols // 128
    pending = []

    def load(src, dst):
        copy = pltpu.make_async_copy(src, dst, local.at[len(pending)])
        copy.start()
        pending.append(copy)
        return copy

    l_gt, l_a = load(gt_i, gt), load(a_i, a)
    l_w = [load(wp_i, wp), load(wf_i, wf), load(g_i, g), load(sl_i, du)]
    l_h2 = load(h2t_i, ht)
    l_m = [load(r1_i, r1), load(wo_i, wo), load(o_i, o)]
    l_b = [load(q_i, q), load(k_i, k), load(v_i, v), load(kt_i, kt), load(ot_i, ot), load(wq_i, wq)]
    l_pt = load(pt_i.at[pl.ds(0, 2)], pt)
    me.barrier(True)

    def swap(first, src, dst, j):
        at = block(j, step)
        return net.build(first + j, src.at[at], dst.at[at], me.tp)

    f2, f3, f4 = net.take(n_blocks), net.take(n_blocks), net.take(n_blocks)
    ex2 = lambda j: swap(f2, p2s, p2r, j)
    ex3 = lambda j: swap(f3, p3s, p3r, j)
    ex4 = lambda j: swap(f4, p2s, p4r, j)
    lead = (1 - c) * (n_blocks // 2) + t
    mine = pl.ds((1 - c) * half + t * quarter, quarter)
    there = pl.ds(t * quarter, quarter)
    out_y = net.make(p2r.at[mine], out.at[c, there], me.ctx)
    out_t = net.make(out.at[1 - c, there], out.at[1 - c, there], me.tp)
    tok_y = net.make(p4r.at[mine], gtok.at[c, there], me.ctx)
    tok_t = net.make(gtok.at[1 - c, there], gtok.at[1 - c, there], me.tp)

    def write_to(ref):
        def write(at, value):
            ref[at, :] = value
        return write

    if direct:
        b = list(buffers)
        s_p = Sum(me, net, gp, b[0], b[1], b[2], 16)
        s_f = SumCtx(me, net, gf, b[3], b[4], b[5], b[6], 16)
        s_o = Sum(me, net, go, b[7], b[8], b[9], 16)
        s_q = [
            Sum(me, net, gq.at[p], b[10].at[p], b[11].at[p], b[12].at[p], 16)
            for p in range(n_pairs)
        ]
        s_s = Sum(me, net, small, b[13], b[14], b[15], 8)
        order = s_p.order
    two = 2 * shard
    n_z = width // two

    def weight_rows(dst, lhs, rhs, each):
        @pl.loop(0, n_z)
        def _(s):
            zz = lax.rem(me.o + 1 + s, n_z) if direct else s
            value = dot(lhs[pl.ds(pl.multiple_of(zz * two, two), two), :], rhs)
            value = value.astype(BF16).reshape(2, shard, value.shape[1])
            dst[pl.ds(pl.multiple_of(zz * 2, 2), 2)] = value
            if each is not None:
                for n in range(n_z):

                    @pl.when(s == n)
                    def _():
                        each((n + 1) % n_z)

    l_gt.wait()
    l_a.wait()
    weight_rows(gp, gt, a[...], (lambda s: s_p.one[s].start()) if direct else None)
    for copy in l_w:
        copy.wait()

    @pl.loop(0, n_blocks)
    def _(j):
        at = block(j, step)
        wp_all = wp[...].reshape(width, ff)
        p2s[at, :] = dot(a[at, :], wp_all, NT).astype(BF16)
        low = (dot(g[at, :], wp_all) * du[at, :].astype(F32)).astype(BF16)
        du[at, :] = low

        @pl.when(j > 0)
        def _():
            ex2(j - 1).start()
            ex3(j - 1).start()

        p3s[at, :] = dot(low, wf[...].reshape(width, ff), NT).astype(BF16)
        fcs[0:1, :] = jnp.where(j == 0, 0.0, fcs[0:1, :]) + jnp.sum(
            low.astype(F32), axis=0, keepdims=True
        )

    if direct:
        s_p.add(1)
    l_h2.wait()
    ex2(n_blocks - 1).start()
    ex3(n_blocks - 1).start()
    weight_rows(gf, ht, du[...], s_f.begin_row if direct else None)
    l_h1 = load(h1t_i, ht)
    if direct:
        s_p.add(2)
    for copy in l_m:
        copy.wait()
    sums[...] = jnp.zeros_like(sums)

    @pl.loop(0, n_blocks)
    def _(j):
        at = block(j, step)
        ex2(j).wait_recv()
        ex3(j).wait_recv()
        mid = r1[at, :]
        p2r[at, :] = (
            mid + (p2s[at, :].astype(F32) + p2r[at, :].astype(F32)) + vec[5:6, :]
        ).astype(BF16)
        n, inv = norm(mid)
        dh = p3s[at, :].astype(F32) + p3r[at, :].astype(F32)
        e = dh * vec[3:4, :]
        gj = g[at, :].astype(F32)
        grad = gj + inv * (
            e - jnp.mean(e, axis=-1, keepdims=True) - n * jnp.mean(e * n, axis=-1, keepdims=True)
        )
        r1[at, :] = grad
        sums[2:3, :] += jnp.sum(grad, axis=0, keepdims=True)
        sums[3:4, :] += jnp.sum(dh * n, axis=0, keepdims=True)
        sums[4:5, :] += jnp.sum(dh, axis=0, keepdims=True)
        sums[5:6, :] += jnp.sum(gj, axis=0, keepdims=True)
        gb = grad.astype(BF16)
        gt[:, at] = gb.T
        dob = dot(gb, wo[...].reshape(width, cols)).astype(BF16)
        do[at, :] = dob
        dot_t[:, at] = dob.T

    l_x = load(x_i, g)
    own_out = load(p2r.at[pl.ds(c * half, half)], out.at[c])
    if direct:
        s_p.add(3)
    weight_rows(go, gt, o[...], (lambda s: s_o.one[s].start()) if direct else None)
    for copy in l_b:
        copy.wait()
    l_h1.wait()
    side = lax.broadcasted_iota(jnp.int32, (step, 128), 1) // HD
    side_all = lax.broadcasted_iota(jnp.int32, (rows, 128), 1) // HD
    zero = jnp.zeros((), BF16)
    dst = [a.at[:, pl.ds(0, rows)], du.at[:, pl.ds(0, rows)]]
    events = [{}, {}, {}]
    if direct:
        events[0] = {
            0: lambda: s_p.add(0),
            1: lambda: s_f.cross(1),
            2: lambda: s_f.cross(2),
            3: lambda: s_o.add(1),
            4: lambda: s_o.add(2),
            5: lambda: s_f.cross(3),
            6: lambda: s_o.add(3),
            7: lambda: s_o.add(0),
        }
        events[1] = {
            0: s_p.total,
            1: lambda: s_f.cross(0),
            2: out_y.start,
            3: lambda: s_f.add(1),
            5: lambda: s_f.add(2),
            7: lambda: s_f.add(3),
        }
        events[2] = {
            0: s_o.total,
            1: lambda: s_f.add(0),
            2: lambda: s_p.final(write_to(rp)),
            4: lambda: s_q[0].add(1),
            6: lambda: s_q[0].add(2),
        }
    else:
        events[1] = {2: out_y.start}
    for p in range(n_pairs):
        pair = pl.ds(p * 128, 128)
        l_pt.wait()
        for hh in range(2):
            head = pl.ds((p * 2 + hh) * HD, HD)

            @pl.loop(0, n_blocks)
            def _(j):
                for n, event in events[p].items():
                    if n // n_blocks == hh:

                        @pl.when(j == n % n_blocks)
                        def _():
                            event()

                at = block(j, step)
                inner = jnp.sum(
                    dot_t[head, at].astype(F32) * ot[head, at].astype(F32), axis=0, keepdims=True
                )
                dp = dot(v[:, pair], jnp.where(side == hh, do[at, pair], zero), NT)
                ds = (pt[hh, :, at].astype(F32) * (dp - inner)).astype(BF16)
                dst[hh][:, at] = ds
                dqt[pl.ds(hh * HD, HD), at] = dot(kt[head, :], ds)

        qp, dp_ = q[:, pair], do[:, pair]
        dk = dot(dst[0][...], jnp.where(side_all == 0, qp, zero)) + dot(
            dst[1][...], jnp.where(side_all == 1, qp, zero)
        )
        dv = dot(pt[0], jnp.where(side_all == 0, dp_, zero)) + dot(
            pt[1], jnp.where(side_all == 1, dp_, zero)
        )
        if p + 1 < n_pairs:
            l_pt = load(pt_i.at[pl.ds(2 * p + 2, 2)], pt)
        chunk = jnp.concatenate(
            [(dqt[...].T * SCALE).astype(BF16), dk.astype(BF16), dv.astype(BF16)], axis=1
        )
        for n in range(3):
            dqkv[:, pl.ds(n * cols + p * 128, 128)] = chunk[:, n * 128 : n * 128 + 128]
        weight_rows(
            gq.at[p], ht, chunk, (lambda s, p=p: s_q[p].one[s].start()) if direct else None
        )

    @pl.loop(0, n_blocks)
    def _(j):
        ex2(j).wait_send()

    @pl.loop(0, n_blocks)
    def _(j):
        jj = lax.rem(lead + j, n_blocks)
        at = block(jj, step)
        p2s[at, :] = dot(dqkv[at, :], wq[...].reshape(width, 3 * cols), NT).astype(BF16)

        @pl.when(j > 0)
        def _():
            ex4(lax.rem(lead + j - 1, n_blocks)).start()

    qvs[...] = jnp.zeros_like(qvs)

    @pl.loop(0, n_blocks)
    def _(j):
        at = block(j, step)
        qvs[0:1, :] += jnp.sum(dqkv[at, :].astype(F32), axis=0, keepdims=True)

    ex4(lax.rem(lead + n_blocks - 1, n_blocks)).start()
    l_x.wait()
    if direct:
        s_f.total()

    @pl.loop(0, n_blocks)
    def _(j):
        jj = lax.rem(lead + j, n_blocks)
        at = block(jj, step)
        ex4(jj).wait_recv()
        n, inv = norm(g[at, :].astype(F32))
        dh = p2s[at, :].astype(F32) + p4r[at, :].astype(F32)
        e = dh * vec[0:1, :]
        p4r[at, :] = (
            r1[at, :]
            + inv
            * (e - jnp.mean(e, axis=-1, keepdims=True) - n * jnp.mean(e * n, axis=-1, keepdims=True))
        ).astype(BF16)
        low_sums[pl.ds(jj, 1), :] = jnp.sum(dh * n, axis=0, keepdims=True)
        low_sums[pl.ds(n_blocks + jj, 1), :] = jnp.sum(dh, axis=0, keepdims=True)

        @pl.when(j == 1)
        def _():
            tok_y.start()

    own_tok = load(p4r.at[pl.ds(c * half, half)], gtok.at[c])
    for n in range(2):
        sums[n : n + 1, :] = jnp.sum(
            low_sums[n * n_blocks : (n + 1) * n_blocks, :], axis=0, keepdims=True
        )
    small[...] = jnp.zeros_like(small)
    each = width // small.shape[0]
    row = lax.broadcasted_iota(jnp.int32, (8, cols), 0)
    wide_row = lax.broadcasted_iota(jnp.int32, (8, ff), 0)
    top, low = small.at[:, pl.ds(0, 8)], small.at[:, pl.ds(8, 8)]
    gather_lanes(top, sums[...], 0, each, each, 0)
    for s in range(2):
        part = qvs[0:1, pl.ds(2 * s * cols, cols)]
        gather_lanes(top, jnp.where(row == 6, part, 0.0), s * (each // 2), each // 2, each // 2, 0)
    fc = fcs[0:1, :]
    gather_lanes(top, jnp.where(wide_row == 7, fc, 0.0), 0, each, 2 * each, 0)
    gather_lanes(low, jnp.where(wide_row == 0, fc, 0.0), 0, each, 2 * each, each)
    out_y.wait_recv()
    out_t.start()
    if direct:
        s_s.begin()
        s_q[0].add(3)
        s_q[0].add(0)
        for s in order:
            s_q[1].add(s)
        s_o.final(write_to(ro))
        s_f.final(write_to(rf))
        for s in order:
            s_s.add(s)
        for s in order:
            s_q[2].add(s)
        s_s.total()
        for p in range(n_pairs):
            s_q[p].total()
    tok_y.wait_recv()
    tok_t.start()
    if direct:
        s_s.final(write_to(rsmall))
        for p in range(n_pairs):

            def write(at, value, p=p):
                for n in range(3):
                    rq[at, pl.ds(n * cols + p * 128, 128)] = value[:, n * 128 : n * 128 + 128]

            s_q[p].final(write)
    else:
        dumps = [load(gp, rp), load(gf, rf), load(go, ro), load(gq, rq), load(small, rsmall)]
        for copy in dumps:
            copy.wait()
    out_t.wait_recv()
    tok_t.wait_recv()

    @pl.loop(0, n_blocks)
    def _(j):
        ex3(j).wait_send()
        ex4(j).wait_send()

    net.finish()
    own_out.wait()
    own_tok.wait()


VM = pl.BlockSpec(memory_space=pltpu.VMEM)
SM = pl.BlockSpec(memory_space=pltpu.SMEM)
ANY = pl.BlockSpec(memory_space=pl.ANY)


def call(body, ins, outs, scratch=(), specs=None, out_specs=None, name=None, cid=None):
    params = dict(vmem_limit_bytes=LIMIT)
    if cid is not None:
        params.update(collective_id=cid, has_side_effects=True)
    return pl.pallas_call(
        body,
        out_shape=[jax.ShapeDtypeStruct(s, t) for s, t in outs],
        in_specs=specs or [VM] * len(ins),
        out_specs=out_specs or [VM] * len(outs),
        scratch_shapes=list(scratch),
        name=name,
        compiler_params=pltpu.CompilerParams(**params),
    )(*ins)


def on_device(n_dp, tokens, lengths, ln1_gain, ln1_bias, w_qkv, qv_bias, w_out, out_bias,
              ln2_gain, ln2_bias, w_fc, fc_bias, w_proj, proj_bias, cotangent):
    _, half, width = tokens.shape
    rows = 2 * half
    shard = w_fc.shape[0]
    cols = w_out.shape[1]
    ff = w_fc.shape[1]
    dma = pltpu.SemaphoreType.DMA
    ctx = lax.axis_index("ctx")
    length = lax.dynamic_slice(lengths, (ctx,), (1,))
    lines = [ln1_gain, ln1_bias, out_bias, ln2_gain, ln2_bias, proj_bias,
             qv_bias[:, :, 0].T.reshape(shard)] + list(fc_bias[:, 0].reshape(2, shard))
    small = jnp.pad(jnp.stack(lines), ((0, 16 - len(lines)), (0, 128 - shard)))
    wq_own = w_qkv.reshape(shard, 3 * cols)
    direct = n_dp == 8
    if direct:
        ins = (length, tokens, cotangent, small, wq_own, w_out, w_fc, w_proj)
    else:
        def whole(a):
            return lax.dynamic_index_in_dim(
                lax.all_gather(a, "ctx", axis=1, tiled=True), ctx, 0, False)

        ins = (length, whole(tokens), whole(cotangent)) + tuple(
            lax.all_gather(a, "dp") for a in (small, wq_own, w_out, w_fc, w_proj))
    act = ((rows, width), BF16)
    act_t = ((width, rows), BF16)
    head = ((rows, cols), BF16)
    head_t = ((cols, rows), BF16)
    wide = ((rows, ff), BF16)
    mats = [((n_dp, shard, n), BF16) for n in (3 * cols, cols, ff, ff)]
    outs = [((8, width), F32), act, act_t, act, act_t, head, head, head, head_t, head, head_t,
            ((cols // HD, rows, rows), BF16), ((rows, width), F32), wide, wide, act_t] + mats
    step = 256
    held = [((n_dp, 16, 128), F32)] + mats[:3] + [
        act, act, act, act_t, act, act_t, head, head, head, head_t, head_t, head, head_t,
        ((2, 2, rows, step), BF16), act, act, ((rows, width), F32), wide, wide, act_t,
        ((16, cols), F32), ((8, ff), F32)]
    (vec, g, gt, xs, h1t, q, k, v, kt, o, ot, pt, r1, a, sl, h2t, wq, wo, wf, wp) = call(
        functools.partial(forward_kernel, n_dp, direct), ins, outs,
        [pltpu.VMEM(*h) for h in held]
        + [dma((72,)), dma((72,)), dma((40,)), dma((2, 2)), dma((3, rows // step))],
        [SM] + [ANY] * 7, [VM] + [ANY] * 19, "forward", 1)
    groups = 8
    part = width // groups
    wq, wo, wf, wp = [w.reshape(groups, part, -1) for w in (wq, wo, wf, wp)]
    n_pairs, n_o = cols // 128, n_dp // 2
    narrow = 3 * 128
    held = [(w.shape, BF16) for w in (wq, wo, wf, wp)] + [
        wide, wide, act, act_t, act_t, act, act, act, act, act,
        ((groups, part, ff), BF16), ((groups, part, ff), BF16), ((groups, part, cols), BF16),
        ((n_pairs, groups, part, narrow), BF16), ((n_dp, 16, 128), F32),
        ((rows, width), F32), head, head, head_t, head, head, head, head_t, head_t,
        ((2, rows, rows), BF16), ((128, rows), F32), ((rows, 3 * cols), BF16),
        ((8, width), F32), ((2 * rows // step, width), F32), ((8, ff), F32), ((8, 3 * cols), F32)]
    seq = ((2, half, width), BF16)
    if direct:
        outs = [seq, seq, ((16, 128), F32), ((shard, 3 * cols), F32), ((shard, cols), F32),
                ((shard, ff), F32), ((shard, ff), F32)]
        hr = shard // 2
        for n, lead, r, kind in ((ff, (), shard, BF16), (None, (), 0, BF16),
                                 (cols, (), shard, BF16), (narrow, (n_pairs,), shard, BF16),
                                 (128, (), 16, F32)):
            if n is None:
                held += [((n_dp, hr, ff), kind), ((n_o, hr, ff), kind),
                         ((n_o - 1, hr, ff), kind), ((hr, ff), kind)]
                continue
            held += [(lead + (n_o, r, n), kind), (lead + (n_o - 1, r, n), kind),
                     (lead + (r, n), kind)]
        out_specs = [ANY] * 2 + [VM] * 5
    else:
        outs = [seq, seq, ((n_dp, 16, 128), F32), ((n_pairs, groups, part, narrow), BF16),
                ((groups, part, cols), BF16), ((groups, part, ff), BF16),
                ((groups, part, ff), BF16)]
        out_specs = [ANY] * 7
    out, gtok, rs, rq, ro, rf, rp = call(
        functools.partial(backward_kernel, n_dp, direct),
        (vec, g, gt, xs, h1t, q, k, v, kt, o, ot, pt, r1, a, sl, h2t, wq, wo, wf, wp), outs,
        [pltpu.VMEM(*h) for h in held] + [dma((96,)), dma((96,)), dma((40,))],
        [VM] + [ANY] * 19, out_specs, "backward", 2)
    if not direct:
        def summed(a):
            a = a.reshape(n_dp, shard, -1)
            return lax.psum(lax.psum_scatter(a, "dp", scatter_dimension=0), "ctx").astype(F32)

        rq = rq.reshape(n_pairs, width, 3, 128).transpose(1, 2, 0, 3).reshape(width, 3 * cols)
        rq, ro, rf, rp = [summed(a) for a in (rq, ro, rf, rp)]
        rs = lax.psum(lax.psum_scatter(rs, "dp", scatter_dimension=0), "ctx")
    line = [rs[j, :shard] for j in range(7)]
    return (out, gtok, line[0], line[1], rq.reshape(shard, 3, cols),
            line[6].reshape(2, shard // 2).T[:, :, None], ro, line[2], line[3], line[4],
            rf, rs[7:9, :shard].reshape(2 * shard, 1), rp, line[5])


def solution(mesh):
    dp, seq = P("dp"), P("dp", "ctx", None)
    wide, flat = P("dp", None, "tp"), P("dp", "tp")
    params = (dp, dp, wide, wide, flat, dp, dp, dp, flat, flat, flat, dp)
    return jax.shard_map(
        functools.partial(on_device, mesh.shape["dp"]),
        mesh=mesh,
        in_specs=(seq, dp) + params + (seq,),
        out_specs=(seq, seq) + params,
        check_vma=False,
    )
```

```python
import functools

import jax
import jax.numpy as jnp
from jax import lax
from jax.experimental import pallas as pl
from jax.experimental.pallas import tpu as pltpu
from jax.sharding import PartitionSpec as P

HD = 64
EPS = 1e-05
NEG = -1e30
GELU = 1.702
SCALE = HD ** (-0.5)
F32 = jnp.float32
BF16 = jnp.bfloat16
MESH = pl.DeviceIdType.MESH
LIMIT = 67_000_000
NN = (((1,), (0,)), ((), ()))
NT = (((1,), (1,)), ((), ()))


def dot(a, b, dims=NN):
    return lax.dot_general(a, b, dims, preferred_element_type=F32)


class Net:
    def __init__(self, send, recv):
        self.send, self.recv, self.used, self.all = send, recv, 0, []

    def build(self, k, src, dst, dev):
        return pltpu.make_async_remote_copy(
            src_ref=src, dst_ref=dst, send_sem=self.send.at[k], recv_sem=self.recv.at[k],
            device_id=dev, device_id_type=MESH,
        )

    def take(self, count):
        self.used += count
        return self.used - count

    def make(self, src, dst, dev):
        copy = self.build(self.take(1), src, dst, dev)
        self.all.append(copy)
        return copy

    def put(self, src, dst, dev):
        copy = self.make(src, dst, dev)
        copy.start()
        return copy

    def finish(self):
        for copy in self.all:
            copy.wait_send()


class Place:
    def __init__(self, n_dp, direct=True):
        self.d = lax.axis_index("dp")
        self.c = lax.axis_index("ctx")
        self.t = lax.axis_index("tp")
        self.direct = direct
        self.n_o = n_dp // 2
        self.o, self.i = self.d // 2, self.d % 2

    def outer(self, s):
        return (lax.rem(self.o + s, self.n_o) * 2 + self.i, self.c, self.t)

    def from_outer(self, s):
        return lax.rem(self.o + self.n_o - s, self.n_o) * 2 + self.i

    @property
    def inner(self):
        return (self.o * 2 + 1 - self.i, self.c, self.t)

    @property
    def ctx(self):
        return (self.d, 1 - self.c, self.t)

    @property
    def tp(self):
        return (self.d, self.c, 1 - self.t)

    def barrier(self, ctx=False):
        sem = pltpu.get_barrier_semaphore()
        peers = [self.tp]
        if self.direct or ctx:
            peers.append(self.ctx)
        if self.direct:
            peers += [self.outer(s) for s in range(1, self.n_o)] + [self.inner]
        for peer in peers:
            pl.semaphore_signal(sem, 1, device_id=peer, device_id_type=MESH)
        pl.semaphore_wait(sem, len(peers))


def add_rows(dst, parts, rows, step):
    @pl.loop(0, rows // step)
    def _(j):
        at = pl.ds(pl.multiple_of(j * step, step), step)
        total = parts[0][at, :].astype(F32)
        for part in parts[1:]:
            total = total + part[at, :].astype(F32)
        dst[at, :] = total.astype(dst.dtype)


def norm(x):
    centred = x - jnp.mean(x, axis=-1, keepdims=True)
    inv = lax.rsqrt(jnp.mean(centred * centred, axis=-1, keepdims=True) + EPS)
    return centred * inv, inv


def block(j, size):
    return pl.ds(pl.multiple_of(j * size, size), size)


class Stage:
    def __init__(self, me, net, src, dst, halves):
        self.src, self.dst, self.halves, self.me = src, dst, halves, me
        rows = dst.shape[1]
        part = pl.ds(me.c * (rows // 2), rows // 2)

        def cut(dev):
            return dst.at[dev, part] if halves else dst.at[dev]

        own = src.at[part] if halves else src
        shifts = list(range(1, me.n_o))
        self.outer = [net.make(own, cut(me.d), me.outer(s)) for s in shifts]
        self.inner = [net.make(own, cut(me.d), me.inner)]
        self.ctx = []
        for s in shifts:
            piece = cut(me.from_outer(s))
            self.inner.append(net.make(piece, piece, me.inner))
            if halves:
                self.ctx.append(net.make(piece, piece, me.ctx))
        self.far = []
        if halves:
            for s in [0] + shifts:
                piece = cut(lax.rem(me.o + me.n_o - s, me.n_o) * 2 + 1 - me.i)
                self.far.append(net.make(piece, piece, me.ctx))

    def begin(self):
        for copy in self.outer:
            copy.start()

    def begin_inner(self):
        self.inner[0].start()

    def relay(self, s):
        self.outer[s].wait_recv()
        self.inner[s + 1].start()
        if self.halves:
            self.ctx[s].start()

    def cross(self, s):
        self.inner[s].wait_recv()
        self.far[s].start()

    def arrive(self):
        for copy in self.ctx + self.far if self.halves else self.inner:
            copy.wait_recv()


def placed(small_all, row, first, count, stride, offset, size):
    lane = lax.broadcasted_iota(jnp.int32, (128, size), 0)
    col = lax.broadcasted_iota(jnp.int32, (128, size), 1)
    inside = (lane >= first) & (lane < first + count)

    def add(d, total):
        spot = inside & (col == lane - first + (d * stride + offset))
        return total + lax.dot_general(
            small_all[d, row : row + 8, :], spot.astype(F32), NN,
            precision=lax.Precision.HIGHEST, preferred_element_type=F32,
        )

    return lax.fori_loop(0, small_all.shape[0], add, jnp.zeros((8, size), F32))


def forward_kernel(
    n_dp, direct, length, tok, cot, *refs
):
    n_small = len(refs) - 56
    lines, refs = refs[:n_small], refs[n_small:]
    (wq, wo, wf, wp,
    vec, g_o, gt_o, x_o, h1t_o, q_o, k_o, v_o, kt_o, o_o, ot_o, pt_o, r1_o, a_o, sl_o, h2t_o,
    wq_o, wo_o, wf_o, wp_o,
    small_s, small_v, wq_v, wo_v, wf_v, x, gv, gm, gt, h1, h1t, q, k, v, kt, vt, o, ot, pt, ps, pr, r1, a, sl, h2t,
    bias, fcb, send, recv, local, pts, rows_s) = refs
    me = Place(n_dp, direct)
    net = Net(send, recv)
    d, c, t = me.d, me.c, me.t
    rows, width = x.shape
    cols = q.shape[1]
    half, step = rows // 2, 256
    quarter = half // 2
    shard = width // n_dp
    n_blocks = rows // step
    done = []

    def own(src, dst):
        copy = pltpu.make_async_copy(src, dst, local.at[len(done)])
        copy.start()
        done.append(copy)
        return copy

    if direct:
        ready = [own(wq.at[n], wq_v.at[d, :, pl.ds(n * cols, cols)]) for n in range(3)]
        small_s[...] = jnp.zeros_like(small_s)
        for n in range(6):
            small_s[n : n + 1, 0:shard] = lines[n][...]
        small_s[6:7, 0:shard] = jnp.concatenate([lines[6][0], lines[6][1]], axis=1)
        for n in range(2):
            small_s[7 + n : 8 + n, 0:shard] = lines[7][:, n * shard : (n + 1) * shard]
        small_v[d] = small_s[...]
        me.barrier()
        for copy in ready:
            copy.wait()
    else:
        me.barrier()
    live_length = length[c]
    mine = pl.ds(c * half + t * quarter, quarter)
    theirs = pl.ds((1 - c) * half + t * quarter, quarter)
    first = net.take(n_blocks)

    def exchange(j):
        at = block(j, step)
        return net.build(first + j, ps.at[at], pr.at[at], me.tp)

    if direct:
        tok_y = net.make(tok.at[1 - c, pl.ds(t * quarter, quarter)], x.at[mine], me.ctx)
        tok_t = net.make(x.at[theirs], x.at[theirs], me.tp)
        cot_y = net.make(cot.at[1 - c, pl.ds(t * quarter, quarter)], gv.at[mine], me.ctx)
        cot_t = net.make(gv.at[theirs], gv.at[theirs], me.tp)
        st_s = Stage(me, net, small_s, small_v, False)
        st_q = Stage(me, net, wq_v.at[d], wq_v, True)
        st_o = Stage(me, net, wo, wo_v, True)
        st_f = Stage(me, net, wf, wf_v, True)
        st_p = Stage(me, net, wp, wp_o, False)
        tok_y.start()
        st_s.begin()
        st_s.begin_inner()
        st_q.begin()
        st_q.begin_inner()
        st_o.begin()
        st_o.begin_inner()
        st_f.begin()
        st_p.begin()
        l_x, l_g, l_o, l_f = [
            own(tok.at[c], x.at[pl.ds(c * half, half)]),
            own(cot.at[c], gv.at[pl.ds(c * half, half)]),
            own(wo, wo_v.at[d]),
            own(wf, wf_v.at[d]),
        ]
        first_out = len(done)
        own(wp, wp_o.at[d])
        n_s = me.n_o - 1
        for s in range(n_s):
            st_s.relay(s)
        tok_y.wait_recv()
        tok_t.start()
        for s in (0, 2, 1) if n_s == 3 else range(n_s):
            st_q.relay(s)
        cot_y.start()
        st_s.arrive()
    else:
        ready = [own(lines[0], small_v), own(wq, wq_v)]
        l_x, l_g, l_o, l_f = own(tok, x), own(cot, gv), own(wo, wo_v), own(wf, wf_v)
        first_out = len(done)
        own(wp, wp_o)
        for copy in ready:
            copy.wait()

    vec[...] = placed(small_v, 0, 0, shard, shard, 0, width)
    for s in range(2):
        bias[8 * s : 8 * s + 8, :] = placed(
            small_v, 6, s * (shard // 2), shard // 2, shard // 2, 0, cols
        )
    fcb[...] = placed(small_v, 7, 0, shard, 2 * shard, 0, fcb.shape[1])
    fcb[0:1, :] = fcb[0:1, :] + placed(small_v, 8, 0, shard, 2 * shard, shard, fcb.shape[1])[0:1, :]
    if direct:
        for s in range(me.n_o):
            st_q.cross(s)
        for s in (0, 2, 1) if n_s == 3 else range(n_s):
            st_o.relay(s)
        tok_t.wait_recv()
    l_x.wait()

    @pl.loop(0, n_blocks)
    def _(j):
        at = block(j, step)
        n, _ = norm(x[at, :].astype(F32))
        low = (n * vec[0:1, :] + vec[1:2, :]).astype(BF16)
        h1[at, :] = low
        h1t[:, at] = low.T

    own(x, x_o)
    own(h1t, h1t_o)
    if direct:
        for s in range(me.n_o):
            st_o.cross(s)
        st_f.begin_inner()
        for s in (0, 2, 1) if n_s == 3 else range(n_s):
            st_f.relay(s)
        st_p.begin_inner()
        st_q.arrive()

    @pl.loop(0, n_blocks)
    def _(j):
        at = block(j, step)
        proj = dot(h1[at, :], wq_v[...].reshape(width, 3 * cols))
        q[at, :] = (proj[:, :cols] + bias[0:1, :]).astype(BF16) * SCALE
        kk = proj[:, cols : 2 * cols].astype(BF16)
        vv = (proj[:, 2 * cols :] + bias[8:9, :]).astype(BF16)
        k[at, :] = kk
        v[at, :] = vv
        kt[:, at] = kk.T
        vt[:, at] = vv.T

    own(wq_v, wq_o)
    for src, dst in ((q, q_o), (k, k_o), (v, v_o), (kt, kt_o)):
        own(src, dst)
    if direct:
        for s in range(me.n_o):
            st_f.cross(s)
        cot_y.wait_recv()
        cot_t.start()

    live = lax.broadcasted_iota(jnp.int32, (rows, step), 0) < live_length
    side = lax.broadcasted_iota(jnp.int32, (step, 128), 1) // HD

    def spill(slot, p, at):
        return [
            pltpu.make_async_copy(pt.at[slot, hh], pt_o.at[p * 2 + hh, :, at], pts.at[slot, hh])
            for hh in range(2)
        ]

    steps = (cols // 128) * n_blocks

    @pl.loop(0, steps)
    def _(it):
        p, j = it // n_blocks, it % n_blocks
        pair, at, slot = block(p, 128), block(j, step), it % 2
        if direct:
            for s in range(n_s):

                @pl.when(it == 2 + 3 * s if n_s == 3 else it == 2)
                def _():
                    st_p.relay(s)

        @pl.when(it >= 2)
        def _():
            for copy in spill(slot, p, at):
                copy.wait()

        for hh in range(2):
            qm = jnp.where(side == hh, q[at, pair], jnp.zeros((), BF16))
            s = dot(k[:, pair], qm, NT)
            s = jnp.where(live, s, NEG)
            e = jnp.exp(s - jnp.max(s, axis=0, keepdims=True))
            pb = (e * (1.0 / jnp.sum(e, axis=0, keepdims=True))).astype(BF16)
            pt[slot, hh] = pb
            head = block(p * 2 + hh, HD)
            ot[head, at] = dot(vt[head, :], pb).astype(BF16)
        for copy in spill(slot, p, at):
            copy.start()

    for slot in range(2):
        for copy in spill(slot, 0, pl.ds(0, step)):
            copy.wait()
    own(ot, ot_o)
    if direct:
        st_o.arrive()
    l_o.wait()

    @pl.loop(0, n_blocks)
    def _(j):
        at = block(j, step)
        ob = ot[:, at].T
        o[at, :] = ob
        ps[at, :] = dot(ob, wo_v[...].reshape(width, cols), NT).astype(BF16)

        @pl.when(j > 0)
        def _():
            exchange(j - 1).start()

    own(wo_v, wo_o)
    own(o, o_o)
    exchange(n_blocks - 1).start()
    if direct:
        cot_t.wait_recv()
        st_f.arrive()
    l_g.wait()
    l_f.wait()
    own(wf_v, wf_o)

    @pl.loop(0, n_blocks)
    def _(j):
        at = block(j, step)
        on = j * step + lax.broadcasted_iota(jnp.int32, (step, width), 0) < live_length
        g = jnp.where(on, gv[at, :], jnp.zeros((), BF16))
        gm[at, :] = g
        gt[:, at] = g.T

    own(gm, g_o)
    own(gt, gt_o)

    @pl.loop(0, n_blocks)
    def _(j):
        at = block(j, step)
        exchange(j).wait_recv()
        mid = x[at, :].astype(F32) + (ps[at, :].astype(F32) + pr[at, :].astype(F32)) + vec[2:3, :]
        r1[at, :] = mid
        n, _ = norm(mid)
        h2 = (n * vec[3:4, :] + vec[4:5, :]).astype(BF16)
        h2t[:, at] = h2.T
        u = dot(h2, wf_v[...].reshape(width, fcb.shape[1])) + fcb[0:1, :]
        s = jax.nn.sigmoid(GELU * u)
        a[at, :] = (u * s).astype(BF16)
        sl[at, :] = (s * (1.0 + GELU * u * (1.0 - s))).astype(BF16)
        for n, (src, dst) in enumerate(((r1, r1_o), (a, a_o), (sl, sl_o))):
            pltpu.make_async_copy(src.at[at], dst.at[at], rows_s.at[n, j]).start()

    own(h2t, h2t_o)
    if direct:
        st_p.arrive()
    net.finish()

    @pl.loop(0, n_blocks)
    def _(j):
        at = block(j, step)
        exchange(j).wait_send()
        for n, (src, dst) in enumerate(((r1, r1_o), (a, a_o), (sl, sl_o))):
            pltpu.make_async_copy(src.at[at], dst.at[at], rows_s.at[n, j]).wait()

    for copy in done[first_out:]:
        copy.wait()


def gather_lanes(dst, values, first, count, stride, offset):
    size = values.shape[1]
    lane = lax.broadcasted_iota(jnp.int32, (128, size), 0)
    col = lax.broadcasted_iota(jnp.int32, (128, size), 1)
    inside = (lane >= first) & (lane < first + count)

    @pl.loop(0, dst.shape[0])
    def _(d):
        spot = inside & (col == lane - first + (d * stride + offset))
        dst[d] += lax.dot_general(
            values, spot.astype(F32), NT,
            precision=lax.Precision.HIGHEST, preferred_element_type=F32,
        )


class Sum:
    def __init__(self, me, net, g, x, z, y, step):
        self.me, self.g, self.x, self.z, self.y, self.step = me, g, x, z, y, step
        self.shifts = list(range(1, me.n_o))
        self.order = self.shifts + [0]
        self.one = {
            s: net.make(g.at[self.at(s) * 2 + 1 - me.i], x.at[s], me.inner) for s in self.order
        }
        self.two = {
            s: net.make(g.at[self.at(s) * 2 + me.i], z.at[s - 1], me.outer(s)) for s in self.shifts
        }
        self.three = net.make(g.at[me.d], y, me.ctx)

    def at(self, s):
        return lax.rem(self.me.o + s, self.me.n_o)

    def begin(self):
        for s in self.order:
            self.one[s].start()

    def add(self, s):
        self.one[s].wait_recv()
        part = self.g.at[self.at(s) * 2 + self.me.i]
        add_rows(part, [part, self.x.at[s]], part.shape[0], self.step)
        if s:
            self.two[s].start()

    def total(self):
        for s in self.shifts:
            self.two[s].wait_recv()
        part = self.g.at[self.me.d]
        add_rows(part, [part] + [self.z.at[s - 1] for s in self.shifts], part.shape[0], self.step)
        self.three.start()

    def final(self, write):
        self.three.wait_recv()
        part = self.g.at[self.me.d]

        @pl.loop(0, part.shape[0] // self.step)
        def _(j):
            at = block(j, self.step)
            write(at, part[at, :].astype(F32) + self.y[at, :].astype(F32))


class SumCtx:
    def __init__(self, me, net, g, y, x, z, w, step):
        self.me, self.g, self.y, self.x, self.z, self.w, self.step = me, g, y, x, z, w, step
        self.rows = g.shape[1] // 2
        self.shifts = list(range(1, me.n_o))
        self.order = self.shifts + [0]
        self.mine = pl.ds(me.c * self.rows, self.rows)
        other = pl.ds((1 - me.c) * self.rows, self.rows)
        self.zero, self.zero_own = {}, {}
        for s in self.order:
            dev = self.at(s) * 2 + 1 - me.i
            self.zero[s] = net.make(g.at[dev, other], y.at[dev], me.ctx)
        for s in self.order:
            dev = self.at(s) * 2 + me.i
            self.zero_own[s] = net.make(g.at[dev, other], y.at[dev], me.ctx)
        self.one = {
            s: net.make(g.at[self.at(s) * 2 + 1 - me.i, self.mine], x.at[s], me.inner)
            for s in self.order
        }
        self.two = {
            s: net.make(g.at[self.at(s) * 2 + me.i, self.mine], z.at[s - 1], me.outer(s))
            for s in self.shifts
        }
        self.three = net.make(g.at[me.d, self.mine], w, me.ctx)

    at = Sum.at

    def begin_row(self, s):
        self.zero[s].start()
        self.zero_own[s].start()

    def cross(self, s):
        self.zero[s].wait_recv()
        dev = self.at(s) * 2 + 1 - self.me.i
        part = self.g.at[dev, self.mine]
        add_rows(part, [part, self.y.at[dev]], self.rows, self.step)
        self.one[s].start()

    def add(self, s):
        self.zero_own[s].wait_recv()
        self.one[s].wait_recv()
        dev = self.at(s) * 2 + self.me.i
        part = self.g.at[dev, self.mine]
        add_rows(part, [part, self.y.at[dev], self.x.at[s]], self.rows, self.step)
        if s:
            self.two[s].start()

    def total(self):
        for s in self.shifts:
            self.two[s].wait_recv()
        part = self.g.at[self.me.d, self.mine]
        add_rows(part, [part] + [self.z.at[s - 1] for s in self.shifts], self.rows, self.step)
        self.three.start()

    def final(self, write):
        self.three.wait_recv()
        part = self.g.at[self.me.d, self.mine]

        @pl.loop(0, self.rows // self.step)
        def _(j):
            at = block(j, self.step)
            here = pl.ds(pl.multiple_of(self.me.c * self.rows + j * self.step, self.step), self.step)
            there = pl.ds(
                pl.multiple_of((1 - self.me.c) * self.rows + j * self.step, self.step), self.step
            )
            write(here, part[at, :].astype(F32))
            write(there, self.w[at, :].astype(F32))


def backward_kernel(
    n_dp, direct, vec, g_i, gt_i, x_i, h1t_i, q_i, k_i, v_i, kt_i, o_i, ot_i, pt_i, r1_i, a_i,
    sl_i, h2t_i, wq_i, wo_i, wf_i, wp_i, *refs
):
    n_out = 7
    out, gtok, rsmall, rq_o, ro_o, rf_o, rp_o = refs[:n_out]
    (wq, wo, wf, wp, a, du, g, gt, ht, p2s, p2r, p3s, p3r, p4r, gp, gf, go, gq, small,
     r1, o, do, dot_t, q, k, v, kt, ot, pt, dqt, dqkv, sums, low_sums, fcs, qvs) = refs[n_out : n_out + 35]
    refs = refs[n_out + 35 :]
    send, recv, local = refs[-3:]
    buffers = refs[:-3]
    if direct:
        (rq, ro, rf, rp), buffers = buffers[:4], buffers[4:]
    else:
        rq, ro, rf, rp = rq_o, ro_o, rf_o, rp_o
    me = Place(n_dp, direct)
    net = Net(send, recv)
    d, c, t = me.d, me.c, me.t
    rows, width = g.shape
    cols = q.shape[1]
    ff = a.shape[1]
    half, step = rows // 2, 256
    quarter = half // 2
    n_blocks = rows // step
    groups, shard = gp.shape[0], gp.shape[1]
    n_pairs = cols // 128
    pending = []

    def load(src, dst):
        copy = pltpu.make_async_copy(src, dst, local.at[len(pending)])
        copy.start()
        pending.append(copy)
        return copy

    l_gt, l_a = load(gt_i, gt), load(a_i, a)
    l_w = [load(wp_i, wp), load(wf_i, wf), load(g_i, g), load(sl_i, du)]
    l_h2 = load(h2t_i, ht)
    l_m = [load(r1_i, r1), load(wo_i, wo), load(o_i, o)]
    l_b = [load(q_i, q), load(k_i, k), load(v_i, v), load(kt_i, kt), load(ot_i, ot), load(wq_i, wq)]
    l_pt = load(pt_i.at[pl.ds(0, 2)], pt)
    me.barrier(True)

    def swap(first, src, dst, j):
        at = block(j, step)
        return net.build(first + j, src.at[at], dst.at[at], me.tp)

    f2, f3, f4 = net.take(n_blocks), net.take(n_blocks), net.take(n_blocks)
    ex2 = lambda j: swap(f2, p2s, p2r, j)
    ex3 = lambda j: swap(f3, p3s, p3r, j)
    ex4 = lambda j: swap(f4, p2s, p4r, j)
    lead = (1 - c) * (n_blocks // 2) + t
    mine = pl.ds((1 - c) * half + t * quarter, quarter)
    there = pl.ds(t * quarter, quarter)
    out_y = net.make(p2r.at[mine], out.at[c, there], me.ctx)
    out_t = net.make(out.at[1 - c, there], out.at[1 - c, there], me.tp)
    tok_y = net.make(p4r.at[mine], gtok.at[c, there], me.ctx)
    tok_t = net.make(gtok.at[1 - c, there], gtok.at[1 - c, there], me.tp)

    def write_to(ref):
        def write(at, value):
            ref[at, :] = value
        return write

    if direct:
        b = list(buffers)
        s_p = Sum(me, net, gp, b[0], b[1], b[2], 16)
        s_f = SumCtx(me, net, gf, b[3], b[4], b[5], b[6], 16)
        s_o = Sum(me, net, go, b[7], b[8], b[9], 16)
        s_q = [
            Sum(me, net, gq.at[p], b[10].at[p], b[11].at[p], b[12].at[p], 16)
            for p in range(n_pairs)
        ]
        s_s = Sum(me, net, small, b[13], b[14], b[15], 8)
        order = s_p.order
    two = 2 * shard
    n_z = width // two

    def weight_rows(dst, lhs, rhs, each):
        @pl.loop(0, n_z)
        def _(s):
            zz = lax.rem(me.o + 1 + s, n_z) if direct else s
            value = dot(lhs[pl.ds(pl.multiple_of(zz * two, two), two), :], rhs)
            value = value.astype(BF16).reshape(2, shard, value.shape[1])
            dst[pl.ds(pl.multiple_of(zz * 2, 2), 2)] = value
            if each is not None:
                for n in range(n_z):

                    @pl.when(s == n)
                    def _():
                        each((n + 1) % n_z)

    l_gt.wait()
    l_a.wait()
    weight_rows(gp, gt, a[...], (lambda s: s_p.one[s].start()) if direct else None)
    for copy in l_w:
        copy.wait()

    @pl.loop(0, n_blocks)
    def _(j):
        at = block(j, step)
        wp_all = wp[...].reshape(width, ff)
        p2s[at, :] = dot(a[at, :], wp_all, NT).astype(BF16)
        low = (dot(g[at, :], wp_all) * du[at, :].astype(F32)).astype(BF16)
        du[at, :] = low

        @pl.when(j > 0)
        def _():
            ex2(j - 1).start()
            ex3(j - 1).start()

        p3s[at, :] = dot(low, wf[...].reshape(width, ff), NT).astype(BF16)
        fcs[0:1, :] = jnp.where(j == 0, 0.0, fcs[0:1, :]) + jnp.sum(
            low.astype(F32), axis=0, keepdims=True
        )

    if direct:
        s_p.add(1)
    l_h2.wait()
    ex2(n_blocks - 1).start()
    ex3(n_blocks - 1).start()
    weight_rows(gf, ht, du[...], s_f.begin_row if direct else None)
    l_h1 = load(h1t_i, ht)
    if direct:
        s_p.add(2)
    for copy in l_m:
        copy.wait()
    sums[...] = jnp.zeros_like(sums)

    @pl.loop(0, n_blocks)
    def _(j):
        at = block(j, step)
        ex2(j).wait_recv()
        ex3(j).wait_recv()
        mid = r1[at, :]
        p2r[at, :] = (
            mid + (p2s[at, :].astype(F32) + p2r[at, :].astype(F32)) + vec[5:6, :]
        ).astype(BF16)
        n, inv = norm(mid)
        dh = p3s[at, :].astype(F32) + p3r[at, :].astype(F32)
        e = dh * vec[3:4, :]
        gj = g[at, :].astype(F32)
        grad = gj + inv * (
            e - jnp.mean(e, axis=-1, keepdims=True) - n * jnp.mean(e * n, axis=-1, keepdims=True)
        )
        r1[at, :] = grad
        sums[2:3, :] += jnp.sum(grad, axis=0, keepdims=True)
        sums[3:4, :] += jnp.sum(dh * n, axis=0, keepdims=True)
        sums[4:5, :] += jnp.sum(dh, axis=0, keepdims=True)
        sums[5:6, :] += jnp.sum(gj, axis=0, keepdims=True)
        gb = grad.astype(BF16)
        gt[:, at] = gb.T
        dob = dot(gb, wo[...].reshape(width, cols)).astype(BF16)
        do[at, :] = dob
        dot_t[:, at] = dob.T

    l_x = load(x_i, g)
    own_out = load(p2r.at[pl.ds(c * half, half)], out.at[c])
    if direct:
        s_p.add(3)
    weight_rows(go, gt, o[...], (lambda s: s_o.one[s].start()) if direct else None)
    for copy in l_b:
        copy.wait()
    l_h1.wait()
    copy_p = pltpu.make_async_copy(rp, rp_o, local.at[39]) if direct else None

    def send_p():
        copy_p.start()

    side = lax.broadcasted_iota(jnp.int32, (step, 128), 1) // HD
    side_all = lax.broadcasted_iota(jnp.int32, (rows, 128), 1) // HD
    zero = jnp.zeros((), BF16)
    dst = [a.at[:, pl.ds(0, rows)], du.at[:, pl.ds(0, rows)]]
    events = [{}, {}, {}]
    if direct:
        events[0] = {
            0: lambda: s_p.add(0),
            1: lambda: s_f.cross(1),
            2: lambda: s_f.cross(2),
            3: lambda: s_o.add(1),
            4: lambda: s_o.add(2),
            5: lambda: s_f.cross(3),
            6: lambda: s_o.add(3),
            7: lambda: s_o.add(0),
        }
        events[1] = {
            0: s_p.total,
            1: lambda: s_f.cross(0),
            2: out_y.start,
            3: lambda: s_f.add(1),
            5: lambda: s_f.add(2),
            7: lambda: s_f.add(3),
        }
        events[2] = {
            0: s_o.total,
            1: lambda: s_f.add(0),
            2: lambda: s_p.final(write_to(rp)),
            3: send_p,
            4: lambda: s_q[0].add(1),
            6: lambda: s_q[0].add(2),
        }
    else:
        events[1] = {2: out_y.start}
    for p in range(n_pairs):
        pair = pl.ds(p * 128, 128)
        l_pt.wait()
        for hh in range(2):
            head = pl.ds((p * 2 + hh) * HD, HD)

            @pl.loop(0, n_blocks)
            def _(j):
                for n, event in events[p].items():
                    if n // n_blocks == hh:

                        @pl.when(j == n % n_blocks)
                        def _():
                            event()

                at = block(j, step)
                inner = jnp.sum(
                    dot_t[head, at].astype(F32) * ot[head, at].astype(F32), axis=0, keepdims=True
                )
                dp = dot(v[:, pair], jnp.where(side == hh, do[at, pair], zero), NT)
                ds = (pt[hh, :, at].astype(F32) * (dp - inner)).astype(BF16)
                dst[hh][:, at] = ds
                dqt[pl.ds(hh * HD, HD), at] = dot(kt[head, :], ds)

        qp, dp_ = q[:, pair], do[:, pair]
        dk = dot(dst[0][...], jnp.where(side_all == 0, qp, zero)) + dot(
            dst[1][...], jnp.where(side_all == 1, qp, zero)
        )
        dv = dot(pt[0], jnp.where(side_all == 0, dp_, zero)) + dot(
            pt[1], jnp.where(side_all == 1, dp_, zero)
        )
        if p + 1 < n_pairs:
            l_pt = load(pt_i.at[pl.ds(2 * p + 2, 2)], pt)
        chunk = jnp.concatenate(
            [(dqt[...].T * SCALE).astype(BF16), dk.astype(BF16), dv.astype(BF16)], axis=1
        )
        for n in range(3):
            dqkv[:, pl.ds(n * cols + p * 128, 128)] = chunk[:, n * 128 : n * 128 + 128]
        weight_rows(
            gq.at[p], ht, chunk, (lambda s, p=p: s_q[p].one[s].start()) if direct else None
        )

    @pl.loop(0, n_blocks)
    def _(j):
        ex2(j).wait_send()

    @pl.loop(0, n_blocks)
    def _(j):
        jj = lax.rem(lead + j, n_blocks)
        at = block(jj, step)
        p2s[at, :] = dot(dqkv[at, :], wq[...].reshape(width, 3 * cols), NT).astype(BF16)

        @pl.when(j > 0)
        def _():
            ex4(lax.rem(lead + j - 1, n_blocks)).start()

    qvs[...] = jnp.zeros_like(qvs)

    @pl.loop(0, n_blocks)
    def _(j):
        at = block(j, step)
        qvs[0:1, :] += jnp.sum(dqkv[at, :].astype(F32), axis=0, keepdims=True)

    ex4(lax.rem(lead + n_blocks - 1, n_blocks)).start()
    l_x.wait()
    if direct:
        s_f.total()

    @pl.loop(0, n_blocks)
    def _(j):
        jj = lax.rem(lead + j, n_blocks)
        at = block(jj, step)
        ex4(jj).wait_recv()
        n, inv = norm(g[at, :].astype(F32))
        dh = p2s[at, :].astype(F32) + p4r[at, :].astype(F32)
        e = dh * vec[0:1, :]
        p4r[at, :] = (
            r1[at, :]
            + inv
            * (e - jnp.mean(e, axis=-1, keepdims=True) - n * jnp.mean(e * n, axis=-1, keepdims=True))
        ).astype(BF16)
        low_sums[pl.ds(jj, 1), :] = jnp.sum(dh * n, axis=0, keepdims=True)
        low_sums[pl.ds(n_blocks + jj, 1), :] = jnp.sum(dh, axis=0, keepdims=True)

        @pl.when(j == 1)
        def _():
            tok_y.start()

    own_tok = load(p4r.at[pl.ds(c * half, half)], gtok.at[c])
    for n in range(2):
        sums[n : n + 1, :] = jnp.sum(
            low_sums[n * n_blocks : (n + 1) * n_blocks, :], axis=0, keepdims=True
        )
    small[...] = jnp.zeros_like(small)
    each = width // small.shape[0]
    row = lax.broadcasted_iota(jnp.int32, (8, cols), 0)
    wide_row = lax.broadcasted_iota(jnp.int32, (8, ff), 0)
    top, low = small.at[:, pl.ds(0, 8)], small.at[:, pl.ds(8, 8)]
    gather_lanes(top, sums[...], 0, each, each, 0)
    for s in range(2):
        part = qvs[0:1, pl.ds(2 * s * cols, cols)]
        gather_lanes(top, jnp.where(row == 6, part, 0.0), s * (each // 2), each // 2, each // 2, 0)
    fc = fcs[0:1, :]
    gather_lanes(top, jnp.where(wide_row == 7, fc, 0.0), 0, each, 2 * each, 0)
    gather_lanes(low, jnp.where(wide_row == 0, fc, 0.0), 0, each, 2 * each, each)
    out_y.wait_recv()
    out_t.start()
    if direct:
        s_s.begin()
        s_q[0].add(3)
        s_q[0].add(0)
        for s in order:
            s_q[1].add(s)
        s_o.final(write_to(ro))
        results = [load(ro, ro_o)]
        s_f.final(write_to(rf))
        results.append(load(rf, rf_o))
        for s in order:
            s_s.add(s)
        for s in order:
            s_q[2].add(s)
        s_s.total()
        for p in range(n_pairs):
            s_q[p].total()
    tok_y.wait_recv()
    tok_t.start()
    if direct:
        s_s.final(write_to(rsmall))
        for p in range(n_pairs):

            def write(at, value, p=p):
                for n in range(3):
                    rq[n, at, pl.ds(p * 128, 128)] = value[:, n * 128 : n * 128 + 128]

            s_q[p].final(write)
        results.append(load(rq, rq_o))
    else:
        dumps = [load(gp, rp), load(gf, rf), load(go, ro), load(gq, rq), load(small, rsmall)]
        for copy in dumps:
            copy.wait()
    out_t.wait_recv()
    tok_t.wait_recv()

    @pl.loop(0, n_blocks)
    def _(j):
        ex3(j).wait_send()
        ex4(j).wait_send()

    net.finish()
    own_out.wait()
    own_tok.wait()
    if direct:
        copy_p.wait()
        for copy in results:
            copy.wait()


def finish_kernel(shard, small, *refs):
    big_i, refs = refs[:6], refs[6:]
    big_o, (lines_o, qv_o, fc_o), refs = refs[:6], (refs[6:12], refs[12], refs[13]), refs[14:]
    buffers, sem_i, sem_o = refs[:6], refs[6], refs[7]
    parts = []
    for n, (src, dst, buf) in enumerate(zip(big_i, big_o, buffers)):
        count = src.shape[0] if len(src.shape) == 3 else 1
        for k in range(count):
            at = (lambda r, k=k: r.at[k]) if len(src.shape) == 3 else (lambda r: r)
            load = pltpu.make_async_copy(at(src), at(buf), sem_i.at[len(parts)])
            store = pltpu.make_async_copy(at(buf), at(dst), sem_o.at[len(parts)])
            load.start()
            parts.append((load, store))
    for n in range(6):
        lines_o[n][...] = small[n : n + 1, 0:shard]
    for n in range(2):
        qv_o[n] = small[6:7, n * (shard // 2) : (n + 1) * (shard // 2)]
        fc_o[:, n * shard : (n + 1) * shard] = small[7 + n : 8 + n, 0:shard]
    for load, store in parts:
        load.wait()
        store.start()
    for _, store in parts:
        store.wait()


VM = pl.BlockSpec(memory_space=pltpu.VMEM)
SM = pl.BlockSpec(memory_space=pltpu.SMEM)
ANY = pl.BlockSpec(memory_space=pl.ANY)


def call(body, ins, outs, scratch=(), specs=None, out_specs=None, name=None, cid=None):
    params = dict(vmem_limit_bytes=LIMIT)
    if cid is not None:
        params.update(collective_id=cid, has_side_effects=True)
    return pl.pallas_call(
        body,
        out_shape=[jax.ShapeDtypeStruct(s, t) for s, t in outs],
        in_specs=specs or [VM] * len(ins),
        out_specs=out_specs or [VM] * len(outs),
        scratch_shapes=list(scratch),
        name=name,
        compiler_params=pltpu.CompilerParams(**params),
    )(*ins)


def on_device(n_dp, tokens, lengths, ln1_gain, ln1_bias, w_qkv, qv_bias, w_out, out_bias,
              ln2_gain, ln2_bias, w_fc, fc_bias, w_proj, proj_bias, cotangent):
    _, half, width = tokens.shape
    rows = 2 * half
    shard = w_fc.shape[0]
    cols = w_out.shape[1]
    ff = w_fc.shape[1]
    dma = pltpu.SemaphoreType.DMA
    direct = n_dp == 8
    lines = [ln1_gain, ln1_bias, out_bias, ln2_gain, ln2_bias, proj_bias]
    if direct:
        ins = [lengths, tokens, cotangent] + [a[None] for a in lines] + [
            qv_bias.transpose(1, 2, 0), fc_bias.T, w_qkv.transpose(1, 0, 2), w_out, w_fc, w_proj]
        specs = [SM, ANY, ANY] + [VM] * 8 + [ANY] * 4
    else:
        lines = lines + [qv_bias[:, :, 0].T.reshape(shard)] + list(fc_bias[:, 0].reshape(2, shard))
        small = jnp.pad(jnp.stack(lines), ((0, 16 - len(lines)), (0, 128 - shard)))
        wq_own = w_qkv.reshape(shard, 3 * cols)
        specs = [SM] + [ANY] * 7

        def whole(a):
            return lax.dynamic_index_in_dim(
                lax.all_gather(a, "ctx", axis=1, tiled=True), lax.axis_index("ctx"), 0, False)

        ins = (lengths, whole(tokens), whole(cotangent)) + tuple(
            lax.all_gather(a, "dp") for a in (small, wq_own, w_out, w_fc, w_proj))
    act = ((rows, width), BF16)
    act_t = ((width, rows), BF16)
    head = ((rows, cols), BF16)
    head_t = ((cols, rows), BF16)
    wide = ((rows, ff), BF16)
    mats = [((n_dp, shard, n), BF16) for n in (3 * cols, cols, ff, ff)]
    outs = [((8, width), F32), act, act_t, act, act_t, head, head, head, head_t, head, head_t,
            ((cols // HD, rows, rows), BF16), ((rows, width), F32), wide, wide, act_t] + mats
    step = 256
    held = [((16, 128), F32), ((n_dp, 16, 128), F32)] + mats[:3] + [
        act, act, act, act_t, act, act_t, head, head, head, head_t, head_t, head, head_t,
        ((2, 2, rows, step), BF16), act, act, ((rows, width), F32), wide, wide, act_t,
        ((16, cols), F32), ((8, ff), F32)]
    (vec, g, gt, xs, h1t, q, k, v, kt, o, ot, pt, r1, a, sl, h2t, wq, wo, wf, wp) = call(
        functools.partial(forward_kernel, n_dp, direct), ins, outs,
        [pltpu.VMEM(*h) for h in held]
        + [dma((72,)), dma((72,)), dma((40,)), dma((2, 2)), dma((3, rows // step))],
        specs, [VM] + [ANY] * 19, "forward", 1)
    groups = 8
    part = width // groups
    wq, wo, wf, wp = [w.reshape(groups, part, -1) for w in (wq, wo, wf, wp)]
    n_pairs, n_o = cols // 128, n_dp // 2
    narrow = 3 * 128
    held = [(w.shape, BF16) for w in (wq, wo, wf, wp)] + [
        wide, wide, act, act_t, act_t, act, act, act, act, act,
        ((groups, part, ff), BF16), ((groups, part, ff), BF16), ((groups, part, cols), BF16),
        ((n_pairs, groups, part, narrow), BF16), ((n_dp, 16, 128), F32),
        ((rows, width), F32), head, head, head_t, head, head, head, head_t, head_t,
        ((2, rows, rows), BF16), ((128, rows), F32), ((rows, 3 * cols), BF16),
        ((8, width), F32), ((2 * rows // step, width), F32), ((8, ff), F32), ((8, 3 * cols), F32)]
    seq = ((2, half, width), BF16)
    if direct:
        big = [((3, shard, cols), F32), ((shard, cols), F32), ((shard, ff), F32), ((shard, ff), F32)]
        outs = [seq, seq, ((16, 128), F32)] + big
        held += big
        hr = shard // 2
        for n, lead, r, kind in ((ff, (), shard, BF16), (None, (), 0, BF16),
                                 (cols, (), shard, BF16), (narrow, (n_pairs,), shard, BF16),
                                 (128, (), 16, F32)):
            if n is None:
                held += [((n_dp, hr, ff), kind), ((n_o, hr, ff), kind),
                         ((n_o - 1, hr, ff), kind), ((hr, ff), kind)]
                continue
            held += [(lead + (n_o, r, n), kind), (lead + (n_o - 1, r, n), kind),
                     (lead + (r, n), kind)]
        out_specs = [ANY] * 2 + [VM] + [ANY] * 4
    else:
        outs = [seq, seq, ((n_dp, 16, 128), F32), ((n_pairs, groups, part, narrow), BF16),
                ((groups, part, cols), BF16), ((groups, part, ff), BF16),
                ((groups, part, ff), BF16)]
        out_specs = [ANY] * 7
    out, gtok, rs, rq, ro, rf, rp = call(
        functools.partial(backward_kernel, n_dp, direct),
        (vec, g, gt, xs, h1t, q, k, v, kt, o, ot, pt, r1, a, sl, h2t, wq, wo, wf, wp), outs,
        [pltpu.VMEM(*h) for h in held] + [dma((96,)), dma((96,)), dma((40,))],
        [VM] + [ANY] * 19, out_specs, "backward", 2)
    if not direct:
        def summed(a):
            a = a.reshape(n_dp, shard, -1)
            return lax.psum(lax.psum_scatter(a, "dp", scatter_dimension=0), "ctx").astype(F32)

        rq = rq.reshape(n_pairs, width, 3, 128).transpose(1, 2, 0, 3).reshape(width, 3 * cols)
        rq, ro, rf, rp = [summed(a) for a in (rq, ro, rf, rp)]
        rs = lax.psum(lax.psum_scatter(rs, "dp", scatter_dimension=0), "ctx")
    if direct:
        mats = [seq, seq] + big
        small = [((1, shard), F32)] * 6 + [((2, 1, shard // 2), F32), ((1, 2 * shard), F32)]
        (out, gtok, rq, ro, rf, rp, g1, b1, bo, g2, b2, bp, qv, fc) = call(
            functools.partial(finish_kernel, shard), (rs, out, gtok, rq, ro, rf, rp), mats + small,
            [pltpu.VMEM(*m) for m in mats] + [dma((12,)), dma((12,))],
            [VM] + [ANY] * 6, [ANY] * 6 + [VM] * 8, "finish")
        return (out, gtok, g1[0], b1[0], rq.transpose(1, 0, 2), qv.transpose(2, 0, 1), ro, bo[0],
                g2[0], b2[0], rf, fc.T, rp, bp[0])
    line = [rs[j, :shard] for j in range(7)]
    return (out, gtok, line[0], line[1], rq.reshape(shard, 3, cols),
            line[6].reshape(2, shard // 2).T[:, :, None], ro, line[2], line[3], line[4],
            rf, rs[7:9, :shard].reshape(2 * shard, 1), rp, line[5])


def solution(mesh):
    dp, seq = P("dp"), P("dp", "ctx", None)
    wide, flat = P("dp", None, "tp"), P("dp", "tp")
    params = (dp, dp, wide, wide, flat, dp, dp, dp, flat, flat, flat, dp)
    return jax.shard_map(
        functools.partial(on_device, mesh.shape["dp"]),
        mesh=mesh,
        in_specs=(seq, dp) + params + (seq,),
        out_specs=(seq, seq) + params,
        check_vma=False,
    )
```

```python
import functools

import jax
import jax.numpy as jnp
from jax import lax
from jax.experimental import pallas as pl
from jax.experimental.pallas import tpu as pltpu
from jax.sharding import PartitionSpec as P

HD = 64
EPS = 1e-05
NEG = -1e30
GELU = 1.702
SCALE = HD ** (-0.5)
F32 = jnp.float32
BF16 = jnp.bfloat16
MESH = pl.DeviceIdType.MESH
LIMIT = 67_000_000
NN = (((1,), (0,)), ((), ()))
NT = (((1,), (1,)), ((), ()))


def dot(a, b, dims=NN):
    return lax.dot_general(a, b, dims, preferred_element_type=F32)


class Net:
    def __init__(self, send, recv):
        self.send, self.recv, self.used, self.all = send, recv, 0, []

    def build(self, k, src, dst, dev):
        return pltpu.make_async_remote_copy(
            src_ref=src, dst_ref=dst, send_sem=self.send.at[k], recv_sem=self.recv.at[k],
            device_id=dev, device_id_type=MESH,
        )

    def take(self, count):
        self.used += count
        return self.used - count

    def make(self, src, dst, dev):
        copy = self.build(self.take(1), src, dst, dev)
        self.all.append(copy)
        return copy

    def put(self, src, dst, dev):
        copy = self.make(src, dst, dev)
        copy.start()
        return copy

    def finish(self):
        for copy in self.all:
            copy.wait_send()


class Place:
    def __init__(self, n_dp, direct=True):
        self.d = lax.axis_index("dp")
        self.c = lax.axis_index("ctx")
        self.t = lax.axis_index("tp")
        self.direct = direct
        self.n_o = n_dp // 2
        self.o, self.i = self.d // 2, self.d % 2

    def outer(self, s):
        return (lax.rem(self.o + s, self.n_o) * 2 + self.i, self.c, self.t)

    def from_outer(self, s):
        return lax.rem(self.o + self.n_o - s, self.n_o) * 2 + self.i

    @property
    def inner(self):
        return (self.o * 2 + 1 - self.i, self.c, self.t)

    @property
    def ctx(self):
        return (self.d, 1 - self.c, self.t)

    @property
    def tp(self):
        return (self.d, self.c, 1 - self.t)

    def barrier(self, ctx=False):
        sem = pltpu.get_barrier_semaphore()
        peers = [self.tp]
        if self.direct or ctx:
            peers.append(self.ctx)
        if self.direct:
            peers += [self.outer(s) for s in range(1, self.n_o)] + [self.inner]
        for peer in peers:
            pl.semaphore_signal(sem, 1, device_id=peer, device_id_type=MESH)
        pl.semaphore_wait(sem, len(peers))


def add_rows(dst, parts, rows, step):
    @pl.loop(0, rows // step)
    def _(j):
        at = pl.ds(pl.multiple_of(j * step, step), step)
        total = parts[0][at, :].astype(F32)
        for part in parts[1:]:
            total = total + part[at, :].astype(F32)
        dst[at, :] = total.astype(dst.dtype)


def norm(x):
    centred = x - jnp.mean(x, axis=-1, keepdims=True)
    inv = lax.rsqrt(jnp.mean(centred * centred, axis=-1, keepdims=True) + EPS)
    return centred * inv, inv


def block(j, size):
    return pl.ds(pl.multiple_of(j * size, size), size)


class Stage:
    def __init__(self, me, net, src, dst, halves):
        self.src, self.dst, self.halves, self.me = src, dst, halves, me
        rows = dst.shape[1]
        part = pl.ds(me.c * (rows // 2), rows // 2)

        def cut(dev):
            return dst.at[dev, part] if halves else dst.at[dev]

        own = src.at[part] if halves else src
        shifts = list(range(1, me.n_o))
        self.outer = [net.make(own, cut(me.d), me.outer(s)) for s in shifts]
        self.inner = [net.make(own, cut(me.d), me.inner)]
        self.ctx = []
        for s in shifts:
            piece = cut(me.from_outer(s))
            self.inner.append(net.make(piece, piece, me.inner))
            if halves:
                self.ctx.append(net.make(piece, piece, me.ctx))
        self.far = []
        if halves:
            for s in [0] + shifts:
                piece = cut(lax.rem(me.o + me.n_o - s, me.n_o) * 2 + 1 - me.i)
                self.far.append(net.make(piece, piece, me.ctx))

    def begin(self):
        for copy in self.outer:
            copy.start()

    def begin_inner(self):
        self.inner[0].start()

    def relay(self, s):
        self.outer[s].wait_recv()
        self.inner[s + 1].start()
        if self.halves:
            self.ctx[s].start()

    def cross(self, s):
        self.inner[s].wait_recv()
        self.far[s].start()

    def arrive(self):
        for copy in self.ctx + self.far if self.halves else self.inner:
            copy.wait_recv()


def placed(small_all, row, first, count, stride, offset, size):
    lane = lax.broadcasted_iota(jnp.int32, (128, size), 0)
    col = lax.broadcasted_iota(jnp.int32, (128, size), 1)
    inside = (lane >= first) & (lane < first + count)

    def add(d, total):
        spot = inside & (col == lane - first + (d * stride + offset))
        return total + lax.dot_general(
            small_all[d, row : row + 8, :], spot.astype(F32), NN,
            precision=lax.Precision.HIGHEST, preferred_element_type=F32,
        )

    return lax.fori_loop(0, small_all.shape[0], add, jnp.zeros((8, size), F32))


def forward_kernel(
    n_dp, direct, length, tok, cot, *refs
):
    n_small = len(refs) - 56
    lines, refs = refs[:n_small], refs[n_small:]
    (wq, wo, wf, wp,
    vec, g_o, gt_o, x_o, h1t_o, q_o, k_o, v_o, kt_o, o_o, ot_o, pt_o, r1_o, a_o, sl_o, h2t_o,
    wq_o, wo_o, wf_o, wp_o,
    small_s, small_v, wq_v, wo_v, wf_v, x, gv, gm, gt, h1, h1t, q, k, v, kt, vt, o, ot, pt, ps, pr, r1, a, sl, h2t,
    bias, fcb, send, recv, local, pts, rows_s) = refs
    me = Place(n_dp, direct)
    net = Net(send, recv)
    d, c, t = me.d, me.c, me.t
    rows, width = x.shape
    cols = q.shape[1]
    half, step = rows // 2, 256
    quarter = half // 2
    shard = width // n_dp
    n_blocks = rows // step
    done = []

    def own(src, dst):
        copy = pltpu.make_async_copy(src, dst, local.at[len(done)])
        copy.start()
        done.append(copy)
        return copy

    if direct:
        ready = [own(wq.at[n], wq_v.at[d, :, pl.ds(n * cols, cols)]) for n in range(3)]
        small_s[...] = jnp.zeros_like(small_s)
        for n in range(6):
            small_s[n : n + 1, 0:shard] = lines[n][...]
        small_s[6:7, 0:shard] = jnp.concatenate([lines[6][0], lines[6][1]], axis=1)
        for n in range(2):
            small_s[7 + n : 8 + n, 0:shard] = lines[7][:, n * shard : (n + 1) * shard]
        small_v[d] = small_s[...]
        me.barrier()
        for copy in ready:
            copy.wait()
    else:
        me.barrier()
    live_length = length[c]
    mine = pl.ds(c * half + t * quarter, quarter)
    theirs = pl.ds((1 - c) * half + t * quarter, quarter)
    first = net.take(n_blocks)

    def exchange(j):
        at = block(j, step)
        return net.build(first + j, ps.at[at], pr.at[at], me.tp)

    if direct:
        tok_y = net.make(tok.at[1 - c, pl.ds(t * quarter, quarter)], x.at[mine], me.ctx)
        tok_t = net.make(x.at[theirs], x.at[theirs], me.tp)
        cot_y = net.make(cot.at[1 - c, pl.ds(t * quarter, quarter)], gv.at[mine], me.ctx)
        cot_t = net.make(gv.at[theirs], gv.at[theirs], me.tp)
        st_s = Stage(me, net, small_s, small_v, False)
        st_q = Stage(me, net, wq_v.at[d], wq_v, True)
        st_o = Stage(me, net, wo, wo_v, True)
        st_f = Stage(me, net, wf, wf_v, True)
        st_p = Stage(me, net, wp, wp_o, False)
        tok_y.start()
        st_s.begin()
        st_s.begin_inner()
        st_q.begin()
        st_q.begin_inner()
        st_o.begin()
        st_o.begin_inner()
        st_f.begin()
        st_p.begin()
        l_x, l_g, l_o, l_f = [
            own(tok.at[c], x.at[pl.ds(c * half, half)]),
            own(cot.at[c], gv.at[pl.ds(c * half, half)]),
            own(wo, wo_v.at[d]),
            own(wf, wf_v.at[d]),
        ]
        first_out = len(done)
        own(wp, wp_o.at[d])
        n_s = me.n_o - 1
        for s in range(n_s):
            st_s.relay(s)
        tok_y.wait_recv()
        tok_t.start()
        for s in (0, 2, 1) if n_s == 3 else range(n_s):
            st_q.relay(s)
        cot_y.start()
        st_s.arrive()
    else:
        ready = [own(lines[0], small_v), own(wq, wq_v)]
        l_x, l_g, l_o, l_f = own(tok, x), own(cot, gv), own(wo, wo_v), own(wf, wf_v)
        first_out = len(done)
        own(wp, wp_o)
        for copy in ready:
            copy.wait()

    vec[...] = placed(small_v, 0, 0, shard, shard, 0, width)
    for s in range(2):
        bias[8 * s : 8 * s + 8, :] = placed(
            small_v, 6, s * (shard // 2), shard // 2, shard // 2, 0, cols
        )
    fcb[...] = placed(small_v, 7, 0, shard, 2 * shard, 0, fcb.shape[1])
    fcb[0:1, :] = fcb[0:1, :] + placed(small_v, 8, 0, shard, 2 * shard, shard, fcb.shape[1])[0:1, :]
    if direct:
        for s in range(me.n_o):
            st_q.cross(s)
        for s in (0, 2, 1) if n_s == 3 else range(n_s):
            st_o.relay(s)
        tok_t.wait_recv()
    l_x.wait()

    @pl.loop(0, n_blocks)
    def _(j):
        at = block(j, step)
        n, _ = norm(x[at, :].astype(F32))
        low = (n * vec[0:1, :] + vec[1:2, :]).astype(BF16)
        h1[at, :] = low
        h1t[:, at] = low.T

    own(x, x_o)
    own(h1t, h1t_o)
    if direct:
        for s in range(me.n_o):
            st_o.cross(s)
        st_f.begin_inner()
        for s in (0, 2, 1) if n_s == 3 else range(n_s):
            st_f.relay(s)
        st_p.begin_inner()
        st_q.arrive()

    @pl.loop(0, n_blocks)
    def _(j):
        at = block(j, step)
        proj = dot(h1[at, :], wq_v[...].reshape(width, 3 * cols))
        q[at, :] = (proj[:, :cols] + bias[0:1, :]).astype(BF16) * SCALE
        kk = proj[:, cols : 2 * cols].astype(BF16)
        vv = (proj[:, 2 * cols :] + bias[8:9, :]).astype(BF16)
        k[at, :] = kk
        v[at, :] = vv
        kt[:, at] = kk.T
        vt[:, at] = vv.T

    own(wq_v, wq_o)
    for src, dst in ((q, q_o), (k, k_o), (v, v_o), (kt, kt_o)):
        own(src, dst)
    if direct:
        for s in range(me.n_o):
            st_f.cross(s)
        cot_y.wait_recv()
        cot_t.start()

    live = lax.broadcasted_iota(jnp.int32, (rows, step), 0) < live_length
    side = lax.broadcasted_iota(jnp.int32, (step, 128), 1) // HD

    def spill(slot, p, at):
        return [
            pltpu.make_async_copy(pt.at[slot, hh], pt_o.at[p * 2 + hh, :, at], pts.at[slot, hh])
            for hh in range(2)
        ]

    steps = (cols // 128) * n_blocks

    @pl.loop(0, steps)
    def _(it):
        p, j = it // n_blocks, it % n_blocks
        pair, at, slot = block(p, 128), block(j, step), it % 2
        if direct:
            for s in range(n_s):

                @pl.when(it == 2 + 3 * s if n_s == 3 else it == 2)
                def _():
                    st_p.relay(s)

        @pl.when(it >= 2)
        def _():
            for copy in spill(slot, p, at):
                copy.wait()

        for hh in range(2):
            qm = jnp.where(side == hh, q[at, pair], jnp.zeros((), BF16))
            s = dot(k[:, pair], qm, NT)
            s = jnp.where(live, s, NEG)
            e = jnp.exp(s - jnp.max(s, axis=0, keepdims=True))
            pb = (e * (1.0 / jnp.sum(e, axis=0, keepdims=True))).astype(BF16)
            pt[slot, hh] = pb
            head = block(p * 2 + hh, HD)
            ot[head, at] = dot(vt[head, :], pb).astype(BF16)
        for copy in spill(slot, p, at):
            copy.start()

    for slot in range(2):
        for copy in spill(slot, 0, pl.ds(0, step)):
            copy.wait()
    own(ot, ot_o)
    if direct:
        st_o.arrive()
    l_o.wait()

    @pl.loop(0, n_blocks)
    def _(j):
        at = block(j, step)
        ob = ot[:, at].T
        o[at, :] = ob
        ps[at, :] = dot(ob, wo_v[...].reshape(width, cols), NT).astype(BF16)

        @pl.when(j > 0)
        def _():
            exchange(j - 1).start()

    own(wo_v, wo_o)
    own(o, o_o)
    exchange(n_blocks - 1).start()
    if direct:
        cot_t.wait_recv()
        st_f.arrive()
    l_g.wait()
    l_f.wait()
    own(wf_v, wf_o)

    @pl.loop(0, n_blocks)
    def _(j):
        at = block(j, step)
        on = j * step + lax.broadcasted_iota(jnp.int32, (step, width), 0) < live_length
        g = jnp.where(on, gv[at, :], jnp.zeros((), BF16))
        gm[at, :] = g
        gt[:, at] = g.T

    own(gm, g_o)
    own(gt, gt_o)

    @pl.loop(0, n_blocks)
    def _(j):
        at = block(j, step)
        exchange(j).wait_recv()
        mid = x[at, :].astype(F32) + (ps[at, :].astype(F32) + pr[at, :].astype(F32)) + vec[2:3, :]
        r1[at, :] = mid
        n, _ = norm(mid)
        h2 = (n * vec[3:4, :] + vec[4:5, :]).astype(BF16)
        h2t[:, at] = h2.T
        u = dot(h2, wf_v[...].reshape(width, fcb.shape[1])) + fcb[0:1, :]
        s = jax.nn.sigmoid(GELU * u)
        a[at, :] = (u * s).astype(BF16)
        sl[at, :] = (s * (1.0 + GELU * u * (1.0 - s))).astype(BF16)
        for n, (src, dst) in enumerate(((r1, r1_o), (a, a_o), (sl, sl_o))):
            pltpu.make_async_copy(src.at[at], dst.at[at], rows_s.at[n, j]).start()

    own(h2t, h2t_o)
    if direct:
        st_p.arrive()
    net.finish()

    @pl.loop(0, n_blocks)
    def _(j):
        at = block(j, step)
        exchange(j).wait_send()
        for n, (src, dst) in enumerate(((r1, r1_o), (a, a_o), (sl, sl_o))):
            pltpu.make_async_copy(src.at[at], dst.at[at], rows_s.at[n, j]).wait()

    for copy in done[first_out:]:
        copy.wait()


def gather_lanes(dst, values, first, count, stride, offset):
    size = values.shape[1]
    lane = lax.broadcasted_iota(jnp.int32, (128, size), 0)
    col = lax.broadcasted_iota(jnp.int32, (128, size), 1)
    inside = (lane >= first) & (lane < first + count)

    @pl.loop(0, dst.shape[0])
    def _(d):
        spot = inside & (col == lane - first + (d * stride + offset))
        dst[d] += lax.dot_general(
            values, spot.astype(F32), NT,
            precision=lax.Precision.HIGHEST, preferred_element_type=F32,
        )


class Sum:
    def __init__(self, me, net, g, x, z, y, step):
        self.me, self.g, self.x, self.z, self.y, self.step = me, g, x, z, y, step
        self.shifts = list(range(1, me.n_o))
        self.order = self.shifts + [0]
        self.one = {
            s: net.make(g.at[self.at(s) * 2 + 1 - me.i], x.at[s], me.inner) for s in self.order
        }
        self.two = {
            s: net.make(g.at[self.at(s) * 2 + me.i], z.at[s - 1], me.outer(s)) for s in self.shifts
        }
        self.three = net.make(g.at[me.d], y, me.ctx)

    def at(self, s):
        return lax.rem(self.me.o + s, self.me.n_o)

    def begin(self):
        for s in self.order:
            self.one[s].start()

    def add(self, s):
        self.one[s].wait_recv()
        part = self.g.at[self.at(s) * 2 + self.me.i]
        add_rows(part, [part, self.x.at[s]], part.shape[0], self.step)
        if s:
            self.two[s].start()

    def total(self):
        for s in self.shifts:
            self.two[s].wait_recv()
        part = self.g.at[self.me.d]
        add_rows(part, [part] + [self.z.at[s - 1] for s in self.shifts], part.shape[0], self.step)
        self.three.start()

    def final(self, write):
        self.three.wait_recv()
        part = self.g.at[self.me.d]

        @pl.loop(0, part.shape[0] // self.step)
        def _(j):
            at = block(j, self.step)
            write(at, part[at, :].astype(F32) + self.y[at, :].astype(F32))


class SumCtx:
    def __init__(self, me, net, g, y, x, z, w, step):
        self.me, self.g, self.y, self.x, self.z, self.w, self.step = me, g, y, x, z, w, step
        self.rows = g.shape[1] // 2
        self.shifts = list(range(1, me.n_o))
        self.order = self.shifts + [0]
        self.mine = pl.ds(me.c * self.rows, self.rows)
        other = pl.ds((1 - me.c) * self.rows, self.rows)
        self.zero, self.zero_own = {}, {}
        for s in self.order:
            dev = self.at(s) * 2 + 1 - me.i
            self.zero[s] = net.make(g.at[dev, other], y.at[dev], me.ctx)
        for s in self.order:
            dev = self.at(s) * 2 + me.i
            self.zero_own[s] = net.make(g.at[dev, other], y.at[dev], me.ctx)
        self.one = {
            s: net.make(g.at[self.at(s) * 2 + 1 - me.i, self.mine], x.at[s], me.inner)
            for s in self.order
        }
        self.two = {
            s: net.make(g.at[self.at(s) * 2 + me.i, self.mine], z.at[s - 1], me.outer(s))
            for s in self.shifts
        }
        self.three = net.make(g.at[me.d, self.mine], w, me.ctx)

    at = Sum.at

    def begin_row(self, s):
        self.zero[s].start()
        self.zero_own[s].start()

    def cross(self, s):
        self.zero[s].wait_recv()
        dev = self.at(s) * 2 + 1 - self.me.i
        part = self.g.at[dev, self.mine]
        add_rows(part, [part, self.y.at[dev]], self.rows, self.step)
        self.one[s].start()

    def add(self, s):
        self.zero_own[s].wait_recv()
        self.one[s].wait_recv()
        dev = self.at(s) * 2 + self.me.i
        part = self.g.at[dev, self.mine]
        add_rows(part, [part, self.y.at[dev], self.x.at[s]], self.rows, self.step)
        if s:
            self.two[s].start()

    def total(self):
        for s in self.shifts:
            self.two[s].wait_recv()
        part = self.g.at[self.me.d, self.mine]
        add_rows(part, [part] + [self.z.at[s - 1] for s in self.shifts], self.rows, self.step)
        self.three.start()

    def final(self, write):
        self.three.wait_recv()
        part = self.g.at[self.me.d, self.mine]

        @pl.loop(0, self.rows // self.step)
        def _(j):
            at = block(j, self.step)
            here = pl.ds(pl.multiple_of(self.me.c * self.rows + j * self.step, self.step), self.step)
            there = pl.ds(
                pl.multiple_of((1 - self.me.c) * self.rows + j * self.step, self.step), self.step
            )
            write(here, part[at, :].astype(F32))
            write(there, self.w[at, :].astype(F32))


def backward_kernel(
    n_dp, direct, vec, g_i, gt_i, x_i, h1t_i, q_i, k_i, v_i, kt_i, o_i, ot_i, pt_i, r1_i, a_i,
    sl_i, h2t_i, wq_i, wo_i, wf_i, wp_i, *refs
):
    n_out = 7
    out, gtok, rsmall, rq_o, ro_o, rf_o, rp_o = refs[:n_out]
    (wq, wo, wf, wp, a, du, g, gt, ht, p2s, p2r, p3s, p3r, p4r, gp, gf, go, gq, small,
     r1, o, do, dot_t, q, k, v, kt, ot, pt, dqt, dqkv, sums, low_sums, fcs, qvs) = refs[n_out : n_out + 35]
    refs = refs[n_out + 35 :]
    send, recv, local = refs[-3:]
    buffers = refs[:-3]
    if direct:
        (rq, ro, rf, rp), buffers = buffers[:4], buffers[4:]
    else:
        rq, ro, rf, rp = rq_o, ro_o, rf_o, rp_o
    me = Place(n_dp, direct)
    net = Net(send, recv)
    d, c, t = me.d, me.c, me.t
    rows, width = g.shape
    cols = q.shape[1]
    ff = a.shape[1]
    half, step = rows // 2, 256
    quarter = half // 2
    n_blocks = rows // step
    groups, shard = gp.shape[0], gp.shape[1]
    n_pairs = cols // 128
    pending = []

    def load(src, dst):
        copy = pltpu.make_async_copy(src, dst, local.at[len(pending)])
        copy.start()
        pending.append(copy)
        return copy

    l_gt, l_a = load(gt_i, gt), load(a_i, a)
    l_w = [load(wp_i, wp), load(wf_i, wf), load(g_i, g), load(sl_i, du)]
    l_h2 = load(h2t_i, ht)
    l_m = [load(r1_i, r1), load(wo_i, wo), load(o_i, o)]
    l_b = [load(q_i, q), load(k_i, k), load(v_i, v), load(kt_i, kt), load(ot_i, ot), load(wq_i, wq)]
    l_pt = load(pt_i.at[pl.ds(0, 2)], pt)
    me.barrier(True)

    def swap(first, src, dst, j):
        at = block(j, step)
        return net.build(first + j, src.at[at], dst.at[at], me.tp)

    f2, f3, f4 = net.take(n_blocks), net.take(n_blocks), net.take(n_blocks)
    ex2 = lambda j: swap(f2, p2s, p2r, j)
    ex3 = lambda j: swap(f3, p3s, p3r, j)
    ex4 = lambda j: swap(f4, p2s, p4r, j)
    lead = (1 - c) * (n_blocks // 2) + t
    mine = pl.ds((1 - c) * half + t * quarter, quarter)
    there = pl.ds(t * quarter, quarter)
    out_y = net.make(p2r.at[mine], out.at[c, there], me.ctx)
    out_t = net.make(out.at[1 - c, there], out.at[1 - c, there], me.tp)
    tok_y = net.make(p4r.at[mine], gtok.at[c, there], me.ctx)
    tok_t = net.make(gtok.at[1 - c, there], gtok.at[1 - c, there], me.tp)

    def write_to(ref):
        def write(at, value):
            ref[at, :] = value
        return write

    if direct:
        b = list(buffers)
        s_p = Sum(me, net, gp, b[0], b[1], b[2], 16)
        s_f = SumCtx(me, net, gf, b[3], b[4], b[5], b[6], 16)
        s_o = Sum(me, net, go, b[7], b[8], b[9], 16)
        s_q = [
            Sum(me, net, gq.at[p], b[10].at[p], b[11].at[p], b[12].at[p], 16)
            for p in range(n_pairs)
        ]
        s_s = Sum(me, net, small, b[13], b[14], b[15], 8)
        order = s_p.order
    two = 2 * shard
    n_z = width // two

    def weight_rows(dst, lhs, rhs, each):
        @pl.loop(0, n_z)
        def _(s):
            zz = lax.rem(me.o + 1 + s, n_z) if direct else s
            value = dot(lhs[pl.ds(pl.multiple_of(zz * two, two), two), :], rhs)
            value = value.astype(BF16).reshape(2, shard, value.shape[1])
            dst[pl.ds(pl.multiple_of(zz * 2, 2), 2)] = value
            if each is not None:
                for n in range(n_z):

                    @pl.when(s == n)
                    def _():
                        each((n + 1) % n_z)

    l_gt.wait()
    l_a.wait()
    weight_rows(gp, gt, a[...], (lambda s: s_p.one[s].start()) if direct else None)
    for copy in l_w:
        copy.wait()

    @pl.loop(0, n_blocks)
    def _(j):
        at = block(j, step)
        wp_all = wp[...].reshape(width, ff)
        p2s[at, :] = dot(a[at, :], wp_all, NT).astype(BF16)
        low = (dot(g[at, :], wp_all) * du[at, :].astype(F32)).astype(BF16)
        du[at, :] = low

        @pl.when(j > 0)
        def _():
            ex2(j - 1).start()
            ex3(j - 1).start()

        p3s[at, :] = dot(low, wf[...].reshape(width, ff), NT).astype(BF16)
        fcs[0:1, :] = jnp.where(j == 0, 0.0, fcs[0:1, :]) + jnp.sum(
            low.astype(F32), axis=0, keepdims=True
        )

    if direct:
        s_p.add(1)
    l_h2.wait()
    ex2(n_blocks - 1).start()
    ex3(n_blocks - 1).start()
    weight_rows(gf, ht, du[...], s_f.begin_row if direct else None)
    l_h1 = load(h1t_i, ht)
    if direct:
        s_p.add(2)
    for copy in l_m:
        copy.wait()
    sums[...] = jnp.zeros_like(sums)

    @pl.loop(0, n_blocks)
    def _(j):
        at = block(j, step)
        ex2(j).wait_recv()
        ex3(j).wait_recv()
        mid = r1[at, :]
        p2r[at, :] = (
            mid + (p2s[at, :].astype(F32) + p2r[at, :].astype(F32)) + vec[5:6, :]
        ).astype(BF16)
        n, inv = norm(mid)
        dh = p3s[at, :].astype(F32) + p3r[at, :].astype(F32)
        e = dh * vec[3:4, :]
        gj = g[at, :].astype(F32)
        grad = gj + inv * (
            e - jnp.mean(e, axis=-1, keepdims=True) - n * jnp.mean(e * n, axis=-1, keepdims=True)
        )
        r1[at, :] = grad
        sums[2:3, :] += jnp.sum(grad, axis=0, keepdims=True)
        sums[3:4, :] += jnp.sum(dh * n, axis=0, keepdims=True)
        sums[4:5, :] += jnp.sum(dh, axis=0, keepdims=True)
        sums[5:6, :] += jnp.sum(gj, axis=0, keepdims=True)
        gb = grad.astype(BF16)
        gt[:, at] = gb.T
        dob = dot(gb, wo[...].reshape(width, cols)).astype(BF16)
        do[at, :] = dob
        dot_t[:, at] = dob.T

    l_x = load(x_i, g)
    own_out = load(p2r.at[pl.ds(c * half, half)], out.at[c])
    if direct:
        s_p.add(3)
    weight_rows(go, gt, o[...], (lambda s: s_o.one[s].start()) if direct else None)
    for copy in l_b:
        copy.wait()
    l_h1.wait()
    copy_p = pltpu.make_async_copy(rp, rp_o, local.at[39]) if direct else None

    def send_p():
        copy_p.start()

    side = lax.broadcasted_iota(jnp.int32, (step, 128), 1) // HD
    side_all = lax.broadcasted_iota(jnp.int32, (rows, 128), 1) // HD
    zero = jnp.zeros((), BF16)
    dst = [a.at[:, pl.ds(0, rows)], du.at[:, pl.ds(0, rows)]]
    events = [{}, {}, {}]
    if direct:
        events[0] = {
            0: lambda: s_p.add(0),
            1: lambda: s_f.cross(1),
            2: lambda: s_f.cross(2),
            3: lambda: s_o.add(1),
            4: lambda: s_o.add(2),
            5: lambda: s_f.cross(3),
            6: lambda: s_o.add(3),
            7: lambda: s_o.add(0),
        }
        events[1] = {
            0: s_p.total,
            1: lambda: s_f.cross(0),
            2: out_y.start,
            3: lambda: s_f.add(1),
            5: lambda: s_f.add(2),
            7: lambda: s_f.add(3),
        }
        events[2] = {
            0: s_o.total,
            1: lambda: s_f.add(0),
            2: lambda: s_p.final(write_to(rp)),
            3: send_p,
            4: lambda: s_q[0].add(1),
            5: lambda: s_q[0].add(2),
            6: lambda: s_q[0].add(3),
            7: lambda: s_q[0].add(0),
        }
    else:
        events[1] = {2: out_y.start}
    for p in range(n_pairs):
        pair = pl.ds(p * 128, 128)
        l_pt.wait()
        for hh in range(2):
            head = pl.ds((p * 2 + hh) * HD, HD)

            @pl.loop(0, n_blocks)
            def _(j):
                for n, event in events[p].items():
                    if n // n_blocks == hh:

                        @pl.when(j == n % n_blocks)
                        def _():
                            event()

                at = block(j, step)
                inner = jnp.sum(
                    dot_t[head, at].astype(F32) * ot[head, at].astype(F32), axis=0, keepdims=True
                )
                dp = dot(v[:, pair], jnp.where(side == hh, do[at, pair], zero), NT)
                ds = (pt[hh, :, at].astype(F32) * (dp - inner)).astype(BF16)
                dst[hh][:, at] = ds
                dqt[pl.ds(hh * HD, HD), at] = dot(kt[head, :], ds)

        qp, dp_ = q[:, pair], do[:, pair]
        dk = dot(dst[0][...], jnp.where(side_all == 0, qp, zero)) + dot(
            dst[1][...], jnp.where(side_all == 1, qp, zero)
        )
        dv = dot(pt[0], jnp.where(side_all == 0, dp_, zero)) + dot(
            pt[1], jnp.where(side_all == 1, dp_, zero)
        )
        if p + 1 < n_pairs:
            l_pt = load(pt_i.at[pl.ds(2 * p + 2, 2)], pt)
        chunk = jnp.concatenate(
            [(dqt[...].T * SCALE).astype(BF16), dk.astype(BF16), dv.astype(BF16)], axis=1
        )
        for n in range(3):
            dqkv[:, pl.ds(n * cols + p * 128, 128)] = chunk[:, n * 128 : n * 128 + 128]
        weight_rows(
            gq.at[p], ht, chunk, (lambda s, p=p: s_q[p].one[s].start()) if direct else None
        )

    @pl.loop(0, n_blocks)
    def _(j):
        ex2(j).wait_send()

    @pl.loop(0, n_blocks)
    def _(j):
        jj = lax.rem(lead + j, n_blocks)
        at = block(jj, step)
        p2s[at, :] = dot(dqkv[at, :], wq[...].reshape(width, 3 * cols), NT).astype(BF16)

        @pl.when(j > 0)
        def _():
            ex4(lax.rem(lead + j - 1, n_blocks)).start()

    qvs[...] = jnp.zeros_like(qvs)

    @pl.loop(0, n_blocks)
    def _(j):
        at = block(j, step)
        qvs[0:1, :] += jnp.sum(dqkv[at, :].astype(F32), axis=0, keepdims=True)

    ex4(lax.rem(lead + n_blocks - 1, n_blocks)).start()
    l_x.wait()
    if direct:
        s_f.total()
        for s in order:
            s_q[1].add(s)
    small[...] = jnp.zeros_like(small)
    each = width // small.shape[0]
    row = lax.broadcasted_iota(jnp.int32, (8, cols), 0)
    wide_row = lax.broadcasted_iota(jnp.int32, (8, ff), 0)
    top, low = small.at[:, pl.ds(0, 8)], small.at[:, pl.ds(8, 8)]
    for s in range(2):
        part = qvs[0:1, pl.ds(2 * s * cols, cols)]
        gather_lanes(top, jnp.where(row == 6, part, 0.0), s * (each // 2), each // 2, each // 2, 0)
    fc = fcs[0:1, :]
    gather_lanes(top, jnp.where(wide_row == 7, fc, 0.0), 0, each, 2 * each, 0)
    gather_lanes(low, jnp.where(wide_row == 0, fc, 0.0), 0, each, 2 * each, each)

    @pl.loop(0, n_blocks)
    def _(j):
        jj = lax.rem(lead + j, n_blocks)
        at = block(jj, step)
        ex4(jj).wait_recv()
        n, inv = norm(g[at, :].astype(F32))
        dh = p2s[at, :].astype(F32) + p4r[at, :].astype(F32)
        e = dh * vec[0:1, :]
        p4r[at, :] = (
            r1[at, :]
            + inv
            * (e - jnp.mean(e, axis=-1, keepdims=True) - n * jnp.mean(e * n, axis=-1, keepdims=True))
        ).astype(BF16)
        low_sums[pl.ds(jj, 1), :] = jnp.sum(dh * n, axis=0, keepdims=True)
        low_sums[pl.ds(n_blocks + jj, 1), :] = jnp.sum(dh, axis=0, keepdims=True)

        @pl.when(j == 1)
        def _():
            tok_y.start()

    own_tok = load(p4r.at[pl.ds(c * half, half)], gtok.at[c])
    for n in range(2):
        sums[n : n + 1, :] = jnp.sum(
            low_sums[n * n_blocks : (n + 1) * n_blocks, :], axis=0, keepdims=True
        )
    if direct:
        for s in order:
            s_q[2].add(s)
    gather_lanes(top, sums[...], 0, each, each, 0)
    out_y.wait_recv()
    out_t.start()
    if direct:
        s_s.begin()
        s_q[0].total()
        s_q[1].total()
        for s in order:
            s_s.add(s)
        s_o.final(write_to(ro))
        results = [load(ro, ro_o)]
        s_q[2].total()
        s_f.final(write_to(rf))
        results.append(load(rf, rf_o))
        s_s.total()
    tok_y.wait_recv()
    tok_t.start()
    if direct:
        s_s.final(write_to(rsmall))
        for p in range(n_pairs):

            def write(at, value, p=p):
                for n in range(3):
                    rq[n, at, pl.ds(p * 128, 128)] = value[:, n * 128 : n * 128 + 128]

            s_q[p].final(write)
        results.append(load(rq, rq_o))
    else:
        dumps = [load(gp, rp), load(gf, rf), load(go, ro), load(gq, rq), load(small, rsmall)]
        for copy in dumps:
            copy.wait()
    out_t.wait_recv()
    tok_t.wait_recv()

    @pl.loop(0, n_blocks)
    def _(j):
        ex3(j).wait_send()
        ex4(j).wait_send()

    net.finish()
    own_out.wait()
    own_tok.wait()
    if direct:
        copy_p.wait()
        for copy in results:
            copy.wait()


def finish_kernel(shard, small, *refs):
    big_i, refs = refs[:6], refs[6:]
    big_o, (lines_o, qv_o, fc_o), refs = refs[:6], (refs[6:12], refs[12], refs[13]), refs[14:]
    buffers, sem_i, sem_o = refs[:6], refs[6], refs[7]
    parts = []
    for n, (src, dst, buf) in enumerate(zip(big_i, big_o, buffers)):
        count = src.shape[0] if len(src.shape) == 3 else 1
        for k in range(count):
            at = (lambda r, k=k: r.at[k]) if len(src.shape) == 3 else (lambda r: r)
            load = pltpu.make_async_copy(at(src), at(buf), sem_i.at[len(parts)])
            store = pltpu.make_async_copy(at(buf), at(dst), sem_o.at[len(parts)])
            load.start()
            parts.append((load, store))
    for n in range(6):
        lines_o[n][...] = small[n : n + 1, 0:shard]
    for n in range(2):
        qv_o[n] = small[6:7, n * (shard // 2) : (n + 1) * (shard // 2)]
        fc_o[:, n * shard : (n + 1) * shard] = small[7 + n : 8 + n, 0:shard]
    for load, store in parts:
        load.wait()
        store.start()
    for _, store in parts:
        store.wait()


VM = pl.BlockSpec(memory_space=pltpu.VMEM)
SM = pl.BlockSpec(memory_space=pltpu.SMEM)
ANY = pl.BlockSpec(memory_space=pl.ANY)


def call(body, ins, outs, scratch=(), specs=None, out_specs=None, name=None, cid=None):
    params = dict(vmem_limit_bytes=LIMIT)
    if cid is not None:
        params.update(collective_id=cid, has_side_effects=True)
    return pl.pallas_call(
        body,
        out_shape=[jax.ShapeDtypeStruct(s, t) for s, t in outs],
        in_specs=specs or [VM] * len(ins),
        out_specs=out_specs or [VM] * len(outs),
        scratch_shapes=list(scratch),
        name=name,
        compiler_params=pltpu.CompilerParams(**params),
    )(*ins)


def on_device(n_dp, tokens, lengths, ln1_gain, ln1_bias, w_qkv, qv_bias, w_out, out_bias,
              ln2_gain, ln2_bias, w_fc, fc_bias, w_proj, proj_bias, cotangent):
    _, half, width = tokens.shape
    rows = 2 * half
    shard = w_fc.shape[0]
    cols = w_out.shape[1]
    ff = w_fc.shape[1]
    dma = pltpu.SemaphoreType.DMA
    direct = n_dp == 8
    lines = [ln1_gain, ln1_bias, out_bias, ln2_gain, ln2_bias, proj_bias]
    if direct:
        ins = [lengths, tokens, cotangent] + [a[None] for a in lines] + [
            qv_bias.transpose(1, 2, 0), fc_bias.T, w_qkv.transpose(1, 0, 2), w_out, w_fc, w_proj]
        specs = [SM, ANY, ANY] + [VM] * 8 + [ANY] * 4
    else:
        lines = lines + [qv_bias[:, :, 0].T.reshape(shard)] + list(fc_bias[:, 0].reshape(2, shard))
        small = jnp.pad(jnp.stack(lines), ((0, 16 - len(lines)), (0, 128 - shard)))
        wq_own = w_qkv.reshape(shard, 3 * cols)
        specs = [SM] + [ANY] * 7

        def whole(a):
            return lax.dynamic_index_in_dim(
                lax.all_gather(a, "ctx", axis=1, tiled=True), lax.axis_index("ctx"), 0, False)

        ins = (lengths, whole(tokens), whole(cotangent)) + tuple(
            lax.all_gather(a, "dp") for a in (small, wq_own, w_out, w_fc, w_proj))
    act = ((rows, width), BF16)
    act_t = ((width, rows), BF16)
    head = ((rows, cols), BF16)
    head_t = ((cols, rows), BF16)
    wide = ((rows, ff), BF16)
    mats = [((n_dp, shard, n), BF16) for n in (3 * cols, cols, ff, ff)]
    outs = [((8, width), F32), act, act_t, act, act_t, head, head, head, head_t, head, head_t,
            ((cols // HD, rows, rows), BF16), ((rows, width), F32), wide, wide, act_t] + mats
    step = 256
    held = [((16, 128), F32), ((n_dp, 16, 128), F32)] + mats[:3] + [
        act, act, act, act_t, act, act_t, head, head, head, head_t, head_t, head, head_t,
        ((2, 2, rows, step), BF16), act, act, ((rows, width), F32), wide, wide, act_t,
        ((16, cols), F32), ((8, ff), F32)]
    (vec, g, gt, xs, h1t, q, k, v, kt, o, ot, pt, r1, a, sl, h2t, wq, wo, wf, wp) = call(
        functools.partial(forward_kernel, n_dp, direct), ins, outs,
        [pltpu.VMEM(*h) for h in held]
        + [dma((72,)), dma((72,)), dma((40,)), dma((2, 2)), dma((3, rows // step))],
        specs, [VM] + [ANY] * 19, "forward", 1)
    groups = 8
    part = width // groups
    wq, wo, wf, wp = [w.reshape(groups, part, -1) for w in (wq, wo, wf, wp)]
    n_pairs, n_o = cols // 128, n_dp // 2
    narrow = 3 * 128
    held = [(w.shape, BF16) for w in (wq, wo, wf, wp)] + [
        wide, wide, act, act_t, act_t, act, act, act, act, act,
        ((groups, part, ff), BF16), ((groups, part, ff), BF16), ((groups, part, cols), BF16),
        ((n_pairs, groups, part, narrow), BF16), ((n_dp, 16, 128), F32),
        ((rows, width), F32), head, head, head_t, head, head, head, head_t, head_t,
        ((2, rows, rows), BF16), ((128, rows), F32), ((rows, 3 * cols), BF16),
        ((8, width), F32), ((2 * rows // step, width), F32), ((8, ff), F32), ((8, 3 * cols), F32)]
    seq = ((2, half, width), BF16)
    if direct:
        big = [((3, shard, cols), F32), ((shard, cols), F32), ((shard, ff), F32), ((shard, ff), F32)]
        outs = [seq, seq, ((16, 128), F32)] + big
        held += big
        hr = shard // 2
        for n, lead, r, kind in ((ff, (), shard, BF16), (None, (), 0, BF16),
                                 (cols, (), shard, BF16), (narrow, (n_pairs,), shard, BF16),
                                 (128, (), 16, F32)):
            if n is None:
                held += [((n_dp, hr, ff), kind), ((n_o, hr, ff), kind),
                         ((n_o - 1, hr, ff), kind), ((hr, ff), kind)]
                continue
            held += [(lead + (n_o, r, n), kind), (lead + (n_o - 1, r, n), kind),
                     (lead + (r, n), kind)]
        out_specs = [ANY] * 2 + [VM] + [ANY] * 4
    else:
        outs = [seq, seq, ((n_dp, 16, 128), F32), ((n_pairs, groups, part, narrow), BF16),
                ((groups, part, cols), BF16), ((groups, part, ff), BF16),
                ((groups, part, ff), BF16)]
        out_specs = [ANY] * 7
    out, gtok, rs, rq, ro, rf, rp = call(
        functools.partial(backward_kernel, n_dp, direct),
        (vec, g, gt, xs, h1t, q, k, v, kt, o, ot, pt, r1, a, sl, h2t, wq, wo, wf, wp), outs,
        [pltpu.VMEM(*h) for h in held] + [dma((96,)), dma((96,)), dma((40,))],
        [VM] + [ANY] * 19, out_specs, "backward", 2)
    if not direct:
        def summed(a):
            a = a.reshape(n_dp, shard, -1)
            return lax.psum(lax.psum_scatter(a, "dp", scatter_dimension=0), "ctx").astype(F32)

        rq = rq.reshape(n_pairs, width, 3, 128).transpose(1, 2, 0, 3).reshape(width, 3 * cols)
        rq, ro, rf, rp = [summed(a) for a in (rq, ro, rf, rp)]
        rs = lax.psum(lax.psum_scatter(rs, "dp", scatter_dimension=0), "ctx")
    if direct:
        mats = [seq, seq] + big
        small = [((1, shard), F32)] * 6 + [((2, 1, shard // 2), F32), ((1, 2 * shard), F32)]
        (out, gtok, rq, ro, rf, rp, g1, b1, bo, g2, b2, bp, qv, fc) = call(
            functools.partial(finish_kernel, shard), (rs, out, gtok, rq, ro, rf, rp), mats + small,
            [pltpu.VMEM(*m) for m in mats] + [dma((12,)), dma((12,))],
            [VM] + [ANY] * 6, [ANY] * 6 + [VM] * 8, "finish")
        return (out, gtok, g1[0], b1[0], rq.transpose(1, 0, 2), qv.transpose(2, 0, 1), ro, bo[0],
                g2[0], b2[0], rf, fc.T, rp, bp[0])
    line = [rs[j, :shard] for j in range(7)]
    return (out, gtok, line[0], line[1], rq.reshape(shard, 3, cols),
            line[6].reshape(2, shard // 2).T[:, :, None], ro, line[2], line[3], line[4],
            rf, rs[7:9, :shard].reshape(2 * shard, 1), rp, line[5])


def solution(mesh):
    dp, seq = P("dp"), P("dp", "ctx", None)
    wide, flat = P("dp", None, "tp"), P("dp", "tp")
    params = (dp, dp, wide, wide, flat, dp, dp, dp, flat, flat, flat, dp)
    return jax.shard_map(
        functools.partial(on_device, mesh.shape["dp"]),
        mesh=mesh,
        in_specs=(seq, dp) + params + (seq,),
        out_specs=(seq, seq) + params,
        check_vma=False,
    )
```

```python
import functools

import jax
import jax.numpy as jnp
from jax import lax
from jax.experimental import pallas as pl
from jax.experimental.pallas import tpu as pltpu
from jax.sharding import PartitionSpec as P

HD = 64
EPS = 1e-05
NEG = -1e30
GELU = 1.702
SCALE = HD ** (-0.5)
F32 = jnp.float32
BF16 = jnp.bfloat16
MESH = pl.DeviceIdType.MESH
LIMIT = 67_000_000
NN = (((1,), (0,)), ((), ()))
NT = (((1,), (1,)), ((), ()))


def dot(a, b, dims=NN):
    return lax.dot_general(a, b, dims, preferred_element_type=F32)


class Net:
    def __init__(self, send, recv):
        self.send, self.recv, self.used, self.all = send, recv, 0, []

    def build(self, k, src, dst, dev):
        return pltpu.make_async_remote_copy(
            src_ref=src, dst_ref=dst, send_sem=self.send.at[k], recv_sem=self.recv.at[k],
            device_id=dev, device_id_type=MESH,
        )

    def take(self, count):
        self.used += count
        return self.used - count

    def make(self, src, dst, dev):
        copy = self.build(self.take(1), src, dst, dev)
        self.all.append(copy)
        return copy

    def put(self, src, dst, dev):
        copy = self.make(src, dst, dev)
        copy.start()
        return copy

    def finish(self):
        for copy in self.all:
            copy.wait_send()


class Place:
    def __init__(self, n_dp, direct=True):
        self.d = lax.axis_index("dp")
        self.c = lax.axis_index("ctx")
        self.t = lax.axis_index("tp")
        self.direct = direct
        self.n_o = n_dp // 2
        self.o, self.i = self.d // 2, self.d % 2

    def outer(self, s):
        return (lax.rem(self.o + s, self.n_o) * 2 + self.i, self.c, self.t)

    def from_outer(self, s):
        return lax.rem(self.o + self.n_o - s, self.n_o) * 2 + self.i

    @property
    def inner(self):
        return (self.o * 2 + 1 - self.i, self.c, self.t)

    @property
    def ctx(self):
        return (self.d, 1 - self.c, self.t)

    @property
    def tp(self):
        return (self.d, self.c, 1 - self.t)

    def barrier(self, ctx=False):
        sem = pltpu.get_barrier_semaphore()
        peers = [self.tp]
        if self.direct or ctx:
            peers.append(self.ctx)
        if self.direct:
            peers += [self.outer(s) for s in range(1, self.n_o)] + [self.inner]
        for peer in peers:
            pl.semaphore_signal(sem, 1, device_id=peer, device_id_type=MESH)
        pl.semaphore_wait(sem, len(peers))


def add_rows(dst, parts, rows, step):
    @pl.loop(0, rows // step)
    def _(j):
        at = pl.ds(pl.multiple_of(j * step, step), step)
        total = parts[0][at, :].astype(F32)
        for part in parts[1:]:
            total = total + part[at, :].astype(F32)
        dst[at, :] = total.astype(dst.dtype)


def norm(x):
    centred = x - jnp.mean(x, axis=-1, keepdims=True)
    inv = lax.rsqrt(jnp.mean(centred * centred, axis=-1, keepdims=True) + EPS)
    return centred * inv, inv


def block(j, size):
    return pl.ds(pl.multiple_of(j * size, size), size)


class Stage:
    def __init__(self, me, net, src, dst, halves):
        self.src, self.dst, self.halves, self.me = src, dst, halves, me
        rows = dst.shape[1]
        part = pl.ds(me.c * (rows // 2), rows // 2)

        def cut(dev):
            return dst.at[dev, part] if halves else dst.at[dev]

        own = src.at[part] if halves else src
        shifts = list(range(1, me.n_o))
        self.outer = [net.make(own, cut(me.d), me.outer(s)) for s in shifts]
        self.inner = [net.make(own, cut(me.d), me.inner)]
        self.ctx = []
        for s in shifts:
            piece = cut(me.from_outer(s))
            self.inner.append(net.make(piece, piece, me.inner))
            if halves:
                self.ctx.append(net.make(piece, piece, me.ctx))
        self.far = []
        if halves:
            for s in [0] + shifts:
                piece = cut(lax.rem(me.o + me.n_o - s, me.n_o) * 2 + 1 - me.i)
                self.far.append(net.make(piece, piece, me.ctx))

    def begin(self):
        for copy in self.outer:
            copy.start()

    def begin_inner(self):
        self.inner[0].start()

    def relay(self, s):
        self.outer[s].wait_recv()
        self.inner[s + 1].start()
        if self.halves:
            self.ctx[s].start()

    def cross(self, s):
        self.inner[s].wait_recv()
        self.far[s].start()

    def arrive(self):
        for copy in self.ctx + self.far if self.halves else self.inner:
            copy.wait_recv()


def placed(small_all, row, first, count, stride, offset, size):
    lane = lax.broadcasted_iota(jnp.int32, (128, size), 0)
    col = lax.broadcasted_iota(jnp.int32, (128, size), 1)
    inside = (lane >= first) & (lane < first + count)

    def add(d, total):
        spot = inside & (col == lane - first + (d * stride + offset))
        return total + lax.dot_general(
            small_all[d, row : row + 8, :], spot.astype(F32), NN,
            precision=lax.Precision.HIGHEST, preferred_element_type=F32,
        )

    return lax.fori_loop(0, small_all.shape[0], add, jnp.zeros((8, size), F32))


def forward_kernel(
    n_dp, direct, length, tok, cot, *refs
):
    n_small = len(refs) - 56
    lines, refs = refs[:n_small], refs[n_small:]
    (wq, wo, wf, wp,
    vec, g_o, gt_o, x_o, h1t_o, q_o, k_o, v_o, kt_o, o_o, ot_o, pt_o, r1_o, a_o, sl_o, h2t_o,
    wq_o, wo_o, wf_o, wp_o,
    small_s, small_v, wq_v, wo_v, wf_v, x, gv, gm, gt, h1, h1t, q, k, v, kt, vt, o, ot, pt, ps, pr, r1, a, sl, h2t,
    bias, fcb, send, recv, local, pts, rows_s) = refs
    me = Place(n_dp, direct)
    net = Net(send, recv)
    d, c, t = me.d, me.c, me.t
    rows, width = x.shape
    cols = q.shape[1]
    half, step = rows // 2, 256
    quarter = half // 2
    shard = width // n_dp
    n_blocks = rows // step
    done = []

    def own(src, dst):
        copy = pltpu.make_async_copy(src, dst, local.at[len(done)])
        copy.start()
        done.append(copy)
        return copy

    if direct:
        ready = [own(wq.at[n], wq_v.at[d, :, pl.ds(n * cols, cols)]) for n in range(3)]
        small_s[...] = jnp.zeros_like(small_s)
        for n in range(6):
            small_s[n : n + 1, 0:shard] = lines[n][...]
        small_s[6:7, 0:shard] = jnp.concatenate([lines[6][0], lines[6][1]], axis=1)
        for n in range(2):
            small_s[7 + n : 8 + n, 0:shard] = lines[7][:, n * shard : (n + 1) * shard]
        small_v[d] = small_s[...]
        me.barrier()
        for copy in ready:
            copy.wait()
    else:
        me.barrier()
    live_length = length[c]
    mine = pl.ds(c * half + t * quarter, quarter)
    theirs = pl.ds((1 - c) * half + t * quarter, quarter)
    first = net.take(n_blocks)

    def exchange(j):
        at = block(j, step)
        return net.build(first + j, ps.at[at], pr.at[at], me.tp)

    if direct:
        tok_y = net.make(tok.at[1 - c, pl.ds(t * quarter, quarter)], x.at[mine], me.ctx)
        tok_t = net.make(x.at[theirs], x.at[theirs], me.tp)
        cot_y = net.make(cot.at[1 - c, pl.ds(t * quarter, quarter)], gv.at[mine], me.ctx)
        cot_t = net.make(gv.at[theirs], gv.at[theirs], me.tp)
        st_s = Stage(me, net, small_s, small_v, False)
        st_q = Stage(me, net, wq_v.at[d], wq_v, True)
        st_o = Stage(me, net, wo, wo_v, True)
        st_f = Stage(me, net, wf, wf_v, True)
        st_p = Stage(me, net, wp, wp_o, False)
        tok_y.start()
        st_s.begin()
        st_s.begin_inner()
        st_q.begin()
        st_q.begin_inner()
        st_o.begin()
        st_o.begin_inner()
        st_f.begin()
        st_p.begin()
        l_x, l_g, l_o, l_f = [
            own(tok.at[c], x.at[pl.ds(c * half, half)]),
            own(cot.at[c], gv.at[pl.ds(c * half, half)]),
            own(wo, wo_v.at[d]),
            own(wf, wf_v.at[d]),
        ]
        first_out = len(done)
        own(wp, wp_o.at[d])
        n_s = me.n_o - 1
        for s in range(n_s):
            st_s.relay(s)
        tok_y.wait_recv()
        tok_t.start()
        for s in (0, 2, 1) if n_s == 3 else range(n_s):
            st_q.relay(s)
        cot_y.start()
        st_s.arrive()
    else:
        ready = [own(lines[0], small_v), own(wq, wq_v)]
        l_x, l_g, l_o, l_f = own(tok, x), own(cot, gv), own(wo, wo_v), own(wf, wf_v)
        first_out = len(done)
        own(wp, wp_o)
        for copy in ready:
            copy.wait()

    vec[...] = placed(small_v, 0, 0, shard, shard, 0, width)
    for s in range(2):
        bias[8 * s : 8 * s + 8, :] = placed(
            small_v, 6, s * (shard // 2), shard // 2, shard // 2, 0, cols
        )
    fcb[...] = placed(small_v, 7, 0, shard, 2 * shard, 0, fcb.shape[1])
    fcb[0:1, :] = fcb[0:1, :] + placed(small_v, 8, 0, shard, 2 * shard, shard, fcb.shape[1])[0:1, :]
    if direct:
        for s in range(me.n_o):
            st_q.cross(s)
        for s in (0, 2, 1) if n_s == 3 else range(n_s):
            st_o.relay(s)
        tok_t.wait_recv()
    l_x.wait()

    @pl.loop(0, n_blocks)
    def _(j):
        at = block(j, step)
        n, _ = norm(x[at, :].astype(F32))
        low = (n * vec[0:1, :] + vec[1:2, :]).astype(BF16)
        h1[at, :] = low
        h1t[:, at] = low.T

    own(x, x_o)
    own(h1t, h1t_o)
    if direct:
        st_f.begin_inner()
        for s in (0, 2, 1) if n_s == 3 else range(n_s):
            st_f.relay(s)
        st_p.begin_inner()
        st_q.arrive()

    @pl.loop(0, n_blocks)
    def _(j):
        at = block(j, step)
        proj = dot(h1[at, :], wq_v[...].reshape(width, 3 * cols))
        q[at, :] = (proj[:, :cols] + bias[0:1, :]).astype(BF16) * SCALE
        kk = proj[:, cols : 2 * cols].astype(BF16)
        vv = (proj[:, 2 * cols :] + bias[8:9, :]).astype(BF16)
        k[at, :] = kk
        v[at, :] = vv
        kt[:, at] = kk.T
        vt[:, at] = vv.T

    own(wq_v, wq_o)
    for src, dst in ((q, q_o), (k, k_o), (v, v_o), (kt, kt_o)):
        own(src, dst)

    live = lax.broadcasted_iota(jnp.int32, (rows, step), 0) < live_length
    side = lax.broadcasted_iota(jnp.int32, (step, 128), 1) // HD

    def spill(slot, p, at):
        return [
            pltpu.make_async_copy(pt.at[slot, hh], pt_o.at[p * 2 + hh, :, at], pts.at[slot, hh])
            for hh in range(2)
        ]

    steps = (cols // 128) * n_blocks

    @pl.loop(0, steps)
    def _(it):
        p, j = it // n_blocks, it % n_blocks
        pair, at, slot = block(p, 128), block(j, step), it % 2
        if direct:

            @pl.when(it == 0)
            def _():
                for s in range(me.n_o):
                    st_o.cross(s)
                st_f.cross(0)

            @pl.when(it == 1)
            def _():
                st_f.cross(1)
                cot_y.wait_recv()
                cot_t.start()

            @pl.when(it == 2)
            def _():
                st_f.cross(3)

            @pl.when(it == 3)
            def _():
                st_f.cross(2)

            @pl.when(it == 4)
            def _():
                st_p.relay(0)

            @pl.when(it == 8)
            def _():
                st_p.relay(1)

            @pl.when(it == 11)
            def _():
                st_p.relay(2)

        @pl.when(it >= 2)
        def _():
            for copy in spill(slot, p, at):
                copy.wait()

        for hh in range(2):
            qm = jnp.where(side == hh, q[at, pair], jnp.zeros((), BF16))
            s = dot(k[:, pair], qm, NT)
            s = jnp.where(live, s, NEG)
            e = jnp.exp(s - jnp.max(s, axis=0, keepdims=True))
            pb = (e * (1.0 / jnp.sum(e, axis=0, keepdims=True))).astype(BF16)
            pt[slot, hh] = pb
            head = block(p * 2 + hh, HD)
            ot[head, at] = dot(vt[head, :], pb).astype(BF16)
        for copy in spill(slot, p, at):
            copy.start()

    for slot in range(2):
        for copy in spill(slot, 0, pl.ds(0, step)):
            copy.wait()
    own(ot, ot_o)
    if direct:
        st_o.arrive()
    l_o.wait()

    @pl.loop(0, n_blocks)
    def _(j):
        at = block(j, step)
        ob = ot[:, at].T
        o[at, :] = ob
        ps[at, :] = dot(ob, wo_v[...].reshape(width, cols), NT).astype(BF16)

        @pl.when(j > 0)
        def _():
            exchange(j - 1).start()

    own(wo_v, wo_o)
    own(o, o_o)
    exchange(n_blocks - 1).start()
    if direct:
        cot_t.wait_recv()
        st_f.arrive()
    l_g.wait()
    l_f.wait()
    own(wf_v, wf_o)

    @pl.loop(0, n_blocks)
    def _(j):
        at = block(j, step)
        on = j * step + lax.broadcasted_iota(jnp.int32, (step, width), 0) < live_length
        g = jnp.where(on, gv[at, :], jnp.zeros((), BF16))
        gm[at, :] = g
        gt[:, at] = g.T

    own(gm, g_o)
    own(gt, gt_o)

    @pl.loop(0, n_blocks)
    def _(j):
        at = block(j, step)
        exchange(j).wait_recv()
        mid = x[at, :].astype(F32) + (ps[at, :].astype(F32) + pr[at, :].astype(F32)) + vec[2:3, :]
        r1[at, :] = mid
        n, _ = norm(mid)
        h2 = (n * vec[3:4, :] + vec[4:5, :]).astype(BF16)
        h2t[:, at] = h2.T
        u = dot(h2, wf_v[...].reshape(width, fcb.shape[1])) + fcb[0:1, :]
        s = jax.nn.sigmoid(GELU * u)
        a[at, :] = (u * s).astype(BF16)
        sl[at, :] = (s * (1.0 + GELU * u * (1.0 - s))).astype(BF16)
        for n, (src, dst) in enumerate(((r1, r1_o), (a, a_o), (sl, sl_o))):
            pltpu.make_async_copy(src.at[at], dst.at[at], rows_s.at[n, j]).start()

    own(h2t, h2t_o)
    if direct:
        st_p.arrive()
    net.finish()

    @pl.loop(0, n_blocks)
    def _(j):
        at = block(j, step)
        exchange(j).wait_send()
        for n, (src, dst) in enumerate(((r1, r1_o), (a, a_o), (sl, sl_o))):
            pltpu.make_async_copy(src.at[at], dst.at[at], rows_s.at[n, j]).wait()

    for copy in done[first_out:]:
        copy.wait()


def gather_lanes(dst, values, first, count, stride, offset):
    size = values.shape[1]
    lane = lax.broadcasted_iota(jnp.int32, (128, size), 0)
    col = lax.broadcasted_iota(jnp.int32, (128, size), 1)
    inside = (lane >= first) & (lane < first + count)

    @pl.loop(0, dst.shape[0])
    def _(d):
        spot = inside & (col == lane - first + (d * stride + offset))
        dst[d] += lax.dot_general(
            values, spot.astype(F32), NT,
            precision=lax.Precision.HIGHEST, preferred_element_type=F32,
        )


class Sum:
    def __init__(self, me, net, g, x, z, y, step):
        self.me, self.g, self.x, self.z, self.y, self.step = me, g, x, z, y, step
        self.shifts = list(range(1, me.n_o))
        self.order = self.shifts + [0]
        self.one = {
            s: net.make(g.at[self.at(s) * 2 + 1 - me.i], x.at[s], me.inner) for s in self.order
        }
        self.two = {
            s: net.make(g.at[self.at(s) * 2 + me.i], z.at[s - 1], me.outer(s)) for s in self.shifts
        }
        self.three = net.make(g.at[me.d], y, me.ctx)

    def at(self, s):
        return lax.rem(self.me.o + s, self.me.n_o)

    def begin(self):
        for s in self.order:
            self.one[s].start()

    def add(self, s):
        self.one[s].wait_recv()
        part = self.g.at[self.at(s) * 2 + self.me.i]
        add_rows(part, [part, self.x.at[s]], part.shape[0], self.step)
        if s:
            self.two[s].start()

    def total(self):
        for s in self.shifts:
            self.two[s].wait_recv()
        part = self.g.at[self.me.d]
        add_rows(part, [part] + [self.z.at[s - 1] for s in self.shifts], part.shape[0], self.step)
        self.three.start()

    def final(self, write):
        self.three.wait_recv()
        part = self.g.at[self.me.d]

        @pl.loop(0, part.shape[0] // self.step)
        def _(j):
            at = block(j, self.step)
            write(at, part[at, :].astype(F32) + self.y[at, :].astype(F32))


class SumCtx:
    def __init__(self, me, net, g, y, x, z, w, step):
        self.me, self.g, self.y, self.x, self.z, self.w, self.step = me, g, y, x, z, w, step
        self.rows = g.shape[1] // 2
        self.shifts = list(range(1, me.n_o))
        self.order = self.shifts + [0]
        self.mine = pl.ds(me.c * self.rows, self.rows)
        other = pl.ds((1 - me.c) * self.rows, self.rows)
        self.zero, self.zero_own = {}, {}
        for s in self.order:
            dev = self.at(s) * 2 + 1 - me.i
            self.zero[s] = net.make(g.at[dev, other], y.at[dev], me.ctx)
        for s in self.order:
            dev = self.at(s) * 2 + me.i
            self.zero_own[s] = net.make(g.at[dev, other], y.at[dev], me.ctx)
        self.one = {
            s: net.make(g.at[self.at(s) * 2 + 1 - me.i, self.mine], x.at[s], me.inner)
            for s in self.order
        }
        self.two = {
            s: net.make(g.at[self.at(s) * 2 + me.i, self.mine], z.at[s - 1], me.outer(s))
            for s in self.shifts
        }
        self.three = net.make(g.at[me.d, self.mine], w, me.ctx)

    at = Sum.at

    def begin_row(self, s):
        self.zero[s].start()
        self.zero_own[s].start()

    def cross(self, s):
        self.zero[s].wait_recv()
        dev = self.at(s) * 2 + 1 - self.me.i
        part = self.g.at[dev, self.mine]
        add_rows(part, [part, self.y.at[dev]], self.rows, self.step)
        self.one[s].start()

    def add(self, s):
        self.zero_own[s].wait_recv()
        self.one[s].wait_recv()
        dev = self.at(s) * 2 + self.me.i
        part = self.g.at[dev, self.mine]
        add_rows(part, [part, self.y.at[dev], self.x.at[s]], self.rows, self.step)
        if s:
            self.two[s].start()

    def total(self):
        for s in self.shifts:
            self.two[s].wait_recv()
        part = self.g.at[self.me.d, self.mine]
        add_rows(part, [part] + [self.z.at[s - 1] for s in self.shifts], self.rows, self.step)
        self.three.start()

    def final(self, write):
        self.three.wait_recv()
        part = self.g.at[self.me.d, self.mine]

        @pl.loop(0, self.rows // self.step)
        def _(j):
            at = block(j, self.step)
            here = pl.ds(pl.multiple_of(self.me.c * self.rows + j * self.step, self.step), self.step)
            there = pl.ds(
                pl.multiple_of((1 - self.me.c) * self.rows + j * self.step, self.step), self.step
            )
            write(here, part[at, :].astype(F32))
            write(there, self.w[at, :].astype(F32))


def backward_kernel(
    n_dp, direct, vec, g_i, gt_i, x_i, h1t_i, q_i, k_i, v_i, kt_i, o_i, ot_i, pt_i, r1_i, a_i,
    sl_i, h2t_i, wq_i, wo_i, wf_i, wp_i, *refs
):
    n_out = 7
    out, gtok, rsmall, rq_o, ro_o, rf_o, rp_o = refs[:n_out]
    (wq, wo, wf, wp, a, du, g, gt, ht, p2s, p2r, p3s, p3r, p4r, gp, gf, go, gq, small,
     r1, o, do, dot_t, q, k, v, kt, ot, pt, dqt, dqkv, sums, low_sums, fcs, qvs) = refs[n_out : n_out + 35]
    refs = refs[n_out + 35 :]
    send, recv, local = refs[-3:]
    buffers = refs[:-3]
    if direct:
        (rq, ro, rf, rp), buffers = buffers[:4], buffers[4:]
    else:
        rq, ro, rf, rp = rq_o, ro_o, rf_o, rp_o
    me = Place(n_dp, direct)
    net = Net(send, recv)
    d, c, t = me.d, me.c, me.t
    rows, width = g.shape
    cols = q.shape[1]
    ff = a.shape[1]
    half, step = rows // 2, 256
    quarter = half // 2
    n_blocks = rows // step
    groups, shard = gp.shape[0], gp.shape[1]
    n_pairs = cols // 128
    pending = []

    def load(src, dst):
        copy = pltpu.make_async_copy(src, dst, local.at[len(pending)])
        copy.start()
        pending.append(copy)
        return copy

    l_gt, l_a = load(gt_i, gt), load(a_i, a)
    l_w = [load(wp_i, wp), load(wf_i, wf), load(g_i, g), load(sl_i, du)]
    l_h2 = load(h2t_i, ht)
    l_m = [load(r1_i, r1), load(wo_i, wo), load(o_i, o)]
    l_b = [load(q_i, q), load(k_i, k), load(v_i, v), load(kt_i, kt), load(ot_i, ot), load(wq_i, wq)]
    l_pt = load(pt_i.at[pl.ds(0, 2)], pt)
    me.barrier(True)

    def swap(first, src, dst, j):
        at = block(j, step)
        return net.build(first + j, src.at[at], dst.at[at], me.tp)

    f2, f3, f4 = net.take(n_blocks), net.take(n_blocks), net.take(n_blocks)
    ex2 = lambda j: swap(f2, p2s, p2r, j)
    ex3 = lambda j: swap(f3, p3s, p3r, j)
    ex4 = lambda j: swap(f4, p2s, p4r, j)
    lead = (1 - c) * (n_blocks // 2) + t
    mine = pl.ds((1 - c) * half + t * quarter, quarter)
    there = pl.ds(t * quarter, quarter)
    out_y = net.make(p2r.at[mine], out.at[c, there], me.ctx)
    out_t = net.make(out.at[1 - c, there], out.at[1 - c, there], me.tp)
    tok_y = net.make(p4r.at[mine], gtok.at[c, there], me.ctx)
    tok_t = net.make(gtok.at[1 - c, there], gtok.at[1 - c, there], me.tp)

    def write_to(ref):
        def write(at, value):
            ref[at, :] = value
        return write

    if direct:
        b = list(buffers)
        s_p = Sum(me, net, gp, b[0], b[1], b[2], 16)
        s_f = SumCtx(me, net, gf, b[3], b[4], b[5], b[6], 16)
        s_o = Sum(me, net, go, b[7], b[8], b[9], 16)
        s_q = [
            Sum(me, net, gq.at[p], b[10].at[p], b[11].at[p], b[12].at[p], 16)
            for p in range(n_pairs)
        ]
        s_s = Sum(me, net, small, b[13], b[14], b[15], 8)
        order = s_p.order
    two = 2 * shard
    n_z = width // two

    def weight_rows(dst, lhs, rhs, each):
        @pl.loop(0, n_z)
        def _(s):
            zz = lax.rem(me.o + 1 + s, n_z) if direct else s
            value = dot(lhs[pl.ds(pl.multiple_of(zz * two, two), two), :], rhs)
            value = value.astype(BF16).reshape(2, shard, value.shape[1])
            dst[pl.ds(pl.multiple_of(zz * 2, 2), 2)] = value
            if each is not None:
                for n in range(n_z):

                    @pl.when(s == n)
                    def _():
                        each((n + 1) % n_z)

    l_gt.wait()
    l_a.wait()
    weight_rows(gp, gt, a[...], (lambda s: s_p.one[s].start()) if direct else None)
    for copy in l_w:
        copy.wait()

    @pl.loop(0, n_blocks)
    def _(j):
        at = block(j, step)
        wp_all = wp[...].reshape(width, ff)
        p2s[at, :] = dot(a[at, :], wp_all, NT).astype(BF16)
        low = (dot(g[at, :], wp_all) * du[at, :].astype(F32)).astype(BF16)
        du[at, :] = low

        @pl.when(j > 0)
        def _():
            ex2(j - 1).start()
            ex3(j - 1).start()

        p3s[at, :] = dot(low, wf[...].reshape(width, ff), NT).astype(BF16)
        fcs[0:1, :] = jnp.where(j == 0, 0.0, fcs[0:1, :]) + jnp.sum(
            low.astype(F32), axis=0, keepdims=True
        )

    if direct:
        s_p.add(1)
    l_h2.wait()
    ex2(n_blocks - 1).start()
    ex3(n_blocks - 1).start()
    weight_rows(gf, ht, du[...], s_f.begin_row if direct else None)
    l_h1 = load(h1t_i, ht)
    if direct:
        s_p.add(2)
    for copy in l_m:
        copy.wait()
    sums[...] = jnp.zeros_like(sums)

    @pl.loop(0, n_blocks)
    def _(j):
        at = block(j, step)
        ex2(j).wait_recv()
        ex3(j).wait_recv()
        mid = r1[at, :]
        p2r[at, :] = (
            mid + (p2s[at, :].astype(F32) + p2r[at, :].astype(F32)) + vec[5:6, :]
        ).astype(BF16)
        n, inv = norm(mid)
        dh = p3s[at, :].astype(F32) + p3r[at, :].astype(F32)
        e = dh * vec[3:4, :]
        gj = g[at, :].astype(F32)
        grad = gj + inv * (
            e - jnp.mean(e, axis=-1, keepdims=True) - n * jnp.mean(e * n, axis=-1, keepdims=True)
        )
        r1[at, :] = grad
        sums[2:3, :] += jnp.sum(grad, axis=0, keepdims=True)
        sums[3:4, :] += jnp.sum(dh * n, axis=0, keepdims=True)
        sums[4:5, :] += jnp.sum(dh, axis=0, keepdims=True)
        sums[5:6, :] += jnp.sum(gj, axis=0, keepdims=True)
        gb = grad.astype(BF16)
        gt[:, at] = gb.T
        dob = dot(gb, wo[...].reshape(width, cols)).astype(BF16)
        do[at, :] = dob
        dot_t[:, at] = dob.T

    l_x = load(x_i, g)
    own_out = load(p2r.at[pl.ds(c * half, half)], out.at[c])
    if direct:
        s_p.add(3)
    weight_rows(go, gt, o[...], (lambda s: s_o.one[s].start()) if direct else None)
    for copy in l_b:
        copy.wait()
    l_h1.wait()
    copy_p = pltpu.make_async_copy(rp, rp_o, local.at[39]) if direct else None

    def send_p():
        copy_p.start()

    side = lax.broadcasted_iota(jnp.int32, (step, 128), 1) // HD
    side_all = lax.broadcasted_iota(jnp.int32, (rows, 128), 1) // HD
    zero = jnp.zeros((), BF16)
    dst = [a.at[:, pl.ds(0, rows)], du.at[:, pl.ds(0, rows)]]
    events = [{}, {}, {}]
    if direct:
        events[0] = {
            0: lambda: s_p.add(0),
            1: lambda: s_f.cross(1),
            2: lambda: s_f.cross(2),
            3: lambda: s_o.add(1),
            4: lambda: s_o.add(2),
            5: lambda: s_f.cross(3),
            6: lambda: s_o.add(3),
            7: lambda: s_o.add(0),
        }
        events[1] = {
            0: s_p.total,
            1: lambda: s_f.cross(0),
            2: out_y.start,
            3: lambda: s_f.add(1),
            5: lambda: s_f.add(2),
            7: lambda: s_f.add(3),
        }
        events[2] = {
            0: s_o.total,
            1: lambda: s_f.add(0),
            2: lambda: s_p.final(write_to(rp)),
            3: send_p,
            4: lambda: s_q[0].add(1),
            5: lambda: s_q[0].add(2),
            6: lambda: s_q[0].add(3),
            7: lambda: s_q[0].add(0),
        }
    else:
        events[1] = {2: out_y.start}
    for p in range(n_pairs):
        pair = pl.ds(p * 128, 128)
        l_pt.wait()
        for hh in range(2):
            head = pl.ds((p * 2 + hh) * HD, HD)

            @pl.loop(0, n_blocks)
            def _(j):
                for n, event in events[p].items():
                    if n // n_blocks == hh:

                        @pl.when(j == n % n_blocks)
                        def _():
                            event()

                at = block(j, step)
                inner = jnp.sum(
                    dot_t[head, at].astype(F32) * ot[head, at].astype(F32), axis=0, keepdims=True
                )
                dp = dot(v[:, pair], jnp.where(side == hh, do[at, pair], zero), NT)
                ds = (pt[hh, :, at].astype(F32) * (dp - inner)).astype(BF16)
                dst[hh][:, at] = ds
                dqt[pl.ds(hh * HD, HD), at] = dot(kt[head, :], ds)

        qp, dp_ = q[:, pair], do[:, pair]
        dk = dot(dst[0][...], jnp.where(side_all == 0, qp, zero)) + dot(
            dst[1][...], jnp.where(side_all == 1, qp, zero)
        )
        dv = dot(pt[0], jnp.where(side_all == 0, dp_, zero)) + dot(
            pt[1], jnp.where(side_all == 1, dp_, zero)
        )
        if p + 1 < n_pairs:
            l_pt = load(pt_i.at[pl.ds(2 * p + 2, 2)], pt)
        chunk = jnp.concatenate(
            [(dqt[...].T * SCALE).astype(BF16), dk.astype(BF16), dv.astype(BF16)], axis=1
        )
        for n in range(3):
            dqkv[:, pl.ds(n * cols + p * 128, 128)] = chunk[:, n * 128 : n * 128 + 128]
        weight_rows(
            gq.at[p], ht, chunk, (lambda s, p=p: s_q[p].one[s].start()) if direct else None
        )

    @pl.loop(0, n_blocks)
    def _(j):
        ex2(j).wait_send()

    @pl.loop(0, n_blocks)
    def _(j):
        jj = lax.rem(lead + j, n_blocks)
        at = block(jj, step)
        p2s[at, :] = dot(dqkv[at, :], wq[...].reshape(width, 3 * cols), NT).astype(BF16)

        @pl.when(j > 0)
        def _():
            ex4(lax.rem(lead + j - 1, n_blocks)).start()

    qvs[...] = jnp.zeros_like(qvs)

    @pl.loop(0, n_blocks)
    def _(j):
        at = block(j, step)
        qvs[0:1, :] += jnp.sum(dqkv[at, :].astype(F32), axis=0, keepdims=True)

    ex4(lax.rem(lead + n_blocks - 1, n_blocks)).start()
    l_x.wait()
    if direct:
        s_f.total()
        for s in order:
            s_q[1].add(s)
    small[...] = jnp.zeros_like(small)
    each = width // small.shape[0]
    row = lax.broadcasted_iota(jnp.int32, (8, cols), 0)
    wide_row = lax.broadcasted_iota(jnp.int32, (8, ff), 0)
    top, low = small.at[:, pl.ds(0, 8)], small.at[:, pl.ds(8, 8)]
    for s in range(2):
        part = qvs[0:1, pl.ds(2 * s * cols, cols)]
        gather_lanes(top, jnp.where(row == 6, part, 0.0), s * (each // 2), each // 2, each // 2, 0)
    fc = fcs[0:1, :]
    gather_lanes(top, jnp.where(wide_row == 7, fc, 0.0), 0, each, 2 * each, 0)
    gather_lanes(low, jnp.where(wide_row == 0, fc, 0.0), 0, each, 2 * each, each)

    @pl.loop(0, n_blocks)
    def _(j):
        jj = lax.rem(lead + j, n_blocks)
        at = block(jj, step)
        ex4(jj).wait_recv()
        n, inv = norm(g[at, :].astype(F32))
        dh = p2s[at, :].astype(F32) + p4r[at, :].astype(F32)
        e = dh * vec[0:1, :]
        p4r[at, :] = (
            r1[at, :]
            + inv
            * (e - jnp.mean(e, axis=-1, keepdims=True) - n * jnp.mean(e * n, axis=-1, keepdims=True))
        ).astype(BF16)
        low_sums[pl.ds(jj, 1), :] = jnp.sum(dh * n, axis=0, keepdims=True)
        low_sums[pl.ds(n_blocks + jj, 1), :] = jnp.sum(dh, axis=0, keepdims=True)

        @pl.when(j == 1)
        def _():
            tok_y.start()

    own_tok = load(p4r.at[pl.ds(c * half, half)], gtok.at[c])
    for n in range(2):
        sums[n : n + 1, :] = jnp.sum(
            low_sums[n * n_blocks : (n + 1) * n_blocks, :], axis=0, keepdims=True
        )
    if direct:
        for s in order:
            s_q[2].add(s)
    gather_lanes(top, sums[...], 0, each, each, 0)
    out_y.wait_recv()
    out_t.start()
    if direct:
        s_s.begin()
        s_q[0].total()
        s_q[1].total()
        for s in order:
            s_s.add(s)
        s_o.final(write_to(ro))
        results = [load(ro, ro_o)]
        s_q[2].total()
        s_f.final(write_to(rf))
        results.append(load(rf, rf_o))
        s_s.total()
    tok_y.wait_recv()
    tok_t.start()
    if direct:
        s_s.final(write_to(rsmall))
        for p in range(n_pairs):

            def write(at, value, p=p):
                for n in range(3):
                    rq[n, at, pl.ds(p * 128, 128)] = value[:, n * 128 : n * 128 + 128]

            s_q[p].final(write)
        results.append(load(rq, rq_o))
    else:
        dumps = [load(gp, rp), load(gf, rf), load(go, ro), load(gq, rq), load(small, rsmall)]
        for copy in dumps:
            copy.wait()
    out_t.wait_recv()
    tok_t.wait_recv()

    @pl.loop(0, n_blocks)
    def _(j):
        ex3(j).wait_send()
        ex4(j).wait_send()

    net.finish()
    own_out.wait()
    own_tok.wait()
    if direct:
        copy_p.wait()
        for copy in results:
            copy.wait()


def finish_kernel(shard, small, *refs):
    big_i, refs = refs[:6], refs[6:]
    big_o, (lines_o, qv_o, fc_o), refs = refs[:6], (refs[6:12], refs[12], refs[13]), refs[14:]
    buffers, sem_i, sem_o = refs[:6], refs[6], refs[7]
    parts = []
    for n, (src, dst, buf) in enumerate(zip(big_i, big_o, buffers)):
        count = src.shape[0] if len(src.shape) == 3 else 1
        for k in range(count):
            at = (lambda r, k=k: r.at[k]) if len(src.shape) == 3 else (lambda r: r)
            load = pltpu.make_async_copy(at(src), at(buf), sem_i.at[len(parts)])
            store = pltpu.make_async_copy(at(buf), at(dst), sem_o.at[len(parts)])
            load.start()
            parts.append((load, store))
    for n in range(6):
        lines_o[n][...] = small[n : n + 1, 0:shard]
    for n in range(2):
        qv_o[n] = small[6:7, n * (shard // 2) : (n + 1) * (shard // 2)]
        fc_o[:, n * shard : (n + 1) * shard] = small[7 + n : 8 + n, 0:shard]
    for load, store in parts:
        load.wait()
        store.start()
    for _, store in parts:
        store.wait()


VM = pl.BlockSpec(memory_space=pltpu.VMEM)
SM = pl.BlockSpec(memory_space=pltpu.SMEM)
ANY = pl.BlockSpec(memory_space=pl.ANY)


def call(body, ins, outs, scratch=(), specs=None, out_specs=None, name=None, cid=None):
    params = dict(vmem_limit_bytes=LIMIT)
    if cid is not None:
        params.update(collective_id=cid, has_side_effects=True)
    return pl.pallas_call(
        body,
        out_shape=[jax.ShapeDtypeStruct(s, t) for s, t in outs],
        in_specs=specs or [VM] * len(ins),
        out_specs=out_specs or [VM] * len(outs),
        scratch_shapes=list(scratch),
        name=name,
        compiler_params=pltpu.CompilerParams(**params),
    )(*ins)


def on_device(n_dp, tokens, lengths, ln1_gain, ln1_bias, w_qkv, qv_bias, w_out, out_bias,
              ln2_gain, ln2_bias, w_fc, fc_bias, w_proj, proj_bias, cotangent):
    _, half, width = tokens.shape
    rows = 2 * half
    shard = w_fc.shape[0]
    cols = w_out.shape[1]
    ff = w_fc.shape[1]
    dma = pltpu.SemaphoreType.DMA
    direct = n_dp == 8
    lines = [ln1_gain, ln1_bias, out_bias, ln2_gain, ln2_bias, proj_bias]
    if direct:
        ins = [lengths, tokens, cotangent] + [a[None] for a in lines] + [
            qv_bias.transpose(1, 2, 0), fc_bias.T, w_qkv.transpose(1, 0, 2), w_out, w_fc, w_proj]
        specs = [SM, ANY, ANY] + [VM] * 8 + [ANY] * 4
    else:
        lines = lines + [qv_bias[:, :, 0].T.reshape(shard)] + list(fc_bias[:, 0].reshape(2, shard))
        small = jnp.pad(jnp.stack(lines), ((0, 16 - len(lines)), (0, 128 - shard)))
        wq_own = w_qkv.reshape(shard, 3 * cols)
        specs = [SM] + [ANY] * 7

        def whole(a):
            return lax.dynamic_index_in_dim(
                lax.all_gather(a, "ctx", axis=1, tiled=True), lax.axis_index("ctx"), 0, False)

        ins = (lengths, whole(tokens), whole(cotangent)) + tuple(
            lax.all_gather(a, "dp") for a in (small, wq_own, w_out, w_fc, w_proj))
    act = ((rows, width), BF16)
    act_t = ((width, rows), BF16)
    head = ((rows, cols), BF16)
    head_t = ((cols, rows), BF16)
    wide = ((rows, ff), BF16)
    mats = [((n_dp, shard, n), BF16) for n in (3 * cols, cols, ff, ff)]
    outs = [((8, width), F32), act, act_t, act, act_t, head, head, head, head_t, head, head_t,
            ((cols // HD, rows, rows), BF16), ((rows, width), F32), wide, wide, act_t] + mats
    step = 256
    held = [((16, 128), F32), ((n_dp, 16, 128), F32)] + mats[:3] + [
        act, act, act, act_t, act, act_t, head, head, head, head_t, head_t, head, head_t,
        ((2, 2, rows, step), BF16), act, act, ((rows, width), F32), wide, wide, act_t,
        ((16, cols), F32), ((8, ff), F32)]
    (vec, g, gt, xs, h1t, q, k, v, kt, o, ot, pt, r1, a, sl, h2t, wq, wo, wf, wp) = call(
        functools.partial(forward_kernel, n_dp, direct), ins, outs,
        [pltpu.VMEM(*h) for h in held]
        + [dma((72,)), dma((72,)), dma((40,)), dma((2, 2)), dma((3, rows // step))],
        specs, [VM] + [ANY] * 19, "forward", 1)
    groups = 8
    part = width // groups
    wq, wo, wf, wp = [w.reshape(groups, part, -1) for w in (wq, wo, wf, wp)]
    n_pairs, n_o = cols // 128, n_dp // 2
    narrow = 3 * 128
    held = [(w.shape, BF16) for w in (wq, wo, wf, wp)] + [
        wide, wide, act, act_t, act_t, act, act, act, act, act,
        ((groups, part, ff), BF16), ((groups, part, ff), BF16), ((groups, part, cols), BF16),
        ((n_pairs, groups, part, narrow), BF16), ((n_dp, 16, 128), F32),
        ((rows, width), F32), head, head, head_t, head, head, head, head_t, head_t,
        ((2, rows, rows), BF16), ((128, rows), F32), ((rows, 3 * cols), BF16),
        ((8, width), F32), ((2 * rows // step, width), F32), ((8, ff), F32), ((8, 3 * cols), F32)]
    seq = ((2, half, width), BF16)
    if direct:
        big = [((3, shard, cols), F32), ((shard, cols), F32), ((shard, ff), F32), ((shard, ff), F32)]
        outs = [seq, seq, ((16, 128), F32)] + big
        held += big
        hr = shard // 2
        for n, lead, r, kind in ((ff, (), shard, BF16), (None, (), 0, BF16),
                                 (cols, (), shard, BF16), (narrow, (n_pairs,), shard, BF16),
                                 (128, (), 16, F32)):
            if n is None:
                held += [((n_dp, hr, ff), kind), ((n_o, hr, ff), kind),
                         ((n_o - 1, hr, ff), kind), ((hr, ff), kind)]
                continue
            held += [(lead + (n_o, r, n), kind), (lead + (n_o - 1, r, n), kind),
                     (lead + (r, n), kind)]
        out_specs = [ANY] * 2 + [VM] + [ANY] * 4
    else:
        outs = [seq, seq, ((n_dp, 16, 128), F32), ((n_pairs, groups, part, narrow), BF16),
                ((groups, part, cols), BF16), ((groups, part, ff), BF16),
                ((groups, part, ff), BF16)]
        out_specs = [ANY] * 7
    out, gtok, rs, rq, ro, rf, rp = call(
        functools.partial(backward_kernel, n_dp, direct),
        (vec, g, gt, xs, h1t, q, k, v, kt, o, ot, pt, r1, a, sl, h2t, wq, wo, wf, wp), outs,
        [pltpu.VMEM(*h) for h in held] + [dma((96,)), dma((96,)), dma((40,))],
        [VM] + [ANY] * 19, out_specs, "backward", 2)
    if not direct:
        def summed(a):
            a = a.reshape(n_dp, shard, -1)
            return lax.psum(lax.psum_scatter(a, "dp", scatter_dimension=0), "ctx").astype(F32)

        rq = rq.reshape(n_pairs, width, 3, 128).transpose(1, 2, 0, 3).reshape(width, 3 * cols)
        rq, ro, rf, rp = [summed(a) for a in (rq, ro, rf, rp)]
        rs = lax.psum(lax.psum_scatter(rs, "dp", scatter_dimension=0), "ctx")
    if direct:
        mats = [seq, seq] + big
        small = [((1, shard), F32)] * 6 + [((2, 1, shard // 2), F32), ((1, 2 * shard), F32)]
        (out, gtok, rq, ro, rf, rp, g1, b1, bo, g2, b2, bp, qv, fc) = call(
            functools.partial(finish_kernel, shard), (rs, out, gtok, rq, ro, rf, rp), mats + small,
            [pltpu.VMEM(*m) for m in mats] + [dma((12,)), dma((12,))],
            [VM] + [ANY] * 6, [ANY] * 6 + [VM] * 8, "finish")
        return (out, gtok, g1[0], b1[0], rq.transpose(1, 0, 2), qv.transpose(2, 0, 1), ro, bo[0],
                g2[0], b2[0], rf, fc.T, rp, bp[0])
    line = [rs[j, :shard] for j in range(7)]
    return (out, gtok, line[0], line[1], rq.reshape(shard, 3, cols),
            line[6].reshape(2, shard // 2).T[:, :, None], ro, line[2], line[3], line[4],
            rf, rs[7:9, :shard].reshape(2 * shard, 1), rp, line[5])


def solution(mesh):
    dp, seq = P("dp"), P("dp", "ctx", None)
    wide, flat = P("dp", None, "tp"), P("dp", "tp")
    params = (dp, dp, wide, wide, flat, dp, dp, dp, flat, flat, flat, dp)
    return jax.shard_map(
        functools.partial(on_device, mesh.shape["dp"]),
        mesh=mesh,
        in_specs=(seq, dp) + params + (seq,),
        out_specs=(seq, seq) + params,
        check_vma=False,
    )
```
